128 devices in a mesh: dp: 8 (over y, core), section: 4 (over x), head: 4 (over z).
Axes of the slice: x: 4, y: 4, z: 4, core: 2. Of those that a mesh axis runs over, the one named last changes fastest.
Arguments:
- images: bfloat16 [32, 144, 1408], P(('dp', 'head')), may hold values from -6 to 6
- w_in: bfloat16 [4, 1408, 3072], P('section'), may hold values from -0.15625 to 0.15625
- w_out: bfloat16 [4, 3072, 1408], P('section'), may hold values from -0.109375 to 0.109375
- fpn_weight: bfloat16 [2, 1408, 256], P(None, None, 'section'), may hold values from -0.15625 to 0.15625
- fc6_weight: bfloat16 [256, 49, 512], P('section'), may hold values from -0.0546875 to 0.0546875
- fc7_weight: bfloat16 [512, 512], replicated, may hold values from -0.25 to 0.25
- windows: int32 [3, 32, 128], P(None, ('dp', 'head')), may hold values from 0 to 8, as said below
- bilinear: float32 [2, 7, 4, 32, 128], P(None, None, None, ('dp', 'head')), may hold values from 0 to 1, as said below
- owners: int32 [32, 128, 1], P(('dp', 'head')), may hold values from 0 to 31; in each aligned block of 128 rows (0 to 127, 128 to 255, ..., all dimensions but the last counted through in order) at most 6 rows name the same one
- cotangent: bfloat16 [32, 32, 6, 512], P(('dp', 'head')), may hold values from -6 to 6
Outputs:
- grad_w_in: float32 [4, 1408, 3072], P('section', ('dp', 'head'))
- grad_w_out: float32 [4, 3072, 1408], P('section', ('dp', 'head'))
- grad_fpn: float32 [2, 1408, 256], P(None, None, 'section')
- grad_fc6: float32 [256, 49, 512], P('section', None, ('dp', 'head'))
- grad_fc7: float32 [512, 512], P(None, ('dp', 'head'))
The draws below stay inside these ranges and needn't reach their ends.
Inputs may be any that keep to these rules, and one draw needn't show every extreme that they name: windows[0] is the level (0 or 1); windows[1] and windows[2] are a corner such that a 4x4 window fits the level's grid (12 or 6 cells a side). Along u each row of bilinear has at most two nonzero weights, on adjacent cells, summing to one. `owners`: among the 128 boxes of one image group (aligned blocks) no owner is named more than 6 times.
All inputs are finite; a program needn't handle non-finite values.
Results may differ from the reference program's by a relative error of at most 0.035.
Values may be sent and summed in bfloat16 or wider, within the bound.
No kernel may reach another device: no remote copies, remote signals or barrier semaphores. Data moves between devices by JAX's collectives and lax.ppermute only.
A program may use at most 128 MiB of HBM per device.

```python
import math
import jax
import jax.numpy as jnp
import numpy as np
from jax import lax

D = 1408
FFW = 3072
CHANNELS = 256
HEAD_UNITS = 512
GRID = 12
SPAN = 4
POOLED = 7
IMG_DEV = 1
BOX_IMG = 128
LAYERS = 4
OWNERS = 32
IMAGES = 32
CAP = 6
N_DP = 8
N_HEAD = 4


def draw_windows(key, part):
    key_level, key_corner = jax.random.split(key)
    levels = jax.random.randint(key_level, (IMAGES, BOX_IMG), 0, 2, dtype=jnp.int32)
    corner_pos = jax.random.randint(key_corner, (2, IMAGES, BOX_IMG), 0, GRID - SPAN + 1, dtype=jnp.int32)
    narrow = GRID // 2 - SPAN + 1
    anchors = jnp.where(levels[None] == 0, corner_pos, corner_pos % narrow)
    return jnp.concatenate([levels[None], anchors], axis=0).astype(jnp.int32)


def draw_bilinear(key, part):
    key_cell, key_frac = jax.random.split(key)
    lower_cell = jax.random.randint(key_cell, (2, POOLED, 1, IMAGES, BOX_IMG), 0, SPAN - 1, dtype=jnp.int32)
    fraction = jax.random.uniform(key_frac, (2, POOLED, 1, IMAGES, BOX_IMG), jnp.float32)
    cell_ids = jnp.arange(SPAN, dtype=jnp.int32).reshape(1, 1, SPAN, 1, 1)
    low_part = (1.0 - fraction) * (cell_ids == lower_cell).astype(jnp.float32)
    high_part = fraction * (cell_ids == lower_cell + 1).astype(jnp.float32)
    return (low_part + high_part).astype(jnp.float32)


def steps_of(stream_key, extent, cuts, least, largest):
    factor_of = 1.0
    for dim, shards_of in cuts:
        heights = jax.random.uniform(jax.random.fold_in(jax.random.fold_in(stream_key, 6), dim), (shards_of,), jnp.float32, least / len(cuts), largest / len(cuts))
        factor_of = factor_of * jnp.repeat(jnp.exp(heights), extent[dim] // shards_of).reshape((-1,) + (1,) * (len(extent) - 1 - dim))
    return factor_of


def routed_block(rng, own, number, rows, number_of, top, reach, lean):
    order = jax.random.permutation(rng, number_of)
    crowded, ordinary = shares(number_of, rows * top, reach, lean, True), shares(number_of, rows * top, reach, lean, False)
    places = jnp.arange(number_of)

    def named(sizes, rotation):
        used = int((sizes > 0).sum())
        fixed = max(1, used // 4)
        passed = fixed + (places - fixed + rotation * (used - fixed)) % max(1, number_of - fixed)
        return jnp.zeros((number_of,), jnp.int32).at[order[jnp.where(places < fixed, places, passed)]].set(jnp.asarray(sizes, jnp.int32))

    sizes = jnp.where(number % 4 == 0, named(crowded, number // 4), named(ordinary, number - number // 4 - 1))
    mixed = jax.random.permutation(jax.random.fold_in(own, 3), number_of)
    source_of, taker = mixed[0:number_of // 2 * 2:2], mixed[1:number_of // 2 * 2:2]
    slack = jnp.minimum(sizes[source_of] - 1, reach - sizes[taker]) // 2
    slack = jnp.where((source_of == order[0]) | (taker == order[0]) | (sizes[taker] == 0), 0, jnp.maximum(slack, 0))
    passed = jax.random.randint(jax.random.fold_in(own, 4), (number_of // 2,), 0, 1 << 20) % (slack + 1)
    sizes = sizes.at[source_of].add(-passed).at[taker].add(passed)
    labels = jnp.searchsorted(jnp.cumsum(sizes), jnp.arange(rows * top), side="right").astype(jnp.int32)
    table = labels.reshape(top, rows).T
    table = table[jax.random.permutation(jax.random.fold_in(own, 1), rows)]
    rotation = jax.random.randint(jax.random.fold_in(own, 2), (rows, 1), 0, top)
    return jnp.take_along_axis(table, (jnp.arange(top)[None, :] + rotation) % top, axis=1)


def shares(amount, total, bound, lean, full):
    loads = [(1 << 20) // math.isqrt(standing ** lean) + 1 for standing in range(1, amount + 1)]
    largest = bound if full else min(bound, max(-(-total // amount), total * loads[0] // sum(loads)))
    least = 1 if total - largest >= amount - 1 else 0
    counts, rest = [largest] + [least] * (amount - 1), total - largest - least * (amount - 1)
    while rest > 0:
        movable = [i for i in range(1, amount) if counts[i] < largest] or [i for i in range(1, amount) if counts[i] < bound]
        pool, budget = sum([loads[i] for i in movable]), rest
        for i in movable:
            extra = min(bound - counts[i], max(1, budget * loads[i] // pool), rest)
            counts[i] = counts[i] + extra
            rest = rest - extra
    return np.array(counts)


def gaussian(key, shape, spread, limit, cuts=(), held_as=jnp.bfloat16):
    factor_of = steps_of(key, shape, cuts, -0.22, 0.18) if cuts else 1.0
    entries = jax.random.normal(key, shape, jnp.float32) * spread * factor_of
    return jnp.minimum(jnp.maximum(entries, -limit), limit).astype(held_as)


def setup_inputs(seed: int = 0) -> dict:
    key_of = jax.random.split(jax.random.key(seed), 11)
    images = gaussian(key_of[0], (IMAGES, GRID * GRID, D), 1.0, 6.0, ((0, 32),))
    w_in = gaussian(key_of[1], (LAYERS, D, FFW), D ** -0.5, 0.15625, ((0, 4),))
    w_out = gaussian(key_of[2], (LAYERS, FFW, D), FFW ** -0.5, 0.109375, ((0, 4),))
    fpn_weight = gaussian(key_of[3], (2, D, CHANNELS), D ** -0.5, 0.15625, ((2, 4),))
    fc6_weight = gaussian(key_of[4], (CHANNELS, POOLED * POOLED, HEAD_UNITS), (CHANNELS * POOLED * POOLED) ** -0.5, 0.0546875, ((0, 4),))
    fc7_weight = gaussian(key_of[5], (HEAD_UNITS, HEAD_UNITS), HEAD_UNITS ** -0.5, 0.25)
    windows = draw_windows(jax.random.fold_in(key_of[10], 71), 0)
    bilinear = draw_bilinear(jax.random.fold_in(key_of[10], 71), 0)
    owners_keys = jax.random.split(jax.random.fold_in(key_of[8], 1), IMAGES * BOX_IMG // (IMG_DEV * BOX_IMG))
    owners_turns = jax.random.permutation(jax.random.fold_in(key_of[8], 3), IMAGES * BOX_IMG // (IMG_DEV * BOX_IMG))
    owners = jax.vmap(lambda own, number: routed_block(jax.random.fold_in(key_of[8], 2), own, number, IMG_DEV * BOX_IMG, OWNERS, 1, CAP, 2))(owners_keys, owners_turns).reshape((IMAGES, BOX_IMG, 1))
    cotangent = gaussian(key_of[9], (OWNERS, OWNERS, CAP, HEAD_UNITS), 1.0, 6.0, ((0, 32),))
    return {"images": images, "w_in": w_in, "w_out": w_out, "fpn_weight": fpn_weight, "fc6_weight": fc6_weight, "fc7_weight": fc7_weight, "windows": windows, "bilinear": bilinear, "owners": owners, "cotangent": cotangent}


EPS = 1e-06
GELU_C = math.sqrt(2.0 / math.pi)
HIGH = lax.Precision.HIGHEST

def gelu_parts(values):
    inner_arg = GELU_C * (values + 0.044715 * values * values * values)
    tangent = jnp.tanh(inner_arg)
    result = 0.5 * values * (1.0 + tangent)
    gelu_slope = 0.5 * (1.0 + tangent) + 0.5 * values * (1.0 - tangent * tangent) * GELU_C * (1.0 + 3.0 * 0.044715 * values * values)
    return (result, gelu_slope)

def norm_parts(tokens):
    floats = tokens.astype(jnp.float32)
    centred = floats - lax.optimization_barrier(jnp.mean(floats, axis=-1, keepdims=True))
    scale_inv = lax.rsqrt(lax.optimization_barrier(jnp.mean(centred * centred, axis=-1, keepdims=True)) + EPS)
    return (centred * scale_inv, scale_inv)

def block_forward(tokens, w_first, w_second):
    normed, scale_inv = norm_parts(tokens)
    normed_b = normed.astype(jnp.bfloat16)
    preact = jnp.dot(normed_b, w_first, preferred_element_type=jnp.float32)
    activ, gelu_slope = gelu_parts(preact)
    activ_b = activ.astype(jnp.bfloat16)
    result = (tokens.astype(jnp.float32) + jnp.dot(activ_b, w_second, preferred_element_type=jnp.float32)).astype(jnp.bfloat16)
    return (result, normed_b, preact, activ_b)

def block_backward(grad_out, tokens, preact, w_first, w_second):
    grad_act = jnp.dot(grad_out, w_second.T, preferred_element_type=jnp.float32)
    activ, gelu_slope = gelu_parts(preact)
    grad_pre = (grad_act * gelu_slope).astype(jnp.bfloat16)
    grad_norm = jnp.dot(grad_pre, w_first.T, preferred_element_type=jnp.float32)
    normed, scale_inv = norm_parts(tokens)
    grad_tok = scale_inv * (grad_norm - lax.optimization_barrier(jnp.mean(grad_norm, axis=-1, keepdims=True)) - normed * lax.optimization_barrier(jnp.mean(grad_norm * normed, axis=-1, keepdims=True)))
    return ((grad_out.astype(jnp.float32) + grad_tok).astype(jnp.bfloat16), grad_pre)

def pyramid(top_rows, fpn_first, fpn_second, images_here):
    model_width = top_rows.shape[-1]
    half_grid = GRID // 2
    grid_rows = top_rows.reshape(images_here, GRID, GRID, model_width)
    pooled = grid_rows.astype(jnp.float32).reshape(images_here, half_grid, 2, half_grid, 2, model_width).mean(axis=(2, 4)).astype(jnp.bfloat16)
    level_one = jnp.dot(pooled, fpn_second, preferred_element_type=jnp.float32)
    upsampled = jnp.repeat(jnp.repeat(level_one, 2, axis=1), 2, axis=2)
    level_zero = jnp.dot(grid_rows, fpn_first, preferred_element_type=jnp.float32) + upsampled
    return (level_zero.astype(jnp.bfloat16), level_one.astype(jnp.bfloat16), pooled)

def pyramid_back(top_rows, pooled, fpn_first, fpn_second, grad_zero, grad_one):
    images_here = pooled.shape[0]
    half_grid = pooled.shape[1]
    channels = grad_zero.shape[-1]
    model_width = top_rows.shape[-1]
    grad_one = grad_one + grad_zero.reshape(images_here, half_grid, 2, half_grid, 2, channels).sum(axis=(2, 4))
    zero_b = grad_zero.astype(jnp.bfloat16)
    one_b = grad_one.astype(jnp.bfloat16)
    grid_rows = top_rows.reshape(images_here, GRID, GRID, model_width)
    weight_zero = jnp.einsum('nyxd,nyxc->dc', grid_rows, zero_b, preferred_element_type=jnp.float32)
    weight_one = jnp.einsum('nyxd,nyxc->dc', pooled, one_b, preferred_element_type=jnp.float32)
    back_one = jnp.dot(one_b, fpn_second.T, preferred_element_type=jnp.float32)
    grad_top = jnp.dot(zero_b, fpn_first.T, preferred_element_type=jnp.float32) + 0.25 * jnp.repeat(jnp.repeat(back_one, 2, axis=1), 2, axis=2)
    return (weight_zero, weight_one, grad_top.reshape(images_here * GRID * GRID, model_width))

def window_rows(image_ids, anchor_y, anchor_x, side):
    offsets = jnp.arange(SPAN, dtype=jnp.int32)
    return image_ids[:, None, None] * (side * side) + (anchor_y[:, None, None] + offsets[None, :, None]) * side + anchor_x[:, None, None] + offsets[None, None, :]

def window_pair(image_ids, anchor_y, anchor_x):
    half_grid = GRID // 2
    near_y = jnp.minimum(anchor_y, half_grid - SPAN)
    near_x = jnp.minimum(anchor_x, half_grid - SPAN)
    return (window_rows(image_ids, anchor_y, anchor_x, GRID), window_rows(image_ids, near_y, near_x, half_grid))

def make_crops(level_zero, level_one, image_ids, levels, anchor_y, anchor_x, weights_y, weights_x):
    channels = level_zero.shape[-1]
    rows_zero, rows_one = window_pair(image_ids, anchor_y, anchor_x)
    flat_zero = level_zero.reshape(-1, channels)
    flat_one = level_one.reshape(-1, channels)
    window_cells = jnp.where((levels == 0)[:, None, None, None], flat_zero[rows_zero], flat_one[rows_one]).astype(jnp.float32)
    crop_rows = jnp.einsum('kiu,kjv,kuvc->kcij', weights_y, weights_x, window_cells, precision=HIGH)
    return crop_rows.reshape(crop_rows.shape[0], -1).astype(jnp.bfloat16)

def spread_grads(grad_crops, image_ids, levels, anchor_y, anchor_x, weights_y, weights_x, images_here, channels):
    half_grid = GRID // 2
    grad_cells = grad_crops.astype(jnp.float32).reshape(grad_crops.shape[0], channels, POOLED, POOLED)
    grad_window = jnp.einsum('kiu,kjv,kcij->kuvc', weights_y, weights_x, grad_cells, precision=HIGH)
    at_zero = (levels == 0)[:, None, None, None]
    rows_zero, rows_one = window_pair(image_ids, anchor_y, anchor_x)
    grad_zero = jnp.zeros((images_here * GRID * GRID, channels), jnp.float32).at[rows_zero.reshape(-1)].add(jnp.where(at_zero, grad_window, 0.0).reshape(-1, channels))
    grad_one = jnp.zeros((images_here * half_grid * half_grid, channels), jnp.float32).at[rows_one.reshape(-1)].add(jnp.where(at_zero, 0.0, grad_window).reshape(-1, channels))
    return (grad_zero.reshape(images_here, GRID, GRID, channels), grad_one.reshape(images_here, half_grid, half_grid, channels))

def head_pass(slot_rows, fc6_flat, fc7_weight, cot_rows):
    first_pre = jnp.dot(slot_rows, fc6_flat, preferred_element_type=jnp.float32)
    first_act, first_slope = gelu_parts(first_pre)
    first_b = first_act.astype(jnp.bfloat16)
    second_pre = jnp.dot(first_b, fc7_weight, preferred_element_type=jnp.float32)
    second_act, second_slope = gelu_parts(second_pre)
    grad_second = (cot_rows * second_slope).astype(jnp.bfloat16)
    grad_fc7 = jnp.einsum('rh,rk->hk', first_b, grad_second, preferred_element_type=jnp.float32)
    grad_first = (jnp.dot(grad_second, fc7_weight.T, preferred_element_type=jnp.float32) * first_slope).astype(jnp.bfloat16)
    grad_fc6 = jnp.einsum('rk,rh->kh', slot_rows, grad_first, preferred_element_type=jnp.float32)
    grad_slots = jnp.dot(grad_first, fc6_flat.T, preferred_element_type=jnp.float32).astype(jnp.bfloat16)
    return (grad_slots, grad_fc6, grad_fc7)

def slot_ranks(owner_ids, groups):
    onehot = (owner_ids[:, None] == jnp.arange(groups, dtype=jnp.int32)[None, :]).astype(jnp.int32)
    earlier = jnp.cumsum(onehot, axis=0) - onehot
    return lax.optimization_barrier(jnp.sum(earlier * onehot, axis=1)).astype(jnp.int32)

def rounded(values):
    return lax.optimization_barrier(values.astype(jnp.bfloat16)).astype(jnp.float32)

def reference(images, w_in, w_out, fpn_weight, fc6_weight, fc7_weight, windows, bilinear, owners, cotangent):
    groups = N_DP * N_HEAD
    layer_count = w_in.shape[0]
    fc6_flat = fc6_weight.reshape(-1, HEAD_UNITS)
    per_group = IMG_DEV * BOX_IMG

    def group_terms(group):
        first_image = group * IMG_DEV
        tokens = lax.dynamic_slice_in_dim(images, first_image, IMG_DEV, 0).reshape(IMG_DEV * GRID * GRID, D)
        saved_parts = []
        for layer_idx in range(layer_count):
            result, normed_b, preact, activ_b = block_forward(tokens, w_in[layer_idx], w_out[layer_idx])
            saved_parts.append((tokens, normed_b, preact, activ_b))
            tokens = result
        level_zero, level_one, pooled = pyramid(tokens, fpn_weight[0], fpn_weight[1], IMG_DEV)
        box_windows = lax.dynamic_slice_in_dim(windows, first_image, IMG_DEV, 1).reshape(3, per_group)
        sampling = lax.dynamic_slice_in_dim(bilinear, first_image, IMG_DEV, 3).reshape(2, POOLED, SPAN, per_group)
        weights_y = jnp.transpose(sampling[0], (2, 0, 1))
        weights_x = jnp.transpose(sampling[1], (2, 0, 1))
        image_ids = jnp.repeat(jnp.arange(IMG_DEV, dtype=jnp.int32), BOX_IMG)
        crop_rows = make_crops(level_zero, level_one, image_ids, box_windows[0], box_windows[1], box_windows[2], weights_y, weights_x)
        owner_ids = lax.dynamic_slice_in_dim(owners, first_image, IMG_DEV, 0).reshape(per_group)
        slot_rank = slot_ranks(owner_ids, groups)
        cot_rows = cotangent[owner_ids, group, slot_rank].astype(jnp.float32)
        grad_crops, grad_fc6, grad_fc7 = head_pass(crop_rows, fc6_flat, fc7_weight, cot_rows)
        grad_zero, grad_one = spread_grads(grad_crops, image_ids, box_windows[0], box_windows[1], box_windows[2], weights_y, weights_x, IMG_DEV, CHANNELS)
        weight_zero, weight_one, grad_top = pyramid_back(tokens, pooled, fpn_weight[0], fpn_weight[1], grad_zero, grad_one)
        grad_rows = grad_top.astype(jnp.bfloat16)
        firsts = [None] * layer_count
        seconds = [None] * layer_count
        for layer_idx in reversed(range(layer_count)):
            layer_in, normed_b, preact, activ_b = saved_parts[layer_idx]
            grad_in, grad_pre = block_backward(grad_rows, layer_in, preact, w_in[layer_idx], w_out[layer_idx])
            firsts[layer_idx] = rounded(jnp.dot(normed_b.T, grad_pre, preferred_element_type=jnp.float32))
            seconds[layer_idx] = rounded(jnp.dot(activ_b.T, grad_rows, preferred_element_type=jnp.float32))
            grad_rows = grad_in
        return (jnp.stack(firsts), jnp.stack(seconds), jnp.stack([weight_zero, weight_one]), grad_fc6.reshape(CHANNELS, POOLED * POOLED, HEAD_UNITS), grad_fc7)

    def accumulate(totals, group):
        new_terms = group_terms(group)
        return (jax.tree.map(lambda a, b: a + b, totals, new_terms), None)
    start_sums = (jnp.zeros((layer_count, D, FFW), jnp.float32), jnp.zeros((layer_count, FFW, D), jnp.float32), jnp.zeros((2, D, CHANNELS), jnp.float32), jnp.zeros((CHANNELS, POOLED * POOLED, HEAD_UNITS), jnp.float32), jnp.zeros((HEAD_UNITS, HEAD_UNITS), jnp.float32))
    totals, unused = lax.scan(accumulate, start_sums, jnp.arange(groups, dtype=jnp.int32))
    return (totals[0], totals[1], totals[2], totals[3], totals[4])
```

```python
import math

import jax
import jax.numpy as jnp
import numpy as np
from jax import lax
from jax.experimental import pallas as pl
from jax.experimental.pallas import tpu as pltpu
from jax.sharding import PartitionSpec as P

GRID = 12
HALF = GRID // 2
SPAN = 4
POOLED = 7
BINS = POOLED * POOLED
PAIRS = (BINS + 1) // 2
CELLS = 256

EPS = 1e-06
GELU_C = math.sqrt(2.0 / math.pi)
BF = jnp.bfloat16
F32 = jnp.float32
VMEM_BYTES = 40 * 1024 * 1024

NN = (((1,), (0,)), ((), ()))
NT = (((1,), (1,)), ((), ()))
TN = (((0,), (0,)), ((), ()))


def mm(left, right, dims=NN):
    return lax.dot_general(left, right, dims, preferred_element_type=F32)


def gelu_parts(values):
    inner_arg = GELU_C * (values + 0.044715 * values * values * values)
    tangent = jnp.tanh(inner_arg)
    result = 0.5 * values * (1.0 + tangent)
    slope = 0.5 * (1.0 + tangent) + 0.5 * values * (1.0 - tangent * tangent) * GELU_C * (
        1.0 + 3.0 * 0.044715 * values * values
    )
    return (result, slope)


def norm_parts(tokens):
    floats = tokens.astype(F32)
    centred = floats - jnp.mean(floats, axis=-1, keepdims=True)
    scale_inv = lax.rsqrt(jnp.mean(centred * centred, axis=-1, keepdims=True) + EPS)
    return (centred * scale_inv, scale_inv)


def call(body, outs, args, name, scratch=(), smem_first=False, flops=0, nbytes=0):
    specs = [pl.BlockSpec(memory_space=pltpu.VMEM) for _ in args]
    if smem_first:
        specs[0] = pl.BlockSpec(memory_space=pltpu.SMEM)
    return pl.pallas_call(
        body,
        out_shape=[jax.ShapeDtypeStruct(s, d) for s, d in outs],
        in_specs=specs,
        out_specs=[pl.BlockSpec(memory_space=pltpu.VMEM) for _ in outs],
        scratch_shapes=list(scratch),
        compiler_params=pltpu.CompilerParams(vmem_limit_bytes=VMEM_BYTES),
        cost_estimate=pl.CostEstimate(flops=flops, bytes_accessed=nbytes, transcendentals=0),
        name=name,
    )(*args)


def ring(axis, shift):
    size = lax.axis_size(axis)
    return [(i, (i + shift) % size) for i in range(size)]


def shifted(value, axis, shift):
    return lax.ppermute(value, axis, ring(axis, shift))


def shifted_y(value, shift):
    return shifted(value, "dp", 2 * shift)


def core_swapped(value):
    return lax.ppermute(value, "dp", [(i, i ^ 1) for i in range(lax.axis_size("dp"))])


def pyramid_body(top_ref, weight_ref, avg_ref, place_ref, levels_ref, pooled_ref):
    top = top_ref[...]
    pooled = mm(avg_ref[...], top).astype(BF)
    pooled_ref[...] = pooled
    weights = weight_ref[...]
    from_top = mm(weights, top, NT)
    from_pooled = mm(weights, pooled, NT)
    half = weights.shape[0] // 8
    for s in range(4):
        base = 2 * half * s
        one = from_pooled[base + half : base + 2 * half]
        zero = from_top[base : base + half] + one
        levels_ref[s] = (
            mm(zero.astype(BF), place_ref[0]) + mm(one.astype(BF), place_ref[1])
        ).astype(BF)


def top_grad_body(z0_ref, z1_ref, z2_ref, z3_ref, weight_ref, grad_ref, rows_ref):
    rows = jnp.concatenate([z0_ref[...], z1_ref[...], z2_ref[...], z3_ref[...]], axis=0)
    rows_ref[...] = rows
    grad_ref[...] = mm(rows, weight_ref[...], TN).astype(BF)


def crops_body(
    sec_ref, levels_ref, r0_ref, r1_ref, r2_ref, rows_ref, cols_ref, fc6_ref, part_ref, crops_ref
):
    is_last = sec_ref[0] == 3
    arrived = r0_ref[...] + r1_ref[...] + r2_ref[...]
    own = jnp.where(is_last, levels_ref[3], arrived)
    blank = jnp.zeros_like(own)
    both = jnp.concatenate(
        [jnp.concatenate([own, blank], axis=1), jnp.concatenate([blank, own], axis=1)], axis=0
    )

    def weights(b):
        if b >= BINS:
            return jnp.zeros((rows_ref.shape[1], CELLS), BF)
        return (rows_ref[b // POOLED] * cols_ref[b % POOLED]).astype(BF)

    for p in range(PAIRS):
        pair = jnp.concatenate([weights(2 * p), weights(2 * p + 1)], axis=1)
        crops_ref[:, 128 * p : 128 * (p + 1)] = mm(pair, both, NT).astype(BF)
    part_ref[...] = mm(crops_ref[...], fc6_ref[...]).astype(BF)


def head_body(
    sec_ref,
    p0_ref,
    p1_ref,
    p2_ref,
    p3_ref,
    cot_ref,
    fc7_ref,
    fc6_ref,
    rows_ref,
    cols_ref,
    spread_ref,
    first_ref,
    second_ref,
    grad_ref,
    maps_ref,
    parts_ref,
    back_ref,
):
    sec = sec_ref[0]
    for d, ref in enumerate((p0_ref, p1_ref, p2_ref, p3_ref)):
        parts_ref[lax.rem(sec + 4 - d, 4)] = ref[...].astype(F32)
    first_pre = parts_ref[0] + parts_ref[1] + parts_ref[2] + parts_ref[3]
    first_act, first_slope = gelu_parts(first_pre)
    first_b = first_act.astype(BF)
    first_ref[...] = first_b
    second_pre = mm(first_b, fc7_ref[...])
    second_slope = gelu_parts(second_pre)[1]
    grad_second = (cot_ref[...].astype(F32) * second_slope).astype(BF)
    second_ref[...] = grad_second
    grad_first = (mm(grad_second, fc7_ref[...], NT) * first_slope).astype(BF)
    grad_ref[...] = grad_first
    back_ref[...] = mm(fc6_ref[...], grad_first, NT).astype(BF)
    channels = back_ref.shape[0] // (2 * PAIRS)

    def weights(b):
        if b >= BINS:
            return jnp.zeros((rows_ref.shape[1], CELLS), BF)
        return (rows_ref[b // POOLED] * cols_ref[b % POOLED]).astype(BF)

    total = jnp.zeros((channels, CELLS), F32)
    for p in range(PAIRS):
        lo = 2 * p * channels
        left = jnp.concatenate(
            [back_ref[lo : lo + channels], back_ref[lo + channels : lo + 2 * channels]], axis=1
        )
        right = jnp.concatenate([weights(2 * p), weights(2 * p + 1)], axis=0)
        total = total + mm(left, right)
    total_b = total.astype(BF)
    maps_ref[:channels] = mm(total_b, spread_ref[0]).astype(BF)
    maps_ref[channels:] = mm(total_b, spread_ref[1]).astype(BF)


def head_grads_body(
    grad_ref, crops_ref, second_ref, first_ref, maps_ref, order_ref, top_ref, pooled_ref, out_ref
):
    wide = crops_ref.shape[1]
    units = first_ref.shape[1]
    out_ref[:, :wide] = mm(grad_ref[...], crops_ref[...], TN).astype(BF)
    out_ref[:, wide : wide + units] = mm(second_ref[...], first_ref[...], TN).astype(BF)
    ordered = mm(order_ref[...], maps_ref[...]).astype(BF)
    half = ordered.shape[0] // 2
    out_ref[:half, wide + units :] = mm(ordered[:half], top_ref[...]).astype(BF)
    out_ref[half:, wide + units :] = mm(ordered[half:], pooled_ref[...]).astype(BF)


def first_grad_body(
    core_ref, a0_ref, a1_ref, a2_ref, a3_ref, g0_ref, g1_ref, g2_ref, g3_ref, mine_ref, other_ref
):
    is_zero = core_ref[0] == 0
    lefts = (a0_ref, a1_ref, a2_ref, a3_ref)
    rights = (g0_ref, g1_ref, g2_ref, g3_ref)
    total = mm(lefts[0][...], rights[0][...], TN)
    for d in range(1, 4):
        total = total + mm(lefts[d][...], rights[d][...], TN)
    rows = mine_ref.shape[1]
    for y in range(4):
        low = total[2 * y * rows : (2 * y + 1) * rows]
        high = total[(2 * y + 1) * rows : (2 * y + 2) * rows]
        mine_ref[y] = jnp.where(is_zero, low, high).astype(BF)
        other_ref[y] = jnp.where(is_zero, high, low).astype(BF)


def second_grad_body(
    core_ref, a0_ref, a1_ref, a2_ref, a3_ref, g0_ref, g1_ref, g2_ref, g3_ref, mine_ref, other_ref
):
    is_zero = core_ref[0] == 0
    lefts = (a0_ref, a1_ref, a2_ref, a3_ref)
    rights = (g0_ref, g1_ref, g2_ref, g3_ref)
    total = mm(lefts[0][...], rights[0][...], TN)
    for d in range(1, 4):
        total = total + mm(lefts[d][...], rights[d][...], TN)
    rows = mine_ref.shape[1]
    for z in range(4):
        low = total[z * rows : (z + 1) * rows]
        high = total[(z + 4) * rows : (z + 5) * rows]
        mine_ref[z] = jnp.where(is_zero, low, high).astype(BF)
        other_ref[z] = jnp.where(is_zero, high, low).astype(BF)


def cell_tables():
    index = np.arange(CELLS)
    zero = index < GRID * GRID
    one = (index >= GRID * GRID) & (index < GRID * GRID + HALF * HALF)
    inner = index - GRID * GRID
    row = np.where(zero, index // GRID, np.where(one, inner // HALF, -9))
    col = np.where(zero, index % GRID, np.where(one, inner % HALF, -9))
    return zero, one, row.astype(np.int32), col.astype(np.int32)


def grid_constants():
    cells = np.arange(GRID * GRID)
    block = (cells // GRID // 2) * HALF + (cells % GRID) // 2
    average = 0.25 * (block[:, None] == block[None, :])
    place = np.zeros((2, GRID * GRID, CELLS))
    place[0, cells, cells] = 1.0
    for b in range(HALF * HALF):
        place[1, np.where(block == b)[0][0], GRID * GRID + b] = 1.0
    spread = np.zeros((2, CELLS, GRID * GRID))
    spread[0, cells, cells] = 1.0
    spread[1, GRID * GRID + block, cells] = 0.25
    return average, place, spread


def sampling_tables(windows, bilinear):
    zero, one, row, col = cell_tables()
    levels = windows[0, 0][None, :, None]
    corner_y = windows[1, 0][None, :, None]
    corner_x = windows[2, 0][None, :, None]
    zero = jnp.asarray(zero)[None, None, :]
    one = jnp.asarray(one)[None, None, :]
    row = jnp.asarray(row)[None, None, :]
    col = jnp.asarray(col)[None, None, :]
    box_zero = levels == 0
    forward = jnp.where(box_zero, zero, one)
    backward = jnp.where(box_zero, zero | one, one)
    halved = box_zero & one
    rows = 0.0
    cols = 0.0
    for u in range(SPAN):
        weight_y = bilinear[0, :, u, 0, :][:, :, None]
        weight_x = bilinear[1, :, u, 0, :][:, :, None]
        at_y = corner_y + u
        at_x = corner_x + u
        rows = rows + jnp.where(row == jnp.where(halved, at_y // 2, at_y), weight_y, 0.0)
        cols = cols + jnp.where(col == jnp.where(halved, at_x // 2, at_x), weight_x, 0.0)
    return jnp.where(forward, rows, 0.0), jnp.where(backward, rows, 0.0), cols


def slot_rows(owner_ids, arrived):
    boxes = owner_ids.shape[0]
    index = jnp.arange(boxes)
    same = (owner_ids[:, None] == owner_ids[None, :]) & (index[None, :] < index[:, None])
    rank = jnp.sum(same.astype(jnp.int32), axis=1)
    slots = arrived.shape[1]
    flat = arrived.reshape(-1, arrived.shape[2])
    pick = (owner_ids * slots + rank)[:, None] == jnp.arange(flat.shape[0])[None, :]
    return mm(pick.astype(BF), flat).astype(BF)


def per_device(
    images, w_in, w_out, fpn_weight, fc6_weight, fc7_weight, windows, bilinear, owners, cotangent
):
    section = lax.axis_index("section")
    dp = lax.axis_index("dp")
    z_here = lax.axis_index("head")
    y_here = dp // 2
    core = dp % 2
    w_first = w_in[0]
    w_second = w_out[0]
    width = images.shape[2]
    inner = w_first.shape[1]
    channels = fc6_weight.shape[0]
    units = fc6_weight.shape[2]
    sec_arr = section.astype(jnp.int32).reshape(1)
    core_arr = core.astype(jnp.int32).reshape(1)
    average, place, spread = grid_constants()
    average = jnp.asarray(average, BF)
    place = jnp.asarray(place, BF)
    spread = jnp.asarray(spread, BF)

    fpn_rows = jnp.transpose(fpn_weight, (0, 2, 1)).reshape(2 * channels, width)
    fpn_all = lax.all_gather(fpn_rows, "section", axis=0, tiled=True)
    fc6_rows = jnp.pad(
        jnp.transpose(fc6_weight, (1, 0, 2)), ((0, 2 * PAIRS - BINS), (0, 0), (0, 0))
    ).reshape(2 * PAIRS * channels, units)
    rows_fwd, rows_bwd, cols_all = sampling_tables(windows, bilinear)

    tokens = images[0]
    for tick in range(4):
        normed, scale_inv = norm_parts(tokens)
        normed_b = normed.astype(BF)
        preact = mm(normed_b, w_first)
        activ, slope = gelu_parts(preact)
        activ_b = activ.astype(BF)
        result = (tokens.astype(F32) + mm(activ_b, w_second)).astype(BF)
        if tick == 0:
            padded = jnp.pad(cotangent[0], ((0, 0), (0, 2), (0, 0)))
            padded, result = lax.optimization_barrier((padded, result))
            cot_arrived = lax.all_to_all(
                padded, ("dp", "head"), split_axis=0, concat_axis=0, tiled=True
            )
        if tick < 3:
            incoming = lax.ppermute(result, "section", [(tick, tick + 1)])
            tokens = jnp.where(section == tick + 1, incoming, tokens)
    top = result
    cot_rows = slot_rows(owners[0, :, 0], cot_arrived)

    levels, pooled = call(
        pyramid_body,
        [((4, channels, CELLS), BF), (top.shape, BF)],
        (top, fpn_all, average, place),
        "pyramid",
        flops=10**9,
        nbytes=3 * 10**6,
    )
    sent = [lax.ppermute(levels[s], "section", [(3, s)]) for s in range(3)]
    boxes = windows.shape[2]
    part, crops = call(
        crops_body,
        [((boxes, units), BF), ((boxes, 2 * PAIRS * channels), BF)],
        (sec_arr, levels, *sent, rows_fwd, cols_all, fc6_rows),
        "crops",
        smem_first=True,
        flops=10**9,
        nbytes=6 * 10**6,
    )
    parts = [part] + [shifted(part, "section", d) for d in (1, 2, 3)]
    first_b, grad_second, grad_first, maps = call(
        head_body,
        [((boxes, units), BF)] * 3 + [((2 * channels, GRID * GRID), BF)],
        (sec_arr, *parts, cot_rows, fc7_weight, fc6_rows, rows_bwd, cols_all, spread),
        "head",
        scratch=(
            pltpu.VMEM((4, boxes, units), F32),
            pltpu.VMEM((2 * PAIRS * channels, boxes), BF),
        ),
        smem_first=True,
        flops=10**9,
        nbytes=6 * 10**6,
    )
    returned = [lax.ppermute(maps, "section", [(s, 3)]) for s in range(3)]
    grad_out, map_rows = call(
        top_grad_body,
        [(top.shape, BF), ((8 * channels, GRID * GRID), BF)],
        (*returned, maps, fpn_all),
        "top_grad",
        flops=10**9,
        nbytes=3 * 10**6,
    )

    quarter = inner // 4

    def piece(array, index):
        return lax.dynamic_slice_in_dim(array, index * quarter, quarter, 1)

    act_parts = [piece(activ_b, y_here)] + [
        shifted_y(piece(activ_b, (y_here + d) % 4), d) for d in (1, 2, 3)
    ]
    normed_parts = [normed_b] + [shifted(normed_b, "head", d) for d in (1, 2, 3)]

    for tick in range(4):
        grad_act = mm(grad_out, w_second, NT)
        grad_pre = (grad_act * slope).astype(BF)
        if tick == 3:
            break
        grad_norm = mm(grad_pre, w_first, NT)
        grad_tok = scale_inv * (
            grad_norm
            - jnp.mean(grad_norm, axis=-1, keepdims=True)
            - normed * jnp.mean(grad_norm * normed, axis=-1, keepdims=True)
        )
        grad_in = (grad_out.astype(F32) + grad_tok).astype(BF)
        if tick == 0:
            grad_in, map_rows = lax.optimization_barrier((grad_in, map_rows))
            order = np.zeros((8 * channels, 8 * channels))
            for r in range(8 * channels):
                order[r, ((r % 16) // 4) * 2 * channels + (r // 16) * 4 + r % 4] = 1.0
            (stacked,) = call(
                head_grads_body,
                [((units, crops.shape[1] + units + width), BF)],
                (
                    grad_first,
                    crops,
                    grad_second,
                    first_b,
                    map_rows,
                    jnp.asarray(order, BF),
                    top,
                    pooled,
                ),
                "head_grads",
                flops=10**9,
                nbytes=8 * 10**6,
            )
            stacked = lax.psum_scatter(stacked, "dp", scatter_dimension=0, tiled=True)
            stacked = lax.psum_scatter(stacked, "head", scatter_dimension=0, tiled=True)
        incoming = lax.ppermute(grad_in, "section", [(3 - tick, 2 - tick)])
        grad_out = jnp.where(section == 2 - tick, incoming, grad_out)

    out_parts = [grad_out] + [shifted_y(grad_out, d) for d in (1, 2, 3)]
    pre_parts = [piece(grad_pre, z_here)] + [
        shifted(piece(grad_pre, (z_here + d) % 4), "head", d) for d in (1, 2, 3)
    ]
    rows_in = width // 8
    rows_out = quarter // 8
    mine_second, other_second = call(
        second_grad_body,
        [((4, rows_out, width), BF)] * 2,
        (core_arr, *act_parts, *out_parts),
        "second_grad",
        smem_first=True,
        flops=2 * 10**9,
        nbytes=5 * 10**6,
    )
    mine_first, other_first = call(
        first_grad_body,
        [((4, rows_in, quarter), BF)] * 2,
        (core_arr, *normed_parts, *pre_parts),
        "first_grad",
        smem_first=True,
        flops=2 * 10**9,
        nbytes=5 * 10**6,
    )
    pair_second = mine_second.astype(F32) + core_swapped(other_second).astype(F32)
    pair_first = mine_first.astype(F32) + core_swapped(other_first).astype(F32)

    def block(array, index):
        return lax.dynamic_index_in_dim(array, index, 0, keepdims=False)

    grad_w_out = block(pair_second, z_here)
    for d in (1, 2, 3):
        grad_w_out = grad_w_out + shifted(
            block(pair_second, (z_here + d) % 4).astype(BF), "head", d
        ).astype(F32)
    rows_sum = block(pair_first, y_here)
    for d in (1, 2, 3):
        rows_sum = rows_sum + shifted_y(
            block(pair_first, (y_here + d) % 4).astype(BF), d
        ).astype(F32)
    last_rows = rows_in // 4

    def strip(index):
        return lax.dynamic_slice_in_dim(rows_sum, index * last_rows, last_rows, 0)

    grad_w_in = jnp.zeros((last_rows, inner), F32)
    grad_w_in = lax.dynamic_update_slice(grad_w_in, strip(z_here), (0, z_here * quarter))
    for d in (1, 2, 3):
        got = shifted(strip((z_here + d) % 4).astype(BF), "head", d).astype(F32)
        grad_w_in = lax.dynamic_update_slice(grad_w_in, got, (0, ((z_here - d) % 4) * quarter))

    wide = crops.shape[1]
    fc6_part = stacked[:, :wide].reshape(-1, 2 * PAIRS, channels)[:, :BINS]
    fc6_out = jnp.transpose(fc6_part.astype(F32), (2, 1, 0))
    fc7_out = jnp.transpose(stacked[:, wide : wide + units].astype(F32))
    fpn_part = stacked[:, wide + units :].reshape(4, 4, width)
    got = [lax.ppermute(fpn_part[s], "section", [(3, s)]) for s in range(3)]
    own = jnp.where(section == 3, fpn_part[3], got[0] + got[1] + got[2])
    over_z = jnp.stack([own] + [shifted(own, "head", d) for d in (1, 2, 3)])
    over_core = jnp.stack([over_z, core_swapped(over_z)])
    over_y = jnp.stack([over_core] + [shifted_y(over_core, d) for d in (1, 2, 3)])
    row = jnp.arange(2 * channels)
    block_of, inside = row // 4, row % 4
    from_y = (y_here - block_of // 8) % 4
    from_core = (core + (block_of // 4) % 2) % 2
    from_z = (z_here - block_of) % 4
    target = ((from_y * 2 + from_core) * 4 + from_z) * 4 + inside
    ordered = (row[:, None] == target[None, :]).astype(BF)
    fpn_out = mm(ordered, over_y.reshape(2 * channels, width))
    fpn_out = jnp.transpose(fpn_out.reshape(2, channels, width), (0, 2, 1))
    return (grad_w_in[None], grad_w_out[None], fpn_out, fc6_out, fc7_out)


def solution(mesh):
    return jax.shard_map(
        per_device,
        mesh=mesh,
        in_specs=(
            P(("dp", "head"), None, None),
            P("section", None, None),
            P("section", None, None),
            P(None, None, "section"),
            P("section", None, None),
            P(),
            P(None, ("dp", "head"), None),
            P(None, None, None, ("dp", "head"), None),
            P(("dp", "head"), None, None),
            P(("dp", "head"), None, None, None),
        ),
        out_specs=(
            P("section", ("dp", "head"), None),
            P("section", ("dp", "head"), None),
            P(None, None, "section"),
            P("section", None, ("dp", "head")),
            P(None, ("dp", "head")),
        ),
        check_vma=False,
    )
```

```python
import functools
import math

import jax
import jax.numpy as jnp
import numpy as np
from jax import lax
from jax.experimental import pallas as pl
from jax.experimental.pallas import tpu as pltpu
from jax.sharding import PartitionSpec as P

GRID = 12
HALF = GRID // 2
SPAN = 4
POOLED = 7
BINS = POOLED * POOLED
PAIRS = (BINS + 1) // 2
CELLS = 256

EPS = 1e-06
GELU_C = math.sqrt(2.0 / math.pi)
BF = jnp.bfloat16
F32 = jnp.float32
VMEM_BYTES = 18 * 1024 * 1024
STEP = 512

NN = (((1,), (0,)), ((), ()))
NT = (((1,), (1,)), ((), ()))
TN = (((0,), (0,)), ((), ()))


def mm(left, right, dims=NN):
    return lax.dot_general(left, right, dims, preferred_element_type=F32)


def gelu_parts(values):
    inner_arg = GELU_C * (values + 0.044715 * values * values * values)
    tangent = jnp.tanh(inner_arg)
    result = 0.5 * values * (1.0 + tangent)
    slope = 0.5 * (1.0 + tangent) + 0.5 * values * (1.0 - tangent * tangent) * GELU_C * (
        1.0 + 3.0 * 0.044715 * values * values
    )
    return (result, slope)


def norm_parts(tokens):
    floats = tokens.astype(F32)
    centred = floats - jnp.mean(floats, axis=-1, keepdims=True)
    scale_inv = lax.rsqrt(jnp.mean(centred * centred, axis=-1, keepdims=True) + EPS)
    return (centred * scale_inv, scale_inv)


def call(body, outs, args, name, scratch=(), smem_first=False, flops=0, nbytes=0):
    specs = [pl.BlockSpec(memory_space=pltpu.VMEM) for _ in args]
    if smem_first:
        specs[0] = pl.BlockSpec(memory_space=pltpu.SMEM)
    return pl.pallas_call(
        body,
        out_shape=[jax.ShapeDtypeStruct(s, d) for s, d in outs],
        in_specs=specs,
        out_specs=[pl.BlockSpec(memory_space=pltpu.VMEM) for _ in outs],
        scratch_shapes=list(scratch),
        compiler_params=pltpu.CompilerParams(vmem_limit_bytes=VMEM_BYTES),
        cost_estimate=pl.CostEstimate(flops=flops, bytes_accessed=nbytes, transcendentals=0),
        name=name,
    )(*args)


def ring(axis, shift):
    size = lax.axis_size(axis)
    return [(i, (i + shift) % size) for i in range(size)]


def shifted(value, axis, shift):
    return lax.ppermute(value, axis, ring(axis, shift))


def shifted_y(value, shift):
    return shifted(value, "dp", 2 * shift)


def core_swapped(value):
    return lax.ppermute(value, "dp", [(i, i ^ 1) for i in range(lax.axis_size("dp"))])


def gelu_quick(values):
    square = values * values
    half = 0.5 + 0.5 * jnp.tanh(values * (GELU_C + (GELU_C * 0.044715) * square))
    return half, square


def forward_body(tick, sec_ref, *refs):
    if tick == 0:
        old_ref, w1_ref, w2_ref, *outs = refs
        tokens = old_ref[...]
    else:
        old_ref, new_ref, w1_ref, w2_ref, *outs = refs
        tokens = jnp.where(sec_ref[0] == tick, new_ref[...], old_ref[...])
    result_ref = outs[0]
    if tick > 0:
        outs[1][...] = tokens
    normed = norm_parts(tokens)[0].astype(BF)
    if tick == 3:
        outs[2][...] = normed
    total = tokens.astype(F32)
    for lo in range(0, w1_ref.shape[1], STEP):
        values = mm(normed, w1_ref[:, lo : lo + STEP])
        half, square = gelu_quick(values)
        activ = (values * half).astype(BF)
        if tick == 3:
            outs[3][:, lo : lo + STEP] = activ
            outs[4][:, lo : lo + STEP] = half + (values * (2.0 * half) * (1.0 - half)) * (
                GELU_C + (3.0 * 0.044715 * GELU_C) * square
            )
        total = total + mm(activ, w2_ref[lo : lo + STEP, :])
    result_ref[...] = total.astype(BF)


def backward_body(tick, sec_ref, *refs):
    if tick == 0:
        old_ref, slope_ref, tokens_ref, w1_ref, w2_ref, *outs = refs
        grad_out = old_ref[...]
    else:
        old_ref, new_ref, slope_ref, tokens_ref, w1_ref, w2_ref, *outs = refs
        grad_out = jnp.where(sec_ref[0] == 3 - tick, new_ref[...], old_ref[...])
        outs[1][...] = grad_out
    total = jnp.zeros(grad_out.shape, F32)
    for lo in range(0, w1_ref.shape[1], STEP):
        grad_act = mm(grad_out, w2_ref[lo : lo + STEP, :], NT)
        grad_pre = (grad_act * slope_ref[:, lo : lo + STEP]).astype(BF)
        total = total + mm(grad_pre, w1_ref[:, lo : lo + STEP], NT)
    normed, scale_inv = norm_parts(tokens_ref[...])
    grad_tok = scale_inv * (
        total
        - jnp.mean(total, axis=-1, keepdims=True)
        - normed * jnp.mean(total * normed, axis=-1, keepdims=True)
    )
    outs[0][...] = (grad_out.astype(F32) + grad_tok).astype(BF)


def last_backward_body(grad_ref, slope_ref, w2_ref, out_ref):
    grad_out = grad_ref[...]
    for lo in range(0, w2_ref.shape[0], STEP):
        grad_act = mm(grad_out, w2_ref[lo : lo + STEP, :], NT)
        out_ref[:, lo : lo + STEP] = (grad_act * slope_ref[:, lo : lo + STEP]).astype(BF)


def pyramid_body(top_ref, weight_ref, avg_ref, place_ref, levels_ref, pooled_ref):
    top = top_ref[...]
    pooled = mm(avg_ref[...], top).astype(BF)
    pooled_ref[...] = pooled
    weights = weight_ref[...]
    from_top = mm(weights, top, NT)
    from_pooled = mm(weights, pooled, NT)
    half = weights.shape[0] // 8
    for s in range(4):
        base = 2 * half * s
        one = from_pooled[base + half : base + 2 * half]
        zero = from_top[base : base + half] + one
        levels_ref[s] = (
            mm(zero.astype(BF), place_ref[0]) + mm(one.astype(BF), place_ref[1])
        ).astype(BF)


def top_grad_body(z0_ref, z1_ref, z2_ref, z3_ref, weight_ref, grad_ref, rows_ref):
    rows = jnp.concatenate([z0_ref[...], z1_ref[...], z2_ref[...], z3_ref[...]], axis=0)
    rows_ref[...] = rows
    grad_ref[...] = mm(rows, weight_ref[...], TN).astype(BF)


def crops_body(
    sec_ref, levels_ref, r0_ref, r1_ref, r2_ref, rows_ref, cols_ref, fc6_ref, part_ref, crops_ref
):
    is_last = sec_ref[0] == 3
    arrived = r0_ref[...] + r1_ref[...] + r2_ref[...]
    own = jnp.where(is_last, levels_ref[3], arrived)
    blank = jnp.zeros_like(own)
    both = jnp.concatenate(
        [jnp.concatenate([own, blank], axis=1), jnp.concatenate([blank, own], axis=1)], axis=0
    )

    def weights(b):
        if b >= BINS:
            return jnp.zeros((rows_ref.shape[1], CELLS), BF)
        return (rows_ref[b // POOLED] * cols_ref[b % POOLED]).astype(BF)

    for p in range(PAIRS):
        pair = jnp.concatenate([weights(2 * p), weights(2 * p + 1)], axis=1)
        crops_ref[:, 128 * p : 128 * (p + 1)] = mm(pair, both, NT).astype(BF)
    part_ref[...] = mm(crops_ref[...], fc6_ref[...]).astype(BF)


def head_body(
    sec_ref,
    p0_ref,
    p1_ref,
    p2_ref,
    p3_ref,
    cot_ref,
    fc7_ref,
    fc6_ref,
    rows_ref,
    cols_ref,
    spread_ref,
    first_ref,
    second_ref,
    grad_ref,
    maps_ref,
    parts_ref,
    back_ref,
):
    sec = sec_ref[0]
    for d, ref in enumerate((p0_ref, p1_ref, p2_ref, p3_ref)):
        parts_ref[lax.rem(sec + 4 - d, 4)] = ref[...].astype(F32)
    first_pre = parts_ref[0] + parts_ref[1] + parts_ref[2] + parts_ref[3]
    first_act, first_slope = gelu_parts(first_pre)
    first_b = first_act.astype(BF)
    first_ref[...] = first_b
    second_pre = mm(first_b, fc7_ref[...])
    second_slope = gelu_parts(second_pre)[1]
    grad_second = (cot_ref[...].astype(F32) * second_slope).astype(BF)
    second_ref[...] = grad_second
    grad_first = (mm(grad_second, fc7_ref[...], NT) * first_slope).astype(BF)
    grad_ref[...] = grad_first
    back_ref[...] = mm(fc6_ref[...], grad_first, NT).astype(BF)
    channels = back_ref.shape[0] // (2 * PAIRS)

    def weights(b):
        if b >= BINS:
            return jnp.zeros((rows_ref.shape[1], CELLS), BF)
        return (rows_ref[b // POOLED] * cols_ref[b % POOLED]).astype(BF)

    total = jnp.zeros((channels, CELLS), F32)
    for p in range(PAIRS):
        lo = 2 * p * channels
        left = jnp.concatenate(
            [back_ref[lo : lo + channels], back_ref[lo + channels : lo + 2 * channels]], axis=1
        )
        right = jnp.concatenate([weights(2 * p), weights(2 * p + 1)], axis=0)
        total = total + mm(left, right)
    total_b = total.astype(BF)
    maps_ref[:channels] = mm(total_b, spread_ref[0]).astype(BF)
    maps_ref[channels:] = mm(total_b, spread_ref[1]).astype(BF)


def head_grads_body(
    grad_ref, crops_ref, second_ref, first_ref, maps_ref, order_ref, top_ref, pooled_ref, out_ref
):
    wide = crops_ref.shape[1]
    units = first_ref.shape[1]
    out_ref[:, :wide] = mm(grad_ref[...], crops_ref[...], TN).astype(BF)
    out_ref[:, wide : wide + units] = mm(second_ref[...], first_ref[...], TN).astype(BF)
    ordered = mm(order_ref[...], maps_ref[...]).astype(BF)
    half = ordered.shape[0] // 2
    out_ref[:half, wide + units :] = mm(ordered[:half], top_ref[...]).astype(BF)
    out_ref[half:, wide + units :] = mm(ordered[half:], pooled_ref[...]).astype(BF)


def first_grad_body(
    core_ref, a0_ref, a1_ref, a2_ref, a3_ref, g0_ref, g1_ref, g2_ref, g3_ref, mine_ref, other_ref
):
    is_zero = core_ref[0] == 0
    lefts = (a0_ref, a1_ref, a2_ref, a3_ref)
    rights = (g0_ref, g1_ref, g2_ref, g3_ref)
    total = mm(lefts[0][...], rights[0][...], TN)
    for d in range(1, 4):
        total = total + mm(lefts[d][...], rights[d][...], TN)
    rows = mine_ref.shape[1]
    for y in range(4):
        low = total[2 * y * rows : (2 * y + 1) * rows]
        high = total[(2 * y + 1) * rows : (2 * y + 2) * rows]
        mine_ref[y] = jnp.where(is_zero, low, high).astype(BF)
        other_ref[y] = jnp.where(is_zero, high, low).astype(BF)


def second_grad_body(
    core_ref, a0_ref, a1_ref, a2_ref, a3_ref, g0_ref, g1_ref, g2_ref, g3_ref, mine_ref, other_ref
):
    is_zero = core_ref[0] == 0
    lefts = (a0_ref, a1_ref, a2_ref, a3_ref)
    rights = (g0_ref, g1_ref, g2_ref, g3_ref)
    total = mm(lefts[0][...], rights[0][...], TN)
    for d in range(1, 4):
        total = total + mm(lefts[d][...], rights[d][...], TN)
    rows = mine_ref.shape[1]
    for z in range(4):
        low = total[z * rows : (z + 1) * rows]
        high = total[(z + 4) * rows : (z + 5) * rows]
        mine_ref[z] = jnp.where(is_zero, low, high).astype(BF)
        other_ref[z] = jnp.where(is_zero, high, low).astype(BF)


def cell_tables():
    index = np.arange(CELLS)
    zero = index < GRID * GRID
    one = (index >= GRID * GRID) & (index < GRID * GRID + HALF * HALF)
    inner = index - GRID * GRID
    row = np.where(zero, index // GRID, np.where(one, inner // HALF, -9))
    col = np.where(zero, index % GRID, np.where(one, inner % HALF, -9))
    return zero, one, row.astype(np.int32), col.astype(np.int32)


def grid_constants():
    cells = np.arange(GRID * GRID)
    block = (cells // GRID // 2) * HALF + (cells % GRID) // 2
    average = 0.25 * (block[:, None] == block[None, :])
    place = np.zeros((2, GRID * GRID, CELLS))
    place[0, cells, cells] = 1.0
    for b in range(HALF * HALF):
        place[1, np.where(block == b)[0][0], GRID * GRID + b] = 1.0
    spread = np.zeros((2, CELLS, GRID * GRID))
    spread[0, cells, cells] = 1.0
    spread[1, GRID * GRID + block, cells] = 0.25
    return average, place, spread


def sampling_tables(windows, bilinear):
    zero, one, row, col = cell_tables()
    levels = windows[0, 0][None, :, None]
    corner_y = windows[1, 0][None, :, None]
    corner_x = windows[2, 0][None, :, None]
    zero = jnp.asarray(zero)[None, None, :]
    one = jnp.asarray(one)[None, None, :]
    row = jnp.asarray(row)[None, None, :]
    col = jnp.asarray(col)[None, None, :]
    box_zero = levels == 0
    forward = jnp.where(box_zero, zero, one)
    backward = jnp.where(box_zero, zero | one, one)
    halved = box_zero & one
    rows = 0.0
    cols = 0.0
    for u in range(SPAN):
        weight_y = bilinear[0, :, u, 0, :][:, :, None]
        weight_x = bilinear[1, :, u, 0, :][:, :, None]
        at_y = corner_y + u
        at_x = corner_x + u
        rows = rows + jnp.where(row == jnp.where(halved, at_y // 2, at_y), weight_y, 0.0)
        cols = cols + jnp.where(col == jnp.where(halved, at_x // 2, at_x), weight_x, 0.0)
    return jnp.where(forward, rows, 0.0), jnp.where(backward, rows, 0.0), cols


def slot_rows(owner_ids, arrived):
    boxes = owner_ids.shape[0]
    index = jnp.arange(boxes)
    same = (owner_ids[:, None] == owner_ids[None, :]) & (index[None, :] < index[:, None])
    rank = jnp.sum(same.astype(jnp.int32), axis=1)
    slots = arrived.shape[1]
    flat = arrived.reshape(-1, arrived.shape[2])
    pick = (owner_ids * slots + rank)[:, None] == jnp.arange(flat.shape[0])[None, :]
    return mm(pick.astype(BF), flat).astype(BF)


def per_device(
    images, w_in, w_out, fpn_weight, fc6_weight, fc7_weight, windows, bilinear, owners, cotangent
):
    section = lax.axis_index("section")
    dp = lax.axis_index("dp")
    z_here = lax.axis_index("head")
    y_here = dp // 2
    core = dp % 2
    w_first = w_in[0]
    w_second = w_out[0]
    width = images.shape[2]
    inner = w_first.shape[1]
    channels = fc6_weight.shape[0]
    units = fc6_weight.shape[2]
    sec_arr = section.astype(jnp.int32).reshape(1)
    core_arr = core.astype(jnp.int32).reshape(1)
    average, place, spread = grid_constants()
    average = jnp.asarray(average, BF)
    place = jnp.asarray(place, BF)
    spread = jnp.asarray(spread, BF)

    fpn_rows = jnp.transpose(fpn_weight, (0, 2, 1)).reshape(2 * channels, width)
    fpn_all = lax.all_gather(fpn_rows, "section", axis=0, tiled=True)
    fc6_rows = jnp.pad(
        jnp.transpose(fc6_weight, (1, 0, 2)), ((0, 2 * PAIRS - BINS), (0, 0), (0, 0))
    ).reshape(2 * PAIRS * channels, units)
    rows_fwd, rows_bwd, cols_all = sampling_tables(windows, bilinear)

    tokens = images[0]
    shape = tokens.shape
    wide_shape = (shape[0], inner)
    incoming = None
    for tick in range(4):
        outs = [(shape, BF)]
        if tick > 0:
            outs.append((shape, BF))
        if tick == 3:
            outs += [(shape, BF), (wide_shape, BF), (wide_shape, F32)]
        inputs = (tokens,) if tick == 0 else (tokens, incoming)
        results = call(
            functools.partial(forward_body, tick),
            outs,
            (sec_arr, *inputs, w_first, w_second),
            f"block_forward_{tick}",
            smem_first=True,
            flops=3 * 10**9,
            nbytes=18 * 10**6,
        )
        result = results[0]
        if tick > 0:
            tokens = results[1]
        if tick == 3:
            normed_b, activ_b, slope = results[2:]
            break
        if tick == 0:
            padded = jnp.pad(cotangent[0], ((0, 0), (0, 2), (0, 0)))
            padded, result = lax.optimization_barrier((padded, result))
            cot_arrived = lax.all_to_all(
                padded, ("dp", "head"), split_axis=0, concat_axis=0, tiled=True
            )
        incoming = lax.ppermute(result, "section", [(tick, tick + 1)])
        if tick == 0:
            incoming, cot_arrived = lax.optimization_barrier((incoming, cot_arrived))
            cot_rows = slot_rows(owners[0, :, 0], cot_arrived)
        if tick == 1:
            tables = (rows_fwd, rows_bwd, cols_all, fc6_rows, cot_rows, fpn_all)
            incoming, tables = lax.optimization_barrier((incoming, tables))
            rows_fwd, rows_bwd, cols_all, fc6_rows, cot_rows, fpn_all = tables
    top = result

    levels, pooled = call(
        pyramid_body,
        [((4, channels, CELLS), BF), (top.shape, BF)],
        (top, fpn_all, average, place),
        "pyramid",
        flops=10**9,
        nbytes=3 * 10**6,
    )
    sent = [lax.ppermute(levels[s], "section", [(3, s)]) for s in range(3)]
    boxes = windows.shape[2]
    part, crops = call(
        crops_body,
        [((boxes, units), BF), ((boxes, 2 * PAIRS * channels), BF)],
        (sec_arr, levels, *sent, rows_fwd, cols_all, fc6_rows),
        "crops",
        smem_first=True,
        flops=10**9,
        nbytes=6 * 10**6,
    )
    parts = [part] + [shifted(part, "section", d) for d in (1, 2, 3)]
    normed_b, part = lax.optimization_barrier((normed_b, part))
    normed_parts = [normed_b] + [shifted(normed_b, "head", d) for d in (1, 2, 3)]
    first_b, grad_second, grad_first, maps = call(
        head_body,
        [((boxes, units), BF)] * 3 + [((2 * channels, GRID * GRID), BF)],
        (sec_arr, *parts, cot_rows, fc7_weight, fc6_rows, rows_bwd, cols_all, spread),
        "head",
        scratch=(
            pltpu.VMEM((4, boxes, units), F32),
            pltpu.VMEM((2 * PAIRS * channels, boxes), BF),
        ),
        smem_first=True,
        flops=10**9,
        nbytes=6 * 10**6,
    )
    returned = [lax.ppermute(maps, "section", [(s, 3)]) for s in range(3)]
    grad_out, map_rows = call(
        top_grad_body,
        [(top.shape, BF), ((8 * channels, GRID * GRID), BF)],
        (*returned, maps, fpn_all),
        "top_grad",
        flops=10**9,
        nbytes=3 * 10**6,
    )

    quarter = inner // 4

    def piece(array, index):
        return lax.dynamic_slice_in_dim(array, index * quarter, quarter, 1)

    act_pieces = [piece(activ_b, (y_here + d) % 4) for d in range(4)]

    incoming = None
    for tick in range(3):
        outs = [(shape, BF)]
        if tick > 0:
            outs.append((shape, BF))
        inputs = (grad_out,) if tick == 0 else (grad_out, incoming)
        results = call(
            functools.partial(backward_body, tick),
            outs,
            (sec_arr, *inputs, slope, tokens, w_first, w_second),
            f"block_backward_{tick}",
            smem_first=True,
            flops=3 * 10**9,
            nbytes=18 * 10**6,
        )
        grad_in = results[0]
        if tick > 0:
            grad_out = results[1]
        if tick == 0:
            grad_in, map_rows = lax.optimization_barrier((grad_in, map_rows))
            incoming = lax.ppermute(grad_in, "section", [(3, 2)])
            order = np.zeros((8 * channels, 8 * channels))
            for r in range(8 * channels):
                order[r, ((r % 16) // 4) * 2 * channels + (r // 16) * 4 + r % 4] = 1.0
            (stacked,) = call(
                head_grads_body,
                [((units, crops.shape[1] + units + width), BF)],
                (
                    grad_first,
                    crops,
                    grad_second,
                    first_b,
                    map_rows,
                    jnp.asarray(order, BF),
                    top,
                    pooled,
                ),
                "head_grads",
                flops=10**9,
                nbytes=8 * 10**6,
            )
            incoming, stacked = lax.optimization_barrier((incoming, stacked))
            stacked = lax.psum_scatter(stacked, "dp", scatter_dimension=0, tiled=True)
        elif tick == 1:
            grad_in, act_pieces = lax.optimization_barrier((grad_in, act_pieces))
            incoming = lax.ppermute(grad_in, "section", [(2, 1)])
            act_parts = act_pieces[:1] + [shifted_y(act_pieces[d], d) for d in (1, 2, 3)]
        else:
            incoming = lax.ppermute(grad_in, "section", [(1, 0)])
            held = (incoming, act_parts, normed_parts, stacked)
            incoming, act_parts, normed_parts, stacked = lax.optimization_barrier(held)
    grad_out = jnp.where(section == 0, incoming, grad_out)

    stacked = lax.psum_scatter(stacked, "head", scatter_dimension=0, tiled=True)
    out_parts = [grad_out] + [shifted_y(grad_out, d) for d in (1, 2, 3)]
    (grad_pre,) = call(
        last_backward_body,
        [(wide_shape, BF)],
        (grad_out, slope, w_second),
        "block_backward_3",
        flops=2 * 10**9,
        nbytes=10 * 10**6,
    )
    pre_parts = [piece(grad_pre, z_here)] + [
        shifted(piece(grad_pre, (z_here + d) % 4), "head", d) for d in (1, 2, 3)
    ]
    rows_in = width // 8
    rows_out = quarter // 8
    mine_first, other_first = call(
        first_grad_body,
        [((4, rows_in, quarter), BF)] * 2,
        (core_arr, *normed_parts, *pre_parts),
        "first_grad",
        smem_first=True,
        flops=2 * 10**9,
        nbytes=5 * 10**6,
    )
    mine_second, other_second = call(
        second_grad_body,
        [((4, rows_out, width), BF)] * 2,
        (core_arr, *act_parts, *out_parts),
        "second_grad",
        smem_first=True,
        flops=2 * 10**9,
        nbytes=5 * 10**6,
    )
    other_second, stacked = lax.optimization_barrier((other_second, stacked))
    wide = crops.shape[1]
    fpn_part = stacked[:, wide + units :].reshape(4, 4, width)
    fpn_got = [lax.ppermute(fpn_part[s], "section", [(3, s)]) for s in range(3)]
    swapped_second = core_swapped(other_second)
    swapped_first = core_swapped(other_first)
    swapped_second, fpn_got = lax.optimization_barrier((swapped_second, fpn_got))
    pair_second = mine_second.astype(F32) + swapped_second.astype(F32)
    pair_first = mine_first.astype(F32) + swapped_first.astype(F32)

    def block(array, index):
        return lax.dynamic_index_in_dim(array, index, 0, keepdims=False)

    rows_sum = block(pair_first, y_here)
    got_first = [shifted_y(block(pair_first, (y_here + d) % 4).astype(BF), d) for d in (1, 2, 3)]
    grad_w_out = block(pair_second, z_here)
    got_second = [
        shifted(block(pair_second, (z_here + d) % 4).astype(BF), "head", d) for d in (1, 2, 3)
    ]
    own = jnp.where(section == 3, fpn_part[3], fpn_got[0] + fpn_got[1] + fpn_got[2])
    over_z = [own] + [shifted(own, "head", d) for d in (1, 2, 3)]
    got_first, over_z = lax.optimization_barrier((got_first, over_z))
    over_z = jnp.stack(over_z)
    over_core = jnp.stack([over_z, core_swapped(over_z)])
    for got in got_first:
        rows_sum = rows_sum + got.astype(F32)
    last_rows = rows_in // 4

    def strip(index):
        return lax.dynamic_slice_in_dim(rows_sum, index * last_rows, last_rows, 0)

    strips = [shifted(strip((z_here + d) % 4).astype(BF), "head", d) for d in (1, 2, 3)]
    over_y = jnp.stack([over_core] + [shifted_y(over_core, d) for d in (1, 2, 3)])
    for got in got_second:
        grad_w_out = grad_w_out + got.astype(F32)
    grad_w_in = jnp.zeros((last_rows, inner), F32)
    grad_w_in = lax.dynamic_update_slice(grad_w_in, strip(z_here), (0, z_here * quarter))
    for d, got in zip((1, 2, 3), strips):
        grad_w_in = lax.dynamic_update_slice(
            grad_w_in, got.astype(F32), (0, ((z_here - d) % 4) * quarter)
        )

    fc6_part = stacked[:, :wide].reshape(-1, 2 * PAIRS, channels)[:, :BINS]
    fc6_out = jnp.transpose(fc6_part.astype(F32), (2, 1, 0))
    fc7_out = jnp.transpose(stacked[:, wide : wide + units].astype(F32))
    row = jnp.arange(2 * channels)
    block_of, inside = row // 4, row % 4
    from_y = (y_here - block_of // 8) % 4
    from_core = (core + (block_of // 4) % 2) % 2
    from_z = (z_here - block_of) % 4
    target = ((from_y * 2 + from_core) * 4 + from_z) * 4 + inside
    ordered = (row[:, None] == target[None, :]).astype(BF)
    fpn_out = mm(ordered, over_y.reshape(2 * channels, width))
    fpn_out = jnp.transpose(fpn_out.reshape(2, channels, width), (0, 2, 1))
    return (grad_w_in[None], grad_w_out[None], fpn_out, fc6_out, fc7_out)


def solution(mesh):
    return jax.shard_map(
        per_device,
        mesh=mesh,
        in_specs=(
            P(("dp", "head"), None, None),
            P("section", None, None),
            P("section", None, None),
            P(None, None, "section"),
            P("section", None, None),
            P(),
            P(None, ("dp", "head"), None),
            P(None, None, None, ("dp", "head"), None),
            P(("dp", "head"), None, None),
            P(("dp", "head"), None, None, None),
        ),
        out_specs=(
            P("section", ("dp", "head"), None),
            P("section", ("dp", "head"), None),
            P(None, None, "section"),
            P("section", None, ("dp", "head")),
            P(None, ("dp", "head")),
        ),
        check_vma=False,
    )
```

```python
import functools
import math

import jax
import jax.numpy as jnp
import numpy as np
from jax import lax
from jax.experimental import pallas as pl
from jax.experimental.pallas import tpu as pltpu
from jax.sharding import PartitionSpec as P

GRID = 12
HALF = GRID // 2
SPAN = 4
POOLED = 7
BINS = POOLED * POOLED
PAIRS = (BINS + 1) // 2
CELLS = 256

EPS = 1e-06
GELU_C = math.sqrt(2.0 / math.pi)
BF = jnp.bfloat16
F32 = jnp.float32
STEP = 512

NN = (((1,), (0,)), ((), ()))
NT = (((1,), (1,)), ((), ()))
TN = (((0,), (0,)), ((), ()))


def mm(left, right, dims=NN):
    return lax.dot_general(left, right, dims, preferred_element_type=F32)


def gelu_parts(values):
    inner_arg = GELU_C * (values + 0.044715 * values * values * values)
    tangent = jnp.tanh(inner_arg)
    result = 0.5 * values * (1.0 + tangent)
    slope = 0.5 * (1.0 + tangent) + 0.5 * values * (1.0 - tangent * tangent) * GELU_C * (
        1.0 + 3.0 * 0.044715 * values * values
    )
    return (result, slope)


def norm_parts(tokens):
    floats = tokens.astype(F32)
    centred = floats - jnp.mean(floats, axis=-1, keepdims=True)
    scale_inv = lax.rsqrt(jnp.mean(centred * centred, axis=-1, keepdims=True) + EPS)
    return (centred * scale_inv, scale_inv)


class Staged:
    def __init__(self, source, buffer, sems, chunk_axis):
        self.buffer = buffer
        self.shape = buffer.shape
        self.axis = chunk_axis
        self.copies = []
        self.waited = set()
        if chunk_axis is None:
            self.copies.append(pltpu.make_async_copy(source, buffer, sems.at[0]))
        else:
            for j in range(self.shape[chunk_axis] // STEP):
                at = self.part(j)
                self.copies.append(
                    pltpu.make_async_copy(source.at[at], buffer.at[at], sems.at[j])
                )

    def part(self, j):
        span = pl.ds(j * STEP, STEP)
        return (span, slice(None)) if self.axis == 0 else (slice(None), span)

    def start(self, j):
        if j < len(self.copies):
            self.copies[j].start()

    def wait(self, j):
        if j not in self.waited:
            self.waited.add(j)
            self.copies[j].wait()

    def chunk(self, j):
        self.wait(j)
        return self.buffer[self.part(j)]

    def __getitem__(self, index):
        self.wait(0)
        return self.buffer[index]

    def finish(self):
        for j in range(len(self.copies)):
            self.wait(j)


def call(body, outs, args, name, scratch=(), scalars=0, chunks=None, flops=0, nbytes=0, vmem=18):
    chunks = chunks or {}
    count = len(args) - scalars
    axes = [chunks.get(i + scalars) for i in range(count)]
    sizes = [
        1 if axis is None else arg.shape[axis] // STEP for axis, arg in zip(axes, args[scalars:])
    ]

    def kernel(*refs):
        given, sources = refs[:scalars], refs[scalars : len(args)]
        results = refs[len(args) : len(args) + len(outs)]
        rest = refs[len(args) + len(outs) :]
        buffers, sems, extra = rest[:count], rest[count : 2 * count], rest[2 * count :]
        staged = [Staged(*parts) for parts in zip(sources, buffers, sems, axes)]
        for j in range(max(sizes)):
            for item in staged:
                item.start(j)
        body(*given, *staged, *results, *extra)
        for item in staged:
            item.finish()

    return pl.pallas_call(
        kernel,
        out_shape=[jax.ShapeDtypeStruct(s, d) for s, d in outs],
        in_specs=[pl.BlockSpec(memory_space=pltpu.SMEM)] * scalars
        + [pl.BlockSpec(memory_space=pl.ANY)] * count,
        out_specs=[pl.BlockSpec(memory_space=pltpu.VMEM) for _ in outs],
        scratch_shapes=[pltpu.VMEM(arg.shape, arg.dtype) for arg in args[scalars:]]
        + [pltpu.SemaphoreType.DMA((size,)) for size in sizes]
        + list(scratch),
        compiler_params=pltpu.CompilerParams(vmem_limit_bytes=vmem * 1024 * 1024),
        cost_estimate=pl.CostEstimate(flops=flops, bytes_accessed=nbytes, transcendentals=0),
        name=name,
    )(*args)


def in_hbm(array):
    return pltpu.with_memory_space_constraint(array, pltpu.HBM)


def ring(axis, shift):
    size = lax.axis_size(axis)
    return [(i, (i + shift) % size) for i in range(size)]


def shifted(value, axis, shift):
    return lax.ppermute(value, axis, ring(axis, shift))


def shifted_y(value, shift):
    return shifted(value, "dp", 2 * shift)


def core_swapped(value):
    return lax.ppermute(value, "dp", [(i, i ^ 1) for i in range(lax.axis_size("dp"))])


def gelu_quick(values):
    square = values * values
    half = 0.5 + 0.5 * jnp.tanh(values * (GELU_C + (GELU_C * 0.044715) * square))
    return half, square


def forward_body(tick, sec_ref, *refs):
    if tick == 0:
        old_ref, w1_ref, w2_ref, *outs = refs
        tokens = old_ref[...]
    else:
        old_ref, new_ref, w1_ref, w2_ref, *outs = refs
        tokens = jnp.where(sec_ref[0] == tick, new_ref[...], old_ref[...])
    result_ref = outs[0]
    if tick > 0:
        outs[1][...] = tokens
    normed = norm_parts(tokens)[0].astype(BF)
    if tick == 3:
        outs[2][...] = normed
    total = tokens.astype(F32)
    for j in range(w1_ref.shape[1] // STEP):
        lo = j * STEP
        values = mm(normed, w1_ref.chunk(j))
        half, square = gelu_quick(values)
        activ = (values * half).astype(BF)
        if tick == 3:
            outs[3][:, lo : lo + STEP] = activ
            outs[4][:, lo : lo + STEP] = half + (values * (2.0 * half) * (1.0 - half)) * (
                GELU_C + (3.0 * 0.044715 * GELU_C) * square
            )
        total = total + mm(activ, w2_ref.chunk(j))
    result_ref[...] = total.astype(BF)


def backward_body(tick, sec_ref, *refs):
    if tick == 0:
        old_ref, slope_ref, tokens_ref, w1_ref, w2_ref, *outs = refs
        grad_out = old_ref[...]
    else:
        old_ref, new_ref, slope_ref, tokens_ref, w1_ref, w2_ref, *outs = refs
        grad_out = jnp.where(sec_ref[0] == 3 - tick, new_ref[...], old_ref[...])
        outs[1][...] = grad_out
    total = jnp.zeros(grad_out.shape, F32)
    for j in range(w1_ref.shape[1] // STEP):
        grad_act = mm(grad_out, w2_ref.chunk(j), NT)
        grad_pre = (grad_act * slope_ref.chunk(j)).astype(BF)
        total = total + mm(grad_pre, w1_ref.chunk(j), NT)
    normed, scale_inv = norm_parts(tokens_ref[...])
    grad_tok = scale_inv * (
        total
        - jnp.mean(total, axis=-1, keepdims=True)
        - normed * jnp.mean(total * normed, axis=-1, keepdims=True)
    )
    outs[0][...] = (grad_out.astype(F32) + grad_tok).astype(BF)


def last_backward_body(grad_ref, slope_ref, w2_ref, out_ref):
    grad_out = grad_ref[...]
    for j in range(w2_ref.shape[0] // STEP):
        grad_act = mm(grad_out, w2_ref.chunk(j), NT)
        out_ref[:, j * STEP : (j + 1) * STEP] = (grad_act * slope_ref.chunk(j)).astype(BF)


def pyramid_body(top_ref, weight_ref, avg_ref, place_ref, levels_ref, pooled_ref):
    top = top_ref[...]
    pooled = mm(avg_ref[...], top).astype(BF)
    pooled_ref[...] = pooled
    weights = weight_ref[...]
    from_top = mm(weights, top, NT)
    from_pooled = mm(weights, pooled, NT)
    half = weights.shape[0] // 8
    for s in range(4):
        base = 2 * half * s
        one = from_pooled[base + half : base + 2 * half]
        zero = from_top[base : base + half] + one
        levels_ref[s] = (
            mm(zero.astype(BF), place_ref[0]) + mm(one.astype(BF), place_ref[1])
        ).astype(BF)


def top_grad_body(z0_ref, z1_ref, z2_ref, z3_ref, weight_ref, grad_ref, rows_ref):
    rows = jnp.concatenate([z0_ref[...], z1_ref[...], z2_ref[...], z3_ref[...]], axis=0)
    rows_ref[...] = rows
    grad_ref[...] = mm(rows, weight_ref[...], TN).astype(BF)


def crops_body(
    sec_ref, levels_ref, r0_ref, r1_ref, r2_ref, rows_ref, cols_ref, fc6_ref, part_ref, crops_ref
):
    is_last = sec_ref[0] == 3
    arrived = r0_ref[...] + r1_ref[...] + r2_ref[...]
    own = jnp.where(is_last, levels_ref[3], arrived)
    blank = jnp.zeros_like(own)
    both = jnp.concatenate(
        [jnp.concatenate([own, blank], axis=1), jnp.concatenate([blank, own], axis=1)], axis=0
    )

    def weights(b):
        if b >= BINS:
            return jnp.zeros((rows_ref.shape[1], CELLS), BF)
        return (rows_ref[b // POOLED] * cols_ref[b % POOLED]).astype(BF)

    for p in range(PAIRS):
        pair = jnp.concatenate([weights(2 * p), weights(2 * p + 1)], axis=1)
        crops_ref[:, 128 * p : 128 * (p + 1)] = mm(pair, both, NT).astype(BF)
    part_ref[...] = mm(crops_ref[...], fc6_ref[...]).astype(BF)


def head_body(
    sec_ref,
    p0_ref,
    p1_ref,
    p2_ref,
    p3_ref,
    cot_ref,
    fc7_ref,
    fc6_ref,
    rows_ref,
    cols_ref,
    spread_ref,
    first_ref,
    second_ref,
    grad_ref,
    maps_ref,
    parts_ref,
    back_ref,
):
    sec = sec_ref[0]
    for d, ref in enumerate((p0_ref, p1_ref, p2_ref, p3_ref)):
        parts_ref[lax.rem(sec + 4 - d, 4)] = ref[...].astype(F32)
    first_pre = parts_ref[0] + parts_ref[1] + parts_ref[2] + parts_ref[3]
    first_act, first_slope = gelu_parts(first_pre)
    first_b = first_act.astype(BF)
    first_ref[...] = first_b
    second_pre = mm(first_b, fc7_ref[...])
    second_slope = gelu_parts(second_pre)[1]
    grad_second = (cot_ref[...].astype(F32) * second_slope).astype(BF)
    second_ref[...] = grad_second
    grad_first = (mm(grad_second, fc7_ref[...], NT) * first_slope).astype(BF)
    grad_ref[...] = grad_first
    back_ref[...] = mm(fc6_ref[...], grad_first, NT).astype(BF)
    channels = back_ref.shape[0] // (2 * PAIRS)

    def weights(b):
        if b >= BINS:
            return jnp.zeros((rows_ref.shape[1], CELLS), BF)
        return (rows_ref[b // POOLED] * cols_ref[b % POOLED]).astype(BF)

    total = jnp.zeros((channels, CELLS), F32)
    for p in range(PAIRS):
        lo = 2 * p * channels
        left = jnp.concatenate(
            [back_ref[lo : lo + channels], back_ref[lo + channels : lo + 2 * channels]], axis=1
        )
        right = jnp.concatenate([weights(2 * p), weights(2 * p + 1)], axis=0)
        total = total + mm(left, right)
    total_b = total.astype(BF)
    maps_ref[:channels] = mm(total_b, spread_ref[0]).astype(BF)
    maps_ref[channels:] = mm(total_b, spread_ref[1]).astype(BF)


def head_grads_body(
    grad_ref, crops_ref, second_ref, first_ref, maps_ref, order_ref, top_ref, pooled_ref, out_ref
):
    wide = crops_ref.shape[1]
    units = first_ref.shape[1]
    out_ref[:, :wide] = mm(grad_ref[...], crops_ref[...], TN).astype(BF)
    out_ref[:, wide : wide + units] = mm(second_ref[...], first_ref[...], TN).astype(BF)
    ordered = mm(order_ref[...], maps_ref[...]).astype(BF)
    half = ordered.shape[0] // 2
    out_ref[:half, wide + units :] = mm(ordered[:half], top_ref[...]).astype(BF)
    out_ref[half:, wide + units :] = mm(ordered[half:], pooled_ref[...]).astype(BF)


def first_grad_body(
    core_ref, a0_ref, a1_ref, a2_ref, a3_ref, g0_ref, g1_ref, g2_ref, g3_ref, mine_ref, other_ref
):
    is_zero = core_ref[0] == 0
    lefts = (a0_ref, a1_ref, a2_ref, a3_ref)
    rights = (g0_ref, g1_ref, g2_ref, g3_ref)
    total = mm(lefts[0][...], rights[0][...], TN)
    for d in range(1, 4):
        total = total + mm(lefts[d][...], rights[d][...], TN)
    rows = mine_ref.shape[1]
    for y in range(4):
        low = total[2 * y * rows : (2 * y + 1) * rows]
        high = total[(2 * y + 1) * rows : (2 * y + 2) * rows]
        mine_ref[y] = jnp.where(is_zero, low, high).astype(BF)
        other_ref[y] = jnp.where(is_zero, high, low).astype(BF)


def second_grad_body(
    core_ref, a0_ref, a1_ref, a2_ref, a3_ref, g0_ref, g1_ref, g2_ref, g3_ref, mine_ref, other_ref
):
    is_zero = core_ref[0] == 0
    lefts = (a0_ref, a1_ref, a2_ref, a3_ref)
    rights = (g0_ref, g1_ref, g2_ref, g3_ref)
    total = mm(lefts[0][...], rights[0][...], TN)
    for d in range(1, 4):
        total = total + mm(lefts[d][...], rights[d][...], TN)
    rows = mine_ref.shape[1]
    for z in range(4):
        low = total[z * rows : (z + 1) * rows]
        high = total[(z + 4) * rows : (z + 5) * rows]
        mine_ref[z] = jnp.where(is_zero, low, high).astype(BF)
        other_ref[z] = jnp.where(is_zero, high, low).astype(BF)


def cell_tables():
    index = np.arange(CELLS)
    zero = index < GRID * GRID
    one = (index >= GRID * GRID) & (index < GRID * GRID + HALF * HALF)
    inner = index - GRID * GRID
    row = np.where(zero, index // GRID, np.where(one, inner // HALF, -9))
    col = np.where(zero, index % GRID, np.where(one, inner % HALF, -9))
    return zero, one, row.astype(np.int32), col.astype(np.int32)


def grid_constants():
    cells = np.arange(GRID * GRID)
    block = (cells // GRID // 2) * HALF + (cells % GRID) // 2
    average = 0.25 * (block[:, None] == block[None, :])
    place = np.zeros((2, GRID * GRID, CELLS))
    place[0, cells, cells] = 1.0
    for b in range(HALF * HALF):
        place[1, np.where(block == b)[0][0], GRID * GRID + b] = 1.0
    spread = np.zeros((2, CELLS, GRID * GRID))
    spread[0, cells, cells] = 1.0
    spread[1, GRID * GRID + block, cells] = 0.25
    return average, place, spread


def sampling_tables(windows, bilinear):
    zero, one, row, col = cell_tables()
    levels = windows[0, 0][None, :, None]
    corner_y = windows[1, 0][None, :, None]
    corner_x = windows[2, 0][None, :, None]
    zero = jnp.asarray(zero)[None, None, :]
    one = jnp.asarray(one)[None, None, :]
    row = jnp.asarray(row)[None, None, :]
    col = jnp.asarray(col)[None, None, :]
    box_zero = levels == 0
    forward = jnp.where(box_zero, zero, one)
    backward = jnp.where(box_zero, zero | one, one)
    halved = box_zero & one
    rows = 0.0
    cols = 0.0
    for u in range(SPAN):
        weight_y = bilinear[0, :, u, 0, :][:, :, None]
        weight_x = bilinear[1, :, u, 0, :][:, :, None]
        at_y = corner_y + u
        at_x = corner_x + u
        rows = rows + jnp.where(row == jnp.where(halved, at_y // 2, at_y), weight_y, 0.0)
        cols = cols + jnp.where(col == jnp.where(halved, at_x // 2, at_x), weight_x, 0.0)
    return jnp.where(forward, rows, 0.0), jnp.where(backward, rows, 0.0), cols


def slot_rows(owner_ids, arrived):
    boxes = owner_ids.shape[0]
    index = jnp.arange(boxes)
    same = (owner_ids[:, None] == owner_ids[None, :]) & (index[None, :] < index[:, None])
    rank = jnp.sum(same.astype(jnp.int32), axis=1)
    slots = arrived.shape[1]
    flat = arrived.reshape(-1, arrived.shape[2])
    pick = (owner_ids * slots + rank)[:, None] == jnp.arange(flat.shape[0])[None, :]
    return mm(pick.astype(BF), flat).astype(BF)


def per_device(
    images, w_in, w_out, fpn_weight, fc6_weight, fc7_weight, windows, bilinear, owners, cotangent
):
    section = lax.axis_index("section")
    dp = lax.axis_index("dp")
    z_here = lax.axis_index("head")
    y_here = dp // 2
    core = dp % 2
    w_first = in_hbm(w_in[0])
    w_second = in_hbm(w_out[0])
    width = images.shape[2]
    inner = w_first.shape[1]
    channels = fc6_weight.shape[0]
    units = fc6_weight.shape[2]
    sec_arr = section.astype(jnp.int32).reshape(1)
    core_arr = core.astype(jnp.int32).reshape(1)
    average, place, spread = grid_constants()
    average = jnp.asarray(average, BF)
    place = jnp.asarray(place, BF)
    spread = jnp.asarray(spread, BF)

    fpn_rows = jnp.transpose(fpn_weight, (0, 2, 1)).reshape(2 * channels, width)
    fpn_all = lax.all_gather(fpn_rows, "section", axis=0, tiled=True)
    tokens = images[0]
    shape = tokens.shape
    wide_shape = (shape[0], inner)
    incoming = None
    for tick in range(4):
        outs = [(shape, BF)]
        if tick > 0:
            outs.append((shape, BF))
        if tick == 3:
            outs += [(shape, BF), (wide_shape, BF), (wide_shape, F32)]
        inputs = (tokens,) if tick == 0 else (tokens, incoming)
        results = call(
            functools.partial(forward_body, tick),
            outs,
            (sec_arr, *inputs, w_first, w_second),
            f"block_forward_{tick}",
            scalars=1,
            chunks={1 + len(inputs): 1, 2 + len(inputs): 0},
            vmem=34,
            flops=3 * 10**9,
            nbytes=18 * 10**6,
        )
        result = results[0]
        if tick > 0:
            tokens = results[1]
        if tick == 3:
            normed_b, activ_b, slope = results[2:]
            break
        if tick == 0:
            padded = jnp.pad(cotangent[0], ((0, 0), (0, 2), (0, 0)))
            padded, result = lax.optimization_barrier((padded, result))
            cot_arrived = lax.all_to_all(
                padded, ("dp", "head"), split_axis=0, concat_axis=0, tiled=True
            )
        if tick == 1:
            late = (result, windows, bilinear, fc6_weight, cot_arrived)
            result, windows, bilinear, fc6_weight, cot_arrived = lax.optimization_barrier(late)
        incoming = lax.ppermute(result, "section", [(tick, tick + 1)])
        if tick == 0:
            incoming, cot_arrived = lax.optimization_barrier((incoming, cot_arrived))
        if tick == 1:
            cot_rows = slot_rows(owners[0, :, 0], cot_arrived)
            fc6_rows = jnp.pad(
                jnp.transpose(fc6_weight, (1, 0, 2)), ((0, 2 * PAIRS - BINS), (0, 0), (0, 0))
            ).reshape(2 * PAIRS * channels, units)
            rows_fwd, rows_bwd, cols_all = sampling_tables(windows, bilinear)
            tables = (rows_fwd, rows_bwd, cols_all, fc6_rows, cot_rows, fpn_all)
            incoming, tables = lax.optimization_barrier((incoming, tables))
            rows_fwd, rows_bwd, cols_all, fc6_rows, cot_rows, fpn_all = tables
    top = result

    levels, pooled = call(
        pyramid_body,
        [((4, channels, CELLS), BF), (top.shape, BF)],
        (top, in_hbm(fpn_all), in_hbm(average), in_hbm(place)),
        "pyramid",
        flops=10**9,
        nbytes=3 * 10**6,
    )
    sent = [lax.ppermute(levels[s], "section", [(3, s)]) for s in range(3)]
    boxes = windows.shape[2]
    part, crops = call(
        crops_body,
        [((boxes, units), BF), ((boxes, 2 * PAIRS * channels), BF)],
        (sec_arr, levels, *sent, in_hbm(rows_fwd), in_hbm(cols_all), in_hbm(fc6_rows)),
        "crops",
        scalars=1,
        flops=10**9,
        nbytes=6 * 10**6,
    )
    parts = [part] + [shifted(part, "section", d) for d in (1, 2, 3)]
    first_b, grad_second, grad_first, maps = call(
        head_body,
        [((boxes, units), BF)] * 3 + [((2 * channels, GRID * GRID), BF)],
        (
            sec_arr,
            *parts,
            cot_rows,
            in_hbm(fc7_weight),
            in_hbm(fc6_rows),
            in_hbm(rows_bwd),
            in_hbm(cols_all),
            in_hbm(spread),
        ),
        "head",
        scratch=(
            pltpu.VMEM((4, boxes, units), F32),
            pltpu.VMEM((2 * PAIRS * channels, boxes), BF),
        ),
        scalars=1,
        flops=10**9,
        nbytes=6 * 10**6,
    )
    returned = [lax.ppermute(maps, "section", [(s, 3)]) for s in range(3)]
    grad_out, map_rows = call(
        top_grad_body,
        [(top.shape, BF), ((8 * channels, GRID * GRID), BF)],
        (*returned, maps, in_hbm(fpn_all)),
        "top_grad",
        flops=10**9,
        nbytes=3 * 10**6,
    )

    quarter = inner // 4

    def piece(array, index):
        return lax.dynamic_slice_in_dim(array, index * quarter, quarter, 1)

    act_pieces = [piece(activ_b, (y_here + d) % 4) for d in range(4)]

    incoming = None
    for tick in range(3):
        outs = [(shape, BF)]
        if tick > 0:
            outs.append((shape, BF))
        inputs = (grad_out,) if tick == 0 else (grad_out, incoming)
        results = call(
            functools.partial(backward_body, tick),
            outs,
            (sec_arr, *inputs, slope, tokens, w_first, w_second),
            f"block_backward_{tick}",
            scalars=1,
            chunks={1 + len(inputs): 1, 3 + len(inputs): 1, 4 + len(inputs): 0},
            vmem=34,
            flops=3 * 10**9,
            nbytes=18 * 10**6,
        )
        grad_in = results[0]
        if tick > 0:
            grad_out = results[1]
        if tick == 0:
            held = (grad_in, map_rows, normed_b)
            grad_in, map_rows, normed_b = lax.optimization_barrier(held)
            incoming = lax.ppermute(grad_in, "section", [(3, 2)])
            normed_parts = [normed_b] + [shifted(normed_b, "head", d) for d in (1, 2, 3)]
            order = np.zeros((8 * channels, 8 * channels))
            for r in range(8 * channels):
                order[r, ((r % 16) // 4) * 2 * channels + (r // 16) * 4 + r % 4] = 1.0
            (stacked,) = call(
                head_grads_body,
                [((units, crops.shape[1] + units + width), BF)],
                (
                    grad_first,
                    crops,
                    grad_second,
                    first_b,
                    map_rows,
                    in_hbm(jnp.asarray(order, BF)),
                    top,
                    pooled,
                ),
                "head_grads",
                vmem=30,
                flops=10**9,
                nbytes=8 * 10**6,
            )
            incoming, stacked = lax.optimization_barrier((incoming, stacked))
            stacked = lax.psum_scatter(stacked, "dp", scatter_dimension=0, tiled=True)
        elif tick == 1:
            grad_in, act_pieces = lax.optimization_barrier((grad_in, act_pieces))
            incoming = lax.ppermute(grad_in, "section", [(2, 1)])
            act_parts = act_pieces[:1] + [shifted_y(act_pieces[d], d) for d in (1, 2, 3)]
            incoming, normed_parts = lax.optimization_barrier((incoming, normed_parts))
        else:
            incoming = lax.ppermute(grad_in, "section", [(1, 0)])
            incoming, act_parts = lax.optimization_barrier((incoming, act_parts))
    grad_out = jnp.where(section == 0, incoming, grad_out)

    out_parts = [grad_out] + [shifted_y(grad_out, d) for d in (1, 2, 3)]
    (grad_pre,) = call(
        last_backward_body,
        [(wide_shape, BF)],
        (grad_out, slope, w_second),
        "block_backward_3",
        chunks={1: 1, 2: 0},
        flops=2 * 10**9,
        nbytes=10 * 10**6,
    )
    grad_pre, stacked = lax.optimization_barrier((grad_pre, stacked))
    stacked = lax.psum_scatter(stacked, "head", scatter_dimension=0, tiled=True)
    pre_parts = [piece(grad_pre, z_here)] + [
        shifted(piece(grad_pre, (z_here + d) % 4), "head", d) for d in (1, 2, 3)
    ]
    pre_parts, out_parts = lax.optimization_barrier((pre_parts, out_parts))
    rows_in = width // 8
    rows_out = quarter // 8
    mine_first, other_first = call(
        first_grad_body,
        [((4, rows_in, quarter), BF)] * 2,
        (core_arr, *normed_parts, *pre_parts),
        "first_grad",
        vmem=24,
        scalars=1,
        flops=2 * 10**9,
        nbytes=5 * 10**6,
    )
    mine_second, other_second = call(
        second_grad_body,
        [((4, rows_out, width), BF)] * 2,
        (core_arr, *act_parts, *out_parts),
        "second_grad",
        vmem=24,
        scalars=1,
        flops=2 * 10**9,
        nbytes=5 * 10**6,
    )
    other_second, stacked = lax.optimization_barrier((other_second, stacked))
    wide = crops.shape[1]
    fpn_part = stacked[:, wide + units :].reshape(4, 4, width)
    fpn_got = [lax.ppermute(fpn_part[s], "section", [(3, s)]) for s in range(3)]
    swapped_second = core_swapped(other_second)
    swapped_first = core_swapped(other_first)
    swapped_second, fpn_got = lax.optimization_barrier((swapped_second, fpn_got))
    pair_second = mine_second.astype(F32) + swapped_second.astype(F32)
    pair_first = mine_first.astype(F32) + swapped_first.astype(F32)

    def block(array, index):
        return lax.dynamic_index_in_dim(array, index, 0, keepdims=False)

    rows_sum = block(pair_first, y_here)
    got_first = [shifted_y(block(pair_first, (y_here + d) % 4).astype(BF), d) for d in (1, 2, 3)]
    grad_w_out = block(pair_second, z_here)
    got_second = [
        shifted(block(pair_second, (z_here + d) % 4).astype(BF), "head", d) for d in (1, 2, 3)
    ]
    own = jnp.where(section == 3, fpn_part[3], fpn_got[0] + fpn_got[1] + fpn_got[2])
    over_z = [own] + [shifted(own, "head", d) for d in (1, 2, 3)]
    got_first, over_z = lax.optimization_barrier((got_first, over_z))
    over_z = jnp.stack(over_z)
    over_core = jnp.stack([over_z, core_swapped(over_z)])
    for got in got_first:
        rows_sum = rows_sum + got.astype(F32)
    last_rows = rows_in // 4

    def strip(index):
        return lax.dynamic_slice_in_dim(rows_sum, index * last_rows, last_rows, 0)

    strips = [shifted(strip((z_here + d) % 4).astype(BF), "head", d) for d in (1, 2, 3)]
    over_y = jnp.stack([over_core] + [shifted_y(over_core, d) for d in (1, 2, 3)])
    for got in got_second:
        grad_w_out = grad_w_out + got.astype(F32)
    grad_w_in = jnp.zeros((last_rows, inner), F32)
    grad_w_in = lax.dynamic_update_slice(grad_w_in, strip(z_here), (0, z_here * quarter))
    for d, got in zip((1, 2, 3), strips):
        grad_w_in = lax.dynamic_update_slice(
            grad_w_in, got.astype(F32), (0, ((z_here - d) % 4) * quarter)
        )

    fc6_part = stacked[:, :wide].reshape(-1, 2 * PAIRS, channels)[:, :BINS]
    fc6_out = jnp.transpose(fc6_part.astype(F32), (2, 1, 0))
    fc7_out = jnp.transpose(stacked[:, wide : wide + units].astype(F32))
    row = jnp.arange(2 * channels)
    block_of, inside = row // 4, row % 4
    from_y = (y_here - block_of // 8) % 4
    from_core = (core + (block_of // 4) % 2) % 2
    from_z = (z_here - block_of) % 4
    target = ((from_y * 2 + from_core) * 4 + from_z) * 4 + inside
    ordered = (row[:, None] == target[None, :]).astype(BF)
    fpn_out = mm(ordered, over_y.reshape(2 * channels, width))
    fpn_out = jnp.transpose(fpn_out.reshape(2, channels, width), (0, 2, 1))
    return (grad_w_in[None], grad_w_out[None], fpn_out, fc6_out, fc7_out)


def solution(mesh):
    return jax.shard_map(
        per_device,
        mesh=mesh,
        in_specs=(
            P(("dp", "head"), None, None),
            P("section", None, None),
            P("section", None, None),
            P(None, None, "section"),
            P("section", None, None),
            P(),
            P(None, ("dp", "head"), None),
            P(None, None, None, ("dp", "head"), None),
            P(("dp", "head"), None, None),
            P(("dp", "head"), None, None, None),
        ),
        out_specs=(
            P("section", ("dp", "head"), None),
            P("section", ("dp", "head"), None),
            P(None, None, "section"),
            P("section", None, ("dp", "head")),
            P(None, ("dp", "head")),
        ),
        check_vma=False,
    )
```

```python
import functools
import math

import jax
import jax.numpy as jnp
import numpy as np
from jax import lax
from jax.experimental import pallas as pl
from jax.experimental.pallas import tpu as pltpu
from jax.sharding import PartitionSpec as P

GRID = 12
HALF = GRID // 2
SPAN = 4
POOLED = 7
BINS = POOLED * POOLED
PAIRS = (BINS + 1) // 2
CELLS = 256

EPS = 1e-06
GELU_C = math.sqrt(2.0 / math.pi)
BF = jnp.bfloat16
F32 = jnp.float32
STEP = 512
AHEAD = 2

NN = (((1,), (0,)), ((), ()))
NT = (((1,), (1,)), ((), ()))
TN = (((0,), (0,)), ((), ()))


def mm(left, right, dims=NN):
    return lax.dot_general(left, right, dims, preferred_element_type=F32)


def gelu_parts(values):
    inner_arg = GELU_C * (values + 0.044715 * values * values * values)
    tangent = jnp.tanh(inner_arg)
    result = 0.5 * values * (1.0 + tangent)
    slope = 0.5 * (1.0 + tangent) + 0.5 * values * (1.0 - tangent * tangent) * GELU_C * (
        1.0 + 3.0 * 0.044715 * values * values
    )
    return (result, slope)


def norm_parts(tokens):
    floats = tokens.astype(F32)
    centred = floats - jnp.mean(floats, axis=-1, keepdims=True)
    scale_inv = lax.rsqrt(jnp.mean(centred * centred, axis=-1, keepdims=True) + EPS)
    return (centred * scale_inv, scale_inv)


class Staged:
    def __init__(self, source, buffer, sems, chunk_axis):
        self.buffer = buffer
        self.shape = buffer.shape
        self.axis = chunk_axis
        self.copies = []
        self.waited = set()
        if chunk_axis is None:
            self.copies.append(pltpu.make_async_copy(source, buffer, sems.at[0]))
        else:
            for j in range(self.shape[chunk_axis] // STEP):
                at = self.part(j)
                self.copies.append(
                    pltpu.make_async_copy(source.at[at], buffer.at[at], sems.at[j])
                )

    def part(self, j):
        span = pl.ds(j * STEP, STEP)
        return (span, slice(None)) if self.axis == 0 else (slice(None), span)

    def start(self, j):
        if j < len(self.copies):
            self.copies[j].start()

    def wait(self, j):
        if j not in self.waited:
            self.waited.add(j)
            self.copies[j].wait()

    def chunk(self, j):
        self.wait(j)
        self.start(j + AHEAD)
        return self.buffer[self.part(j)]

    def __getitem__(self, index):
        self.wait(0)
        return self.buffer[index]

    def finish(self):
        for j in range(len(self.copies)):
            self.wait(j)


def call(body, outs, args, name, scratch=(), scalars=0, chunks=None, flops=0, nbytes=0, vmem=18):
    chunks = chunks or {}
    count = len(args) - scalars
    axes = [chunks.get(i + scalars) for i in range(count)]
    sizes = [
        1 if axis is None else arg.shape[axis] // STEP for axis, arg in zip(axes, args[scalars:])
    ]

    def kernel(*refs):
        given, sources = refs[:scalars], refs[scalars : len(args)]
        results = refs[len(args) : len(args) + len(outs)]
        rest = refs[len(args) + len(outs) :]
        buffers, sems, extra = rest[:count], rest[count : 2 * count], rest[2 * count :]
        staged = [Staged(*parts) for parts in zip(sources, buffers, sems, axes)]
        for j in range(AHEAD):
            for item in staged:
                item.start(j)
        body(*given, *staged, *results, *extra)
        for item in staged:
            item.finish()

    return pl.pallas_call(
        kernel,
        out_shape=[jax.ShapeDtypeStruct(s, d) for s, d in outs],
        in_specs=[pl.BlockSpec(memory_space=pltpu.SMEM)] * scalars
        + [pl.BlockSpec(memory_space=pl.ANY)] * count,
        out_specs=[pl.BlockSpec(memory_space=pltpu.VMEM) for _ in outs],
        scratch_shapes=[pltpu.VMEM(arg.shape, arg.dtype) for arg in args[scalars:]]
        + [pltpu.SemaphoreType.DMA((size,)) for size in sizes]
        + list(scratch),
        compiler_params=pltpu.CompilerParams(vmem_limit_bytes=vmem * 1024 * 1024),
        cost_estimate=pl.CostEstimate(flops=flops, bytes_accessed=nbytes, transcendentals=0),
        name=name,
    )(*args)


def direct(
    body,
    outs,
    args,
    name,
    scratch=(),
    scalars=0,
    flops=0,
    nbytes=0,
    vmem=18,
    out_space=pltpu.VMEM,
):
    return pl.pallas_call(
        body,
        out_shape=[jax.ShapeDtypeStruct(s, d) for s, d in outs],
        in_specs=[pl.BlockSpec(memory_space=pltpu.SMEM)] * scalars
        + [pl.BlockSpec(memory_space=pltpu.VMEM)] * (len(args) - scalars),
        out_specs=[pl.BlockSpec(memory_space=out_space) for _ in outs],
        scratch_shapes=list(scratch),
        compiler_params=pltpu.CompilerParams(vmem_limit_bytes=vmem * 1024 * 1024),
        cost_estimate=pl.CostEstimate(flops=flops, bytes_accessed=nbytes, transcendentals=0),
        name=name,
    )(*args)


def in_hbm(array):
    return pltpu.with_memory_space_constraint(array, pltpu.HBM)


def ring(axis, shift):
    size = lax.axis_size(axis)
    return [(i, (i + shift) % size) for i in range(size)]


def shifted(value, axis, shift):
    return lax.ppermute(value, axis, ring(axis, shift))


def shifted_y(value, shift):
    return shifted(value, "dp", 2 * shift)


def core_swapped(value):
    return lax.ppermute(value, "dp", [(i, i ^ 1) for i in range(lax.axis_size("dp"))])


def gelu_quick(values):
    square = values * values
    half = 0.5 + 0.5 * jnp.tanh(values * (GELU_C + (GELU_C * 0.044715) * square))
    return half, square


def forward_body(tick, sec_ref, *refs):
    if tick == 0:
        old_ref, w1_ref, w2_ref, *outs = refs
        tokens = old_ref[...]
    else:
        old_ref, new_ref, w1_ref, w2_ref, *outs = refs
        tokens = jnp.where(sec_ref[0] == tick, new_ref[...], old_ref[...])
    result_ref = outs[0]
    if tick > 0:
        outs[1][...] = tokens
    normed = norm_parts(tokens)[0].astype(BF)
    if tick == 3:
        outs[2][...] = normed
    total = tokens.astype(F32)
    for j in range(w1_ref.shape[1] // STEP):
        lo = j * STEP
        values = mm(normed, w1_ref.chunk(j))
        half, square = gelu_quick(values)
        activ = (values * half).astype(BF)
        if tick == 3:
            outs[3][:, lo : lo + STEP] = activ
            outs[4][:, lo : lo + STEP] = half + (values * (2.0 * half) * (1.0 - half)) * (
                GELU_C + (3.0 * 0.044715 * GELU_C) * square
            )
        total = total + mm(activ, w2_ref.chunk(j))
    result_ref[...] = total.astype(BF)


def backward_body(tick, sec_ref, *refs):
    if tick == 0:
        old_ref, slope_ref, tokens_ref, w1_ref, w2_ref, *outs = refs
        grad_out = old_ref[...]
    else:
        old_ref, new_ref, slope_ref, tokens_ref, w1_ref, w2_ref, *outs = refs
        grad_out = jnp.where(sec_ref[0] == 3 - tick, new_ref[...], old_ref[...])
        outs[1][...] = grad_out
    total = jnp.zeros(grad_out.shape, F32)
    for j in range(w1_ref.shape[1] // STEP):
        grad_act = mm(grad_out, w2_ref.chunk(j), NT)
        grad_pre = (grad_act * slope_ref.chunk(j)).astype(BF)
        total = total + mm(grad_pre, w1_ref.chunk(j), NT)
    normed, scale_inv = norm_parts(tokens_ref[...])
    grad_tok = scale_inv * (
        total
        - jnp.mean(total, axis=-1, keepdims=True)
        - normed * jnp.mean(total * normed, axis=-1, keepdims=True)
    )
    outs[0][...] = (grad_out.astype(F32) + grad_tok).astype(BF)


def last_backward_body(grad_ref, slope_ref, w2_ref, out_ref):
    grad_out = grad_ref[...]
    for j in range(w2_ref.shape[0] // STEP):
        grad_act = mm(grad_out, w2_ref.chunk(j), NT)
        out_ref[:, j * STEP : (j + 1) * STEP] = (grad_act * slope_ref.chunk(j)).astype(BF)


def pyramid_body(top_ref, weight_ref, avg_ref, place_ref, levels_ref, pooled_ref):
    top = top_ref[...]
    pooled = mm(avg_ref[...], top).astype(BF)
    pooled_ref[...] = pooled
    weights = weight_ref[...]
    from_top = mm(weights, top, NT)
    from_pooled = mm(weights, pooled, NT)
    half = weights.shape[0] // 8
    for s in range(4):
        base = 2 * half * s
        one = from_pooled[base + half : base + 2 * half]
        zero = from_top[base : base + half] + one
        levels_ref[s] = (
            mm(zero.astype(BF), place_ref[0]) + mm(one.astype(BF), place_ref[1])
        ).astype(BF)


def top_grad_body(z0_ref, z1_ref, z2_ref, z3_ref, weight_ref, grad_ref, rows_ref):
    rows = jnp.concatenate([z0_ref[...], z1_ref[...], z2_ref[...], z3_ref[...]], axis=0)
    rows_ref[...] = rows
    grad_ref[...] = mm(rows, weight_ref[...], TN).astype(BF)


def crops_body(
    sec_ref, levels_ref, r0_ref, r1_ref, r2_ref, rows_ref, cols_ref, fc6_ref, part_ref, crops_ref
):
    is_last = sec_ref[0] == 3
    arrived = r0_ref[...] + r1_ref[...] + r2_ref[...]
    own = jnp.where(is_last, levels_ref[3], arrived)
    blank = jnp.zeros_like(own)
    both = jnp.concatenate(
        [jnp.concatenate([own, blank], axis=1), jnp.concatenate([blank, own], axis=1)], axis=0
    )

    def weights(b):
        if b >= BINS:
            return jnp.zeros((rows_ref.shape[1], CELLS), BF)
        return (rows_ref[b // POOLED] * cols_ref[b % POOLED]).astype(BF)

    for p in range(PAIRS):
        pair = jnp.concatenate([weights(2 * p), weights(2 * p + 1)], axis=1)
        crops_ref[:, 128 * p : 128 * (p + 1)] = mm(pair, both, NT).astype(BF)
    depth = fc6_ref.shape[0]
    whole = depth // 128 * 128
    part = mm(crops_ref[:, :whole], fc6_ref[:whole])
    part = part + mm(crops_ref[:, whole:depth], fc6_ref[whole:])
    part_ref[...] = part.astype(BF)


def head_body(
    sec_ref,
    p0_ref,
    p1_ref,
    p2_ref,
    p3_ref,
    cot_ref,
    fc7_ref,
    fc6_ref,
    rows_ref,
    cols_ref,
    spread_ref,
    first_ref,
    second_ref,
    grad_ref,
    maps_ref,
    parts_ref,
    back_ref,
):
    sec = sec_ref[0]
    for d, ref in enumerate((p0_ref, p1_ref, p2_ref, p3_ref)):
        parts_ref[lax.rem(sec + 4 - d, 4)] = ref[...].astype(F32)
    first_pre = parts_ref[0] + parts_ref[1] + parts_ref[2] + parts_ref[3]
    first_act, first_slope = gelu_parts(first_pre)
    first_b = first_act.astype(BF)
    first_ref[...] = first_b
    second_pre = mm(first_b, fc7_ref[...])
    second_slope = gelu_parts(second_pre)[1]
    grad_second = (cot_ref[...].astype(F32) * second_slope).astype(BF)
    second_ref[...] = grad_second
    grad_first = (mm(grad_second, fc7_ref[...], NT) * first_slope).astype(BF)
    grad_ref[...] = grad_first
    depth = fc6_ref.shape[0]
    back_ref[:depth] = mm(fc6_ref[...], grad_first, NT).astype(BF)
    back_ref[depth:] = jnp.zeros((back_ref.shape[0] - depth, back_ref.shape[1]), BF)
    channels = back_ref.shape[0] // (2 * PAIRS)

    def weights(b):
        if b >= BINS:
            return jnp.zeros((rows_ref.shape[1], CELLS), BF)
        return (rows_ref[b // POOLED] * cols_ref[b % POOLED]).astype(BF)

    total = jnp.zeros((channels, CELLS), F32)
    for p in range(PAIRS):
        lo = 2 * p * channels
        left = jnp.concatenate(
            [back_ref[lo : lo + channels], back_ref[lo + channels : lo + 2 * channels]], axis=1
        )
        right = jnp.concatenate([weights(2 * p), weights(2 * p + 1)], axis=0)
        total = total + mm(left, right)
    total_b = total.astype(BF)
    maps_ref[:channels] = mm(total_b, spread_ref[0]).astype(BF)
    maps_ref[channels:] = mm(total_b, spread_ref[1]).astype(BF)


def head_grads_body(
    grad_ref,
    crops_ref,
    second_ref,
    first_ref,
    maps_ref,
    order_ref,
    top_ref,
    pooled_ref,
    out_ref,
    held_ref,
    sems,
):
    wide = crops_ref.shape[1]
    units = first_ref.shape[1]
    ordered = mm(order_ref[...], maps_ref[...]).astype(BF)
    rows = ordered.shape[0] // 4
    copies = []
    for j in range(4):
        at = pl.ds(j * rows, rows)
        span = slice(j * rows, (j + 1) * rows)
        held_ref[at, :wide] = mm(grad_ref[:, span], crops_ref[...], TN).astype(BF)
        held_ref[at, wide : wide + units] = mm(second_ref[:, span], first_ref[...], TN).astype(BF)
        cells = top_ref if j < 2 else pooled_ref
        held_ref[at, wide + units :] = mm(ordered[span], cells[...]).astype(BF)
        copies.append(pltpu.make_async_copy(held_ref.at[at], out_ref.at[at], sems.at[j]))
        copies[-1].start()
    for copy in copies:
        copy.wait()


def first_grad_body(
    core_ref, a0_ref, a1_ref, a2_ref, a3_ref, g0_ref, g1_ref, g2_ref, g3_ref, mine_ref, other_ref
):
    is_zero = core_ref[0] == 0
    lefts = (a0_ref, a1_ref, a2_ref, a3_ref)
    rights = (g0_ref, g1_ref, g2_ref, g3_ref)
    total = mm(lefts[0][...], rights[0][...], TN)
    for d in range(1, 4):
        total = total + mm(lefts[d][...], rights[d][...], TN)
    rows = mine_ref.shape[1]
    for y in range(4):
        low = total[2 * y * rows : (2 * y + 1) * rows]
        high = total[(2 * y + 1) * rows : (2 * y + 2) * rows]
        mine_ref[y] = jnp.where(is_zero, low, high).astype(BF)
        other_ref[y] = jnp.where(is_zero, high, low).astype(BF)


def second_grad_body(
    core_ref, a0_ref, a1_ref, a2_ref, a3_ref, g0_ref, g1_ref, g2_ref, g3_ref, mine_ref, other_ref
):
    is_zero = core_ref[0] == 0
    lefts = (a0_ref, a1_ref, a2_ref, a3_ref)
    rights = (g0_ref, g1_ref, g2_ref, g3_ref)
    total = mm(lefts[0][...], rights[0][...], TN)
    for d in range(1, 4):
        total = total + mm(lefts[d][...], rights[d][...], TN)
    rows = mine_ref.shape[1]
    for z in range(4):
        low = total[z * rows : (z + 1) * rows]
        high = total[(z + 4) * rows : (z + 5) * rows]
        mine_ref[z] = jnp.where(is_zero, low, high).astype(BF)
        other_ref[z] = jnp.where(is_zero, high, low).astype(BF)


def pair_body(place_ref, mine_ref, got_ref, kept_ref, one_ref, two_ref, three_ref):
    place = place_ref[0]

    def total(d):
        at = lax.rem(place + d, 4)
        return mine_ref[at].astype(F32) + got_ref[at].astype(F32)

    kept_ref[...] = total(0)
    for d, ref in enumerate((one_ref, two_ref, three_ref)):
        ref[...] = total(d + 1).astype(BF)


def strips_body(
    place_ref, kept_ref, g1_ref, g2_ref, g3_ref, own_ref, one_ref, two_ref, three_ref
):
    total = kept_ref[...]
    for ref in (g1_ref, g2_ref, g3_ref):
        total = total + ref[...].astype(F32)
    rows = own_ref.shape[0]
    strips = [total[j * rows : (j + 1) * rows] for j in range(4)]
    for d, ref in enumerate((own_ref, one_ref, two_ref, three_ref)):
        at = lax.rem(place_ref[0] + d, 4)
        picked = strips[3]
        for j in range(3):
            picked = jnp.where(at == j, strips[j], picked)
        ref[...] = picked.astype(ref.dtype)


def join_body(place_ref, own_ref, g1_ref, g2_ref, g3_ref, out_ref):
    columns = own_ref.shape[1]
    for d, ref in enumerate((own_ref, g1_ref, g2_ref, g3_ref)):
        at = pl.multiple_of(lax.rem(place_ref[0] + 4 - d, 4) * columns, 128)
        out_ref[:, pl.ds(at, columns)] = ref[...].astype(F32)


def cell_tables():
    index = np.arange(CELLS)
    zero = index < GRID * GRID
    one = (index >= GRID * GRID) & (index < GRID * GRID + HALF * HALF)
    inner = index - GRID * GRID
    row = np.where(zero, index // GRID, np.where(one, inner // HALF, -9))
    col = np.where(zero, index % GRID, np.where(one, inner % HALF, -9))
    return zero, one, row.astype(np.int32), col.astype(np.int32)


def grid_constants():
    cells = np.arange(GRID * GRID)
    block = (cells // GRID // 2) * HALF + (cells % GRID) // 2
    average = 0.25 * (block[:, None] == block[None, :])
    place = np.zeros((2, GRID * GRID, CELLS))
    place[0, cells, cells] = 1.0
    for b in range(HALF * HALF):
        place[1, np.where(block == b)[0][0], GRID * GRID + b] = 1.0
    spread = np.zeros((2, CELLS, GRID * GRID))
    spread[0, cells, cells] = 1.0
    spread[1, GRID * GRID + block, cells] = 0.25
    return average, place, spread


def tables_body(boxes_ref, weights_ref, cells_ref, fwd_ref, bwd_ref, cols_ref):
    row, col = cells_ref[0:1], cells_ref[1:2]
    zero, one = cells_ref[2:3] > 0, cells_ref[3:4] > 0
    box_zero = boxes_ref[:, 0:1] == 0
    forward = (box_zero & zero) | (~box_zero & one)
    backward = forward | (box_zero & one)
    halved = box_zero & one
    at_rows, at_cols = [], []
    for u in range(SPAN):
        at_y = boxes_ref[:, 1:2] + u
        at_x = boxes_ref[:, 2:3] + u
        at_rows.append(row == jnp.where(halved, at_y // 2, at_y))
        at_cols.append(col == jnp.where(halved, at_x // 2, at_x))
    for i in range(POOLED):
        rows = jnp.zeros(fwd_ref.shape[1:], F32)
        cols = jnp.zeros(fwd_ref.shape[1:], F32)
        for u in range(SPAN):
            y_at, x_at = SPAN * i + u, SPAN * (POOLED + i) + u
            rows = rows + jnp.where(at_rows[u], weights_ref[:, y_at : y_at + 1], 0.0)
            cols = cols + jnp.where(at_cols[u], weights_ref[:, x_at : x_at + 1], 0.0)
        fwd_ref[i] = jnp.where(forward, rows, 0.0)
        bwd_ref[i] = jnp.where(backward, rows, 0.0)
        cols_ref[i] = cols


def sampling_tables(windows, bilinear):
    zero, one, row, col = cell_tables()
    boxes = windows.shape[2]
    cells = np.stack([row, col, zero.astype(np.int32), one.astype(np.int32)] + [row] * 4)
    weights = jnp.transpose(bilinear.reshape(2 * POOLED * SPAN, boxes))
    corners = jnp.transpose(windows.reshape(3, boxes))
    return direct(
        tables_body,
        [((POOLED, boxes, CELLS), F32)] * 3,
        (corners, weights, jnp.asarray(cells, jnp.int32)),
        "tables",
        nbytes=4 * 10**6,
    )


def slot_rows(owner_ids, arrived):
    boxes = owner_ids.shape[0]
    index = jnp.arange(boxes)
    same = (owner_ids[:, None] == owner_ids[None, :]) & (index[None, :] < index[:, None])
    rank = jnp.sum(same.astype(jnp.int32), axis=1)
    slots = arrived.shape[1]
    flat = arrived.reshape(-1, arrived.shape[2])
    pick = (owner_ids * slots + rank)[:, None] == jnp.arange(flat.shape[0])[None, :]
    return mm(pick.astype(BF), flat).astype(BF)


def per_device(
    images, w_in, w_out, fpn_weight, fc6_weight, fc7_weight, windows, bilinear, owners, cotangent
):
    section = lax.axis_index("section")
    dp = lax.axis_index("dp")
    z_here = lax.axis_index("head")
    y_here = dp // 2
    core = dp % 2
    w_first = in_hbm(w_in[0])
    w_second = in_hbm(w_out[0])
    width = images.shape[2]
    inner = w_first.shape[1]
    channels = fc6_weight.shape[0]
    units = fc6_weight.shape[2]
    sec_arr = section.astype(jnp.int32).reshape(1)
    core_arr = core.astype(jnp.int32).reshape(1)
    average, place, spread = grid_constants()
    average = jnp.asarray(average, BF)
    place = jnp.asarray(place, BF)
    spread = jnp.asarray(spread, BF)

    fpn_rows = jnp.transpose(fpn_weight, (0, 2, 1)).reshape(2 * channels, width)
    fpn_all = lax.all_gather(fpn_rows, "section", axis=0, tiled=True)
    fc6_rows = jnp.transpose(fc6_weight, (1, 0, 2)).reshape(BINS * channels, units)
    tokens = images[0]
    shape = tokens.shape
    wide_shape = (shape[0], inner)
    incoming = None
    for tick in range(4):
        outs = [(shape, BF)]
        if tick > 0:
            outs.append((shape, BF))
        if tick == 3:
            outs += [(shape, BF), (wide_shape, BF), (wide_shape, F32)]
        inputs = (tokens,) if tick == 0 else (tokens, incoming)
        results = call(
            functools.partial(forward_body, tick),
            outs,
            (sec_arr, *inputs, w_first, w_second),
            f"block_forward_{tick}",
            scalars=1,
            chunks={1 + len(inputs): 1, 2 + len(inputs): 0},
            vmem=34,
            flops=3 * 10**9,
            nbytes=18 * 10**6,
        )
        result = results[0]
        if tick > 0:
            tokens = results[1]
        if tick == 3:
            normed_b, activ_b, slope = results[2:]
            break
        if tick == 0:
            padded = jnp.pad(cotangent[0], ((0, 0), (0, 2), (0, 0)))
            padded, result = lax.optimization_barrier((padded, result))
            cot_arrived = lax.all_to_all(
                padded, ("dp", "head"), split_axis=0, concat_axis=0, tiled=True
            )
        incoming = lax.ppermute(result, "section", [(tick, tick + 1)])
        if tick == 0:
            windows, bilinear, result = lax.optimization_barrier((windows, bilinear, result))
            rows_fwd, rows_bwd, cols_all = sampling_tables(windows, bilinear)
            held = (incoming, rows_fwd, rows_bwd, cols_all)
            incoming, rows_fwd, rows_bwd, cols_all = lax.optimization_barrier(held)
        if tick == 1:
            owner_ids, result = lax.optimization_barrier((owners[0, :, 0], result))
            cot_rows = slot_rows(owner_ids, cot_arrived)
            incoming, cot_rows = lax.optimization_barrier((incoming, cot_rows))
    top = result

    levels, pooled = direct(
        pyramid_body,
        [((4, channels, CELLS), BF), (top.shape, BF)],
        (top, fpn_all, average, place),
        "pyramid",
        flops=10**9,
        nbytes=3 * 10**6,
    )
    sent = [lax.ppermute(levels[s], "section", [(3, s)]) for s in range(3)]
    boxes = windows.shape[2]
    part, crops = direct(
        crops_body,
        [((boxes, units), BF), ((boxes, 2 * PAIRS * channels), BF)],
        (sec_arr, levels, *sent, rows_fwd, cols_all, fc6_rows),
        "crops",
        scalars=1,
        flops=10**9,
        nbytes=6 * 10**6,
    )
    parts = [part] + [shifted(part, "section", d) for d in (1, 2, 3)]
    first_b, grad_second, grad_first, maps = direct(
        head_body,
        [((boxes, units), BF)] * 3 + [((2 * channels, GRID * GRID), BF)],
        (
            sec_arr,
            *parts,
            cot_rows,
            fc7_weight,
            fc6_rows,
            rows_bwd,
            cols_all,
            spread,
        ),
        "head",
        scratch=(
            pltpu.VMEM((4, boxes, units), F32),
            pltpu.VMEM((2 * PAIRS * channels, boxes), BF),
        ),
        scalars=1,
        flops=10**9,
        nbytes=6 * 10**6,
    )
    returned = [lax.ppermute(maps, "section", [(s, 3)]) for s in range(3)]
    grad_out, map_rows = direct(
        top_grad_body,
        [(top.shape, BF), ((8 * channels, GRID * GRID), BF)],
        (*returned, maps, fpn_all),
        "top_grad",
        flops=10**9,
        nbytes=3 * 10**6,
    )

    quarter = inner // 4

    def piece(array, index):
        return lax.dynamic_slice_in_dim(array, index * quarter, quarter, 1)

    act_pieces = [piece(activ_b, (y_here + d) % 4) for d in range(4)]

    incoming = None
    for tick in range(3):
        outs = [(shape, BF)]
        if tick > 0:
            outs.append((shape, BF))
        inputs = (grad_out,) if tick == 0 else (grad_out, incoming)
        results = call(
            functools.partial(backward_body, tick),
            outs,
            (sec_arr, *inputs, slope, tokens, w_first, w_second),
            f"block_backward_{tick}",
            scalars=1,
            chunks={1 + len(inputs): 1, 3 + len(inputs): 1, 4 + len(inputs): 0},
            vmem=34,
            flops=3 * 10**9,
            nbytes=18 * 10**6,
        )
        grad_in = results[0]
        if tick > 0:
            grad_out = results[1]
        if tick == 0:
            held = (grad_in, map_rows, normed_b)
            grad_in, map_rows, normed_b = lax.optimization_barrier(held)
            incoming = lax.ppermute(grad_in, "section", [(3, 2)])
            normed_parts = [normed_b] + [shifted(normed_b, "head", d) for d in (1, 2, 3)]
            order = np.zeros((8 * channels, 8 * channels))
            for r in range(8 * channels):
                order[r, ((r % 16) // 4) * 2 * channels + (r // 16) * 4 + r % 4] = 1.0
            stack_shape = (units, crops.shape[1] + units + width)
            (stacked,) = direct(
                head_grads_body,
                [(stack_shape, BF)],
                (
                    grad_first,
                    crops,
                    grad_second,
                    first_b,
                    map_rows,
                    jnp.asarray(order, BF),
                    top,
                    pooled,
                ),
                "head_grads",
                scratch=(pltpu.VMEM(stack_shape, BF), pltpu.SemaphoreType.DMA((4,))),
                flops=10**9,
                nbytes=8 * 10**6,
                vmem=24,
                out_space=pl.ANY,
            )
            incoming, stacked = lax.optimization_barrier((incoming, stacked))
            stacked = lax.psum_scatter(stacked, "dp", scatter_dimension=0, tiled=True)
        elif tick == 1:
            grad_in, act_pieces = lax.optimization_barrier((grad_in, act_pieces))
            incoming = lax.ppermute(grad_in, "section", [(2, 1)])
            act_parts = act_pieces[:1] + [shifted_y(act_pieces[d], d) for d in (1, 2, 3)]
            incoming, act_parts = lax.optimization_barrier((incoming, act_parts))
        else:
            incoming = lax.ppermute(grad_in, "section", [(1, 0)])
            incoming, normed_parts = lax.optimization_barrier((incoming, normed_parts))
    grad_out = jnp.where(section == 0, incoming, grad_out)

    out_parts = [grad_out] + [shifted_y(grad_out, d) for d in (1, 2, 3)]
    (grad_pre,) = call(
        last_backward_body,
        [(wide_shape, BF)],
        (grad_out, slope, w_second),
        "block_backward_3",
        chunks={1: 1, 2: 0},
        flops=2 * 10**9,
        nbytes=10 * 10**6,
    )
    grad_pre, stacked = lax.optimization_barrier((grad_pre, stacked))
    stacked = lax.psum_scatter(stacked, "head", scatter_dimension=0, tiled=True)
    pre_parts = [piece(grad_pre, z_here)] + [
        shifted(piece(grad_pre, (z_here + d) % 4), "head", d) for d in (1, 2, 3)
    ]
    pre_parts, out_parts = lax.optimization_barrier((pre_parts, out_parts))
    rows_in = width // 8
    rows_out = quarter // 8
    mine_first, other_first = call(
        first_grad_body,
        [((4, rows_in, quarter), BF)] * 2,
        (core_arr, *normed_parts, *pre_parts),
        "first_grad",
        vmem=24,
        scalars=1,
        flops=2 * 10**9,
        nbytes=5 * 10**6,
    )
    mine_second, other_second = call(
        second_grad_body,
        [((4, rows_out, width), BF)] * 2,
        (core_arr, *act_parts, *out_parts),
        "second_grad",
        vmem=24,
        scalars=1,
        flops=2 * 10**9,
        nbytes=5 * 10**6,
    )
    swapped_first = core_swapped(other_first)
    swapped_second = core_swapped(other_second)
    z_arr = z_here.astype(jnp.int32).reshape(1)
    y_arr = y_here.astype(jnp.int32).reshape(1)

    def pair_sums(place, mine, swapped, name):
        return direct(
            pair_body,
            [(mine.shape[1:], F32)] + [(mine.shape[1:], BF)] * 3,
            (place, mine, swapped),
            name,
            scalars=1,
            nbytes=5 * 10**6,
        )

    kept_first, *out_first = pair_sums(y_arr, mine_first, swapped_first, "pair_first")
    grad_w_out, *out_second = pair_sums(z_arr, mine_second, swapped_second, "pair_second")
    held = (out_first, out_second, stacked)
    out_first, out_second, stacked = lax.optimization_barrier(held)
    wide = crops.shape[1]
    fpn_part = stacked[:, wide + units :].reshape(4, 4, width)
    fpn_got = [lax.ppermute(fpn_part[s], "section", [(3, s)]) for s in range(3)]
    got_first = [shifted_y(out_first[d - 1], d) for d in (1, 2, 3)]
    got_second = [shifted(out_second[d - 1], "head", d) for d in (1, 2, 3)]
    own = jnp.where(section == 3, fpn_part[3], fpn_got[0] + fpn_got[1] + fpn_got[2])
    fpn_rows = lax.all_to_all(
        jnp.broadcast_to(own[None], (32,) + own.shape),
        ("dp", "head"),
        split_axis=0,
        concat_axis=0,
        tiled=True,
    )
    last_rows = rows_in // 4
    kept_strip, *out_strips = direct(
        strips_body,
        [((last_rows, quarter), F32)] + [((last_rows, quarter), BF)] * 3,
        (z_arr, kept_first, *got_first),
        "strips",
        scalars=1,
        nbytes=3 * 10**6,
    )
    strips = [shifted(out_strips[d - 1], "head", d) for d in (1, 2, 3)]
    for got in got_second:
        grad_w_out = grad_w_out + got.astype(F32)
    (grad_w_in,) = direct(
        join_body,
        [((last_rows, inner), F32)],
        (z_arr, kept_strip, *strips),
        "join",
        scalars=1,
        nbytes=10**6,
    )

    fc6_part = stacked[:, :wide].reshape(-1, 2 * PAIRS, channels)[:, :BINS]
    fc6_out = jnp.transpose(fc6_part.astype(F32), (2, 1, 0))
    fc7_out = jnp.transpose(stacked[:, wide : wide + units].astype(F32))
    fpn_out = fpn_rows.astype(F32)
    fpn_out = jnp.transpose(fpn_out.reshape(2, channels, width), (0, 2, 1))
    return (grad_w_in[None], grad_w_out[None], fpn_out, fc6_out, fc7_out)


def solution(mesh):
    return jax.shard_map(
        per_device,
        mesh=mesh,
        in_specs=(
            P(("dp", "head"), None, None),
            P("section", None, None),
            P("section", None, None),
            P(None, None, "section"),
            P("section", None, None),
            P(),
            P(None, ("dp", "head"), None),
            P(None, None, None, ("dp", "head"), None),
            P(("dp", "head"), None, None),
            P(("dp", "head"), None, None, None),
        ),
        out_specs=(
            P("section", ("dp", "head"), None),
            P("section", ("dp", "head"), None),
            P(None, None, "section"),
            P("section", None, ("dp", "head")),
            P(None, ("dp", "head")),
        ),
        check_vma=False,
    )
```

```python
import functools
import math

import jax
import jax.numpy as jnp
import numpy as np
from jax import lax
from jax.experimental import pallas as pl
from jax.experimental.pallas import tpu as pltpu
from jax.sharding import PartitionSpec as P

GRID = 12
HALF = GRID // 2
SPAN = 4
POOLED = 7
BINS = POOLED * POOLED
PAIRS = (BINS + 1) // 2
CELLS = 256

EPS = 1e-06
GELU_C = math.sqrt(2.0 / math.pi)
BF = jnp.bfloat16
F32 = jnp.float32
STEP = 512
AHEAD = 3

NN = (((1,), (0,)), ((), ()))
NT = (((1,), (1,)), ((), ()))
TN = (((0,), (0,)), ((), ()))


def mm(left, right, dims=NN):
    return lax.dot_general(left, right, dims, preferred_element_type=F32)


def gelu_parts(values):
    inner_arg = GELU_C * (values + 0.044715 * values * values * values)
    tangent = jnp.tanh(inner_arg)
    result = 0.5 * values * (1.0 + tangent)
    slope = 0.5 * (1.0 + tangent) + 0.5 * values * (1.0 - tangent * tangent) * GELU_C * (
        1.0 + 3.0 * 0.044715 * values * values
    )
    return (result, slope)


def norm_parts(tokens):
    floats = tokens.astype(F32)
    centred = floats - jnp.mean(floats, axis=-1, keepdims=True)
    scale_inv = lax.rsqrt(jnp.mean(centred * centred, axis=-1, keepdims=True) + EPS)
    return (centred * scale_inv, scale_inv)


class Staged:
    def __init__(self, source, buffer, sems, chunk_axis):
        self.buffer = buffer
        self.shape = buffer.shape
        self.axis = chunk_axis
        self.copies = []
        self.waited = set()
        if chunk_axis is None:
            self.copies.append(pltpu.make_async_copy(source, buffer, sems.at[0]))
        else:
            for j in range(self.shape[chunk_axis] // STEP):
                at = self.part(j)
                self.copies.append(
                    pltpu.make_async_copy(source.at[at], buffer.at[at], sems.at[j])
                )

    def part(self, j):
        span = pl.ds(j * STEP, STEP)
        return (span, slice(None)) if self.axis == 0 else (slice(None), span)

    def start(self, j):
        if j < len(self.copies):
            self.copies[j].start()

    def wait(self, j):
        if j not in self.waited:
            self.waited.add(j)
            self.copies[j].wait()

    def chunk(self, j):
        self.wait(j)
        self.start(j + AHEAD)
        return self.buffer[self.part(j)]

    def __getitem__(self, index):
        self.wait(0)
        return self.buffer[index]

    def finish(self):
        for j in range(len(self.copies)):
            self.wait(j)


def call(body, outs, args, name, scratch=(), scalars=0, chunks=None, flops=0, nbytes=0, vmem=18):
    chunks = chunks or {}
    count = len(args) - scalars
    axes = [chunks.get(i + scalars) for i in range(count)]
    sizes = [
        1 if axis is None else arg.shape[axis] // STEP for axis, arg in zip(axes, args[scalars:])
    ]

    def kernel(*refs):
        given, sources = refs[:scalars], refs[scalars : len(args)]
        results = refs[len(args) : len(args) + len(outs)]
        rest = refs[len(args) + len(outs) :]
        buffers, sems, extra = rest[:count], rest[count : 2 * count], rest[2 * count :]
        staged = [Staged(*parts) for parts in zip(sources, buffers, sems, axes)]
        for j in range(AHEAD):
            for item in staged:
                item.start(j)
        body(*given, *staged, *results, *extra)
        for item in staged:
            item.finish()

    return pl.pallas_call(
        kernel,
        out_shape=[jax.ShapeDtypeStruct(s, d) for s, d in outs],
        in_specs=[pl.BlockSpec(memory_space=pltpu.SMEM)] * scalars
        + [pl.BlockSpec(memory_space=pl.ANY)] * count,
        out_specs=[pl.BlockSpec(memory_space=pltpu.VMEM) for _ in outs],
        scratch_shapes=[pltpu.VMEM(arg.shape, arg.dtype) for arg in args[scalars:]]
        + [pltpu.SemaphoreType.DMA((size,)) for size in sizes]
        + list(scratch),
        compiler_params=pltpu.CompilerParams(vmem_limit_bytes=vmem * 1024 * 1024),
        cost_estimate=pl.CostEstimate(flops=flops, bytes_accessed=nbytes, transcendentals=0),
        name=name,
    )(*args)


def direct(
    body,
    outs,
    args,
    name,
    scratch=(),
    scalars=0,
    flops=0,
    nbytes=0,
    vmem=18,
    out_space=pltpu.VMEM,
):
    return pl.pallas_call(
        body,
        out_shape=[jax.ShapeDtypeStruct(s, d) for s, d in outs],
        in_specs=[pl.BlockSpec(memory_space=pltpu.SMEM)] * scalars
        + [pl.BlockSpec(memory_space=pltpu.VMEM)] * (len(args) - scalars),
        out_specs=[pl.BlockSpec(memory_space=out_space) for _ in outs],
        scratch_shapes=list(scratch),
        compiler_params=pltpu.CompilerParams(vmem_limit_bytes=vmem * 1024 * 1024),
        cost_estimate=pl.CostEstimate(flops=flops, bytes_accessed=nbytes, transcendentals=0),
        name=name,
    )(*args)


def in_hbm(array):
    return pltpu.with_memory_space_constraint(array, pltpu.HBM)


def ring(axis, shift):
    size = lax.axis_size(axis)
    return [(i, (i + shift) % size) for i in range(size)]


def shifted(value, axis, shift):
    return lax.ppermute(value, axis, ring(axis, shift))


def shifted_y(value, shift):
    return shifted(value, "dp", 2 * shift)


def core_swapped(value):
    return lax.ppermute(value, "dp", [(i, i ^ 1) for i in range(lax.axis_size("dp"))])


def gelu_quick(values):
    square = values * values
    half = 0.5 + 0.5 * jnp.tanh(values * (GELU_C + (GELU_C * 0.044715) * square))
    return half, square


def forward_body(tick, place_ref, *refs):
    if tick == 3:
        *refs, held_ref = refs
    if tick == 0:
        old_ref, w1_ref, w2_ref, *outs = refs
        tokens = old_ref[...]
    else:
        old_ref, new_ref, w1_ref, w2_ref, *outs = refs
        tokens = jnp.where(place_ref[0] == tick, new_ref[...], old_ref[...])
    result_ref = outs[0]
    if tick > 0:
        outs[1][...] = tokens
    normed = norm_parts(tokens)[0].astype(BF)
    if tick == 3:
        outs[2][...] = normed
    total = tokens.astype(F32)
    count = w1_ref.shape[1] // STEP
    values = mm(normed, w1_ref.chunk(0))
    for j in range(count):
        later = mm(normed, w1_ref.chunk(j + 1)) if j + 1 < count else None
        half, square = gelu_quick(values)
        activ = (values * half).astype(BF)
        if tick == 3:
            span = slice(j * STEP, (j + 1) * STEP)
            held_ref[:, span] = activ
            outs[3][:, span] = half + (values * (2.0 * half) * (1.0 - half)) * (
                GELU_C + (3.0 * 0.044715 * GELU_C) * square
            )
        total = total + mm(activ, w2_ref.chunk(j))
        values = later
    result_ref[...] = total.astype(BF)
    if tick == 3:
        put_pieces(place_ref[1], held_ref, outs[4:])


def put_pieces(place, held_ref, outs):
    columns = outs[0].shape[1]
    for d, ref in enumerate(outs):
        at = pl.multiple_of(lax.rem(place + d, 4) * columns, 128)
        ref[...] = held_ref[:, pl.ds(at, columns)]


def backward_body(tick, place_ref, *refs):
    if tick == 0:
        old_ref, slope_ref, tokens_ref, w1_ref, w2_ref, *outs = refs
        grad_out = old_ref[...]
    else:
        old_ref, new_ref, slope_ref, tokens_ref, w1_ref, w2_ref, *outs = refs
        grad_out = jnp.where(place_ref[0] == 3 - tick, new_ref[...], old_ref[...])
        outs[1][...] = grad_out
    total = jnp.zeros(grad_out.shape, F32)
    count = w1_ref.shape[1] // STEP
    grad_act = mm(grad_out, w2_ref.chunk(0), NT)
    for j in range(count):
        later = mm(grad_out, w2_ref.chunk(j + 1), NT) if j + 1 < count else None
        grad_pre = (grad_act * slope_ref.chunk(j)).astype(BF)
        total = total + mm(grad_pre, w1_ref.chunk(j), NT)
        grad_act = later
    normed, scale_inv = norm_parts(tokens_ref[...])
    grad_tok = scale_inv * (
        total
        - jnp.mean(total, axis=-1, keepdims=True)
        - normed * jnp.mean(total * normed, axis=-1, keepdims=True)
    )
    outs[0][...] = (grad_out.astype(F32) + grad_tok).astype(BF)


def last_backward_body(place_ref, grad_ref, slope_ref, w2_ref, *refs):
    *outs, held_ref = refs
    grad_out = grad_ref[...]
    count = w2_ref.shape[0] // STEP
    grad_act = mm(grad_out, w2_ref.chunk(0), NT)
    for j in range(count):
        later = mm(grad_out, w2_ref.chunk(j + 1), NT) if j + 1 < count else None
        held_ref[:, j * STEP : (j + 1) * STEP] = (grad_act * slope_ref.chunk(j)).astype(BF)
        grad_act = later
    put_pieces(place_ref[2], held_ref, outs)


def pick_body(place_ref, old_ref, new_ref, out_ref):
    out_ref[...] = jnp.where(place_ref[0] == 0, new_ref[...], old_ref[...])


def pyramid_body(top_ref, weight_ref, avg_ref, place_ref, levels_ref, pooled_ref):
    top = top_ref[...]
    pooled = mm(avg_ref[...], top).astype(BF)
    pooled_ref[...] = pooled
    weights = weight_ref[...]
    from_top = mm(weights, top, NT)
    from_pooled = mm(weights, pooled, NT)
    half = weights.shape[0] // 8
    for s in range(4):
        base = 2 * half * s
        one = from_pooled[base + half : base + 2 * half]
        zero = from_top[base : base + half] + one
        levels_ref[s] = (
            mm(zero.astype(BF), place_ref[0]) + mm(one.astype(BF), place_ref[1])
        ).astype(BF)


def top_grad_body(z0_ref, z1_ref, z2_ref, z3_ref, weight_ref, grad_ref, rows_ref):
    rows = jnp.concatenate([z0_ref[...], z1_ref[...], z2_ref[...], z3_ref[...]], axis=0)
    rows_ref[...] = rows
    grad_ref[...] = mm(rows, weight_ref[...], TN).astype(BF)


def crops_body(
    sec_ref, levels_ref, r0_ref, r1_ref, r2_ref, rows_ref, cols_ref, fc6_ref, part_ref, crops_ref
):
    is_last = sec_ref[0] == 3
    arrived = r0_ref[...] + r1_ref[...] + r2_ref[...]
    own = jnp.where(is_last, levels_ref[3], arrived)
    blank = jnp.zeros_like(own)
    both = jnp.concatenate(
        [jnp.concatenate([own, blank], axis=1), jnp.concatenate([blank, own], axis=1)], axis=0
    )

    def weights(b):
        if b >= BINS:
            return jnp.zeros((rows_ref.shape[1], CELLS), BF)
        return (rows_ref[b // POOLED] * cols_ref[b % POOLED]).astype(BF)

    for p in range(PAIRS):
        pair = jnp.concatenate([weights(2 * p), weights(2 * p + 1)], axis=1)
        crops_ref[:, 128 * p : 128 * (p + 1)] = mm(pair, both, NT).astype(BF)
    depth = fc6_ref.shape[0]
    whole = depth // 128 * 128
    part = mm(crops_ref[:, :whole], fc6_ref[:whole])
    part = part + mm(crops_ref[:, whole:depth], fc6_ref[whole:])
    part_ref[...] = part.astype(BF)


def head_body(
    sec_ref,
    p0_ref,
    p1_ref,
    p2_ref,
    p3_ref,
    cot_ref,
    fc7_ref,
    fc6_ref,
    rows_ref,
    cols_ref,
    spread_ref,
    first_ref,
    second_ref,
    grad_ref,
    maps_ref,
    parts_ref,
    back_ref,
):
    sec = sec_ref[0]
    for d, ref in enumerate((p0_ref, p1_ref, p2_ref, p3_ref)):
        parts_ref[lax.rem(sec + 4 - d, 4)] = ref[...].astype(F32)
    first_pre = parts_ref[0] + parts_ref[1] + parts_ref[2] + parts_ref[3]
    first_act, first_slope = gelu_parts(first_pre)
    first_b = first_act.astype(BF)
    first_ref[...] = first_b
    second_pre = mm(first_b, fc7_ref[...])
    second_slope = gelu_parts(second_pre)[1]
    grad_second = (cot_ref[...].astype(F32) * second_slope).astype(BF)
    second_ref[...] = grad_second
    grad_first = (mm(grad_second, fc7_ref[...], NT) * first_slope).astype(BF)
    grad_ref[...] = grad_first
    depth = fc6_ref.shape[0]
    back_ref[:depth] = mm(fc6_ref[...], grad_first, NT).astype(BF)
    back_ref[depth:] = jnp.zeros((back_ref.shape[0] - depth, back_ref.shape[1]), BF)
    channels = back_ref.shape[0] // (2 * PAIRS)

    def weights(b):
        if b >= BINS:
            return jnp.zeros((rows_ref.shape[1], CELLS), BF)
        return (rows_ref[b // POOLED] * cols_ref[b % POOLED]).astype(BF)

    total = jnp.zeros((channels, CELLS), F32)
    for p in range(PAIRS):
        lo = 2 * p * channels
        left = jnp.concatenate(
            [back_ref[lo : lo + channels], back_ref[lo + channels : lo + 2 * channels]], axis=1
        )
        right = jnp.concatenate([weights(2 * p), weights(2 * p + 1)], axis=0)
        total = total + mm(left, right)
    total_b = total.astype(BF)
    maps_ref[:channels] = mm(total_b, spread_ref[0]).astype(BF)
    maps_ref[channels:] = mm(total_b, spread_ref[1]).astype(BF)


def head_grads_body(grad_ref, crops_ref, second_ref, first_ref, out_ref, held_ref, sems):
    wide = crops_ref.shape[1]
    rows = out_ref.shape[0] // 4
    copies = []
    for j in range(4):
        at = pl.ds(j * rows, rows)
        span = slice(j * rows, (j + 1) * rows)
        held_ref[at, :wide] = mm(grad_ref[:, span], crops_ref[...], TN).astype(BF)
        held_ref[at, wide:] = mm(second_ref[:, span], first_ref[...], TN).astype(BF)
        copies.append(pltpu.make_async_copy(held_ref.at[at], out_ref.at[at], sems.at[j]))
        copies[-1].start()
    for copy in copies:
        copy.wait()


def map_grads_body(maps_ref, order_ref, top_ref, pooled_ref, out_ref):
    ordered = mm(order_ref[...], maps_ref[...]).astype(BF)
    half = ordered.shape[0] // 2
    out_ref[:half] = mm(ordered[:half], top_ref[...]).astype(BF)
    out_ref[half:] = mm(ordered[half:], pooled_ref[...]).astype(BF)


def first_grad_body(
    core_ref, a0_ref, a1_ref, a2_ref, a3_ref, g0_ref, g1_ref, g2_ref, g3_ref, mine_ref, other_ref
):
    is_zero = core_ref[3] == 0
    lefts = (a0_ref, a1_ref, a2_ref, a3_ref)
    rights = (g0_ref, g1_ref, g2_ref, g3_ref)
    total = mm(lefts[0][...], rights[0][...], TN)
    for d in range(1, 4):
        total = total + mm(lefts[d][...], rights[d][...], TN)
    rows = mine_ref.shape[1]
    for y in range(4):
        low = total[2 * y * rows : (2 * y + 1) * rows]
        high = total[(2 * y + 1) * rows : (2 * y + 2) * rows]
        mine_ref[y] = jnp.where(is_zero, low, high).astype(BF)
        other_ref[y] = jnp.where(is_zero, high, low).astype(BF)


def second_grad_body(
    core_ref, a0_ref, a1_ref, a2_ref, a3_ref, g0_ref, g1_ref, g2_ref, g3_ref, mine_ref, other_ref
):
    is_zero = core_ref[3] == 0
    lefts = (a0_ref, a1_ref, a2_ref, a3_ref)
    rights = (g0_ref, g1_ref, g2_ref, g3_ref)
    total = mm(lefts[0][...], rights[0][...], TN)
    for d in range(1, 4):
        total = total + mm(lefts[d][...], rights[d][...], TN)
    rows = mine_ref.shape[1]
    for z in range(4):
        low = total[z * rows : (z + 1) * rows]
        high = total[(z + 4) * rows : (z + 5) * rows]
        mine_ref[z] = jnp.where(is_zero, low, high).astype(BF)
        other_ref[z] = jnp.where(is_zero, high, low).astype(BF)


def pair_body(which, place_ref, mine_ref, got_ref, kept_ref, one_ref, two_ref, three_ref):
    place = place_ref[which]

    def total(d):
        at = lax.rem(place + d, 4)
        return mine_ref[at].astype(F32) + got_ref[at].astype(F32)

    kept_ref[...] = total(0)
    for d, ref in enumerate((one_ref, two_ref, three_ref)):
        ref[...] = total(d + 1).astype(BF)


def strips_body(
    place_ref, kept_ref, g1_ref, g2_ref, g3_ref, own_ref, one_ref, two_ref, three_ref
):
    total = kept_ref[...]
    for ref in (g1_ref, g2_ref, g3_ref):
        total = total + ref[...].astype(F32)
    rows = own_ref.shape[0]
    strips = [total[j * rows : (j + 1) * rows] for j in range(4)]
    for d, ref in enumerate((own_ref, one_ref, two_ref, three_ref)):
        at = lax.rem(place_ref[2] + d, 4)
        picked = strips[3]
        for j in range(3):
            picked = jnp.where(at == j, strips[j], picked)
        ref[...] = picked.astype(ref.dtype)


def join_body(place_ref, own_ref, g1_ref, g2_ref, g3_ref, out_ref):
    columns = own_ref.shape[1]
    for d, ref in enumerate((own_ref, g1_ref, g2_ref, g3_ref)):
        at = pl.multiple_of(lax.rem(place_ref[2] + 4 - d, 4) * columns, 128)
        out_ref[:, pl.ds(at, columns)] = ref[...].astype(F32)


def cell_tables():
    index = np.arange(CELLS)
    zero = index < GRID * GRID
    one = (index >= GRID * GRID) & (index < GRID * GRID + HALF * HALF)
    inner = index - GRID * GRID
    row = np.where(zero, index // GRID, np.where(one, inner // HALF, -9))
    col = np.where(zero, index % GRID, np.where(one, inner % HALF, -9))
    return zero, one, row.astype(np.int32), col.astype(np.int32)


def grid_constants():
    cells = np.arange(GRID * GRID)
    block = (cells // GRID // 2) * HALF + (cells % GRID) // 2
    average = 0.25 * (block[:, None] == block[None, :])
    place = np.zeros((2, GRID * GRID, CELLS))
    place[0, cells, cells] = 1.0
    for b in range(HALF * HALF):
        place[1, np.where(block == b)[0][0], GRID * GRID + b] = 1.0
    spread = np.zeros((2, CELLS, GRID * GRID))
    spread[0, cells, cells] = 1.0
    spread[1, GRID * GRID + block, cells] = 0.25
    return average, place, spread


def tables_body(boxes_ref, weights_ref, cells_ref, fwd_ref, bwd_ref, cols_ref):
    row, col = cells_ref[0:1], cells_ref[1:2]
    zero, one = cells_ref[2:3] > 0, cells_ref[3:4] > 0
    box_zero = boxes_ref[:, 0:1] == 0
    forward = (box_zero & zero) | (~box_zero & one)
    backward = forward | (box_zero & one)
    halved = box_zero & one
    at_rows, at_cols = [], []
    for u in range(SPAN):
        at_y = boxes_ref[:, 1:2] + u
        at_x = boxes_ref[:, 2:3] + u
        at_rows.append(row == jnp.where(halved, at_y // 2, at_y))
        at_cols.append(col == jnp.where(halved, at_x // 2, at_x))
    for i in range(POOLED):
        rows = jnp.zeros(fwd_ref.shape[1:], F32)
        cols = jnp.zeros(fwd_ref.shape[1:], F32)
        for u in range(SPAN):
            y_at, x_at = SPAN * i + u, SPAN * (POOLED + i) + u
            rows = rows + jnp.where(at_rows[u], weights_ref[:, y_at : y_at + 1], 0.0)
            cols = cols + jnp.where(at_cols[u], weights_ref[:, x_at : x_at + 1], 0.0)
        fwd_ref[i] = jnp.where(forward, rows, 0.0)
        bwd_ref[i] = jnp.where(backward, rows, 0.0)
        cols_ref[i] = cols


def sampling_tables(windows, bilinear):
    zero, one, row, col = cell_tables()
    boxes = windows.shape[2]
    cells = np.stack([row, col, zero.astype(np.int32), one.astype(np.int32)] + [row] * 4)
    weights = jnp.transpose(bilinear.reshape(2 * POOLED * SPAN, boxes))
    corners = jnp.transpose(windows.reshape(3, boxes))
    return direct(
        tables_body,
        [((POOLED, boxes, CELLS), F32)] * 3,
        (corners, weights, jnp.asarray(cells, jnp.int32)),
        "tables",
        nbytes=4 * 10**6,
    )


def slot_rows(owner_ids, arrived):
    boxes = owner_ids.shape[0]
    index = jnp.arange(boxes)
    same = (owner_ids[:, None] == owner_ids[None, :]) & (index[None, :] < index[:, None])
    rank = jnp.sum(same.astype(jnp.int32), axis=1)
    slots = arrived.shape[1]
    flat = arrived.reshape(-1, arrived.shape[2])
    pick = (owner_ids * slots + rank)[:, None] == jnp.arange(flat.shape[0])[None, :]
    return mm(pick.astype(BF), flat).astype(BF)


def per_device(
    images, w_in, w_out, fpn_weight, fc6_weight, fc7_weight, windows, bilinear, owners, cotangent
):
    section = lax.axis_index("section")
    dp = lax.axis_index("dp")
    z_here = lax.axis_index("head")
    y_here = dp // 2
    core = dp % 2
    w_first = in_hbm(w_in[0])
    w_second = in_hbm(w_out[0])
    width = images.shape[2]
    inner = w_first.shape[1]
    channels = fc6_weight.shape[0]
    units = fc6_weight.shape[2]
    places = jnp.stack([section, y_here, z_here, core]).astype(jnp.int32)
    average, place, spread = grid_constants()
    average = jnp.asarray(average, BF)
    place = jnp.asarray(place, BF)
    spread = jnp.asarray(spread, BF)

    fpn_rows = jnp.transpose(fpn_weight, (0, 2, 1)).reshape(2 * channels, width)
    fpn_all = lax.all_gather(fpn_rows, "section", axis=0, tiled=True)
    fc6_rows = jnp.transpose(fc6_weight, (1, 0, 2)).reshape(BINS * channels, units)
    tokens = images[0]
    shape = tokens.shape
    wide_shape = (shape[0], inner)
    incoming = None
    for tick in range(4):
        outs = [(shape, BF)]
        if tick > 0:
            outs.append((shape, BF))
        if tick == 3:
            outs += [(shape, BF), (wide_shape, F32)] + [((shape[0], inner // 4), BF)] * 4
        inputs = (tokens,) if tick == 0 else (tokens, incoming)
        results = call(
            functools.partial(forward_body, tick),
            outs,
            (places, *inputs, w_first, w_second),
            f"block_forward_{tick}",
            scalars=1,
            chunks={1 + len(inputs): 1, 2 + len(inputs): 0},
            scratch=(pltpu.VMEM(wide_shape, BF),) if tick == 3 else (),
            vmem=28,
            flops=3 * 10**9,
            nbytes=18 * 10**6,
        )
        result = results[0]
        if tick > 0:
            tokens = results[1]
        if tick == 3:
            normed_b, slope, *act_pieces = results[2:]
            break
        if tick == 0:
            padded = jnp.pad(cotangent[0], ((0, 0), (0, 2), (0, 0)))
            padded, result = lax.optimization_barrier((padded, result))
            cot_arrived = lax.all_to_all(
                padded, ("dp", "head"), split_axis=0, concat_axis=0, tiled=True
            )
        incoming = lax.ppermute(result, "section", [(tick, tick + 1)])
        if tick == 0:
            windows, bilinear, result = lax.optimization_barrier((windows, bilinear, result))
            rows_fwd, rows_bwd, cols_all = sampling_tables(windows, bilinear)
            held = (incoming, rows_fwd, rows_bwd, cols_all)
            incoming, rows_fwd, rows_bwd, cols_all = lax.optimization_barrier(held)
        if tick == 1:
            owner_ids, result = lax.optimization_barrier((owners[0, :, 0], result))
            cot_rows = slot_rows(owner_ids, cot_arrived)
            incoming, cot_rows = lax.optimization_barrier((incoming, cot_rows))
    top = result

    levels, pooled = direct(
        pyramid_body,
        [((4, channels, CELLS), BF), (top.shape, BF)],
        (top, fpn_all, average, place),
        "pyramid",
        flops=10**9,
        nbytes=3 * 10**6,
    )
    sent = [lax.ppermute(levels[s], "section", [(3, s)]) for s in range(3)]
    boxes = windows.shape[2]
    part, crops = direct(
        crops_body,
        [((boxes, units), BF), ((boxes, 2 * PAIRS * channels), BF)],
        (places, levels, *sent, rows_fwd, cols_all, fc6_rows),
        "crops",
        scalars=1,
        flops=10**9,
        nbytes=6 * 10**6,
    )
    parts = [part] + [shifted(part, "section", d) for d in (1, 2, 3)]
    first_b, grad_second, grad_first, maps = direct(
        head_body,
        [((boxes, units), BF)] * 3 + [((2 * channels, GRID * GRID), BF)],
        (
            places,
            *parts,
            cot_rows,
            fc7_weight,
            fc6_rows,
            rows_bwd,
            cols_all,
            spread,
        ),
        "head",
        scratch=(
            pltpu.VMEM((4, boxes, units), F32),
            pltpu.VMEM((2 * PAIRS * channels, boxes), BF),
        ),
        scalars=1,
        flops=10**9,
        nbytes=6 * 10**6,
    )
    returned = [lax.ppermute(maps, "section", [(s, 3)]) for s in range(3)]
    stack_shape = (units, crops.shape[1] + units)
    (stacked,) = direct(
        head_grads_body,
        [(stack_shape, BF)],
        (grad_first, crops, grad_second, first_b),
        "head_grads",
        scratch=(pltpu.VMEM(stack_shape, BF), pltpu.SemaphoreType.DMA((4,))),
        flops=10**9,
        nbytes=6 * 10**6,
        out_space=pl.ANY,
    )
    returned, stacked = lax.optimization_barrier((returned, stacked))
    stacked = lax.psum_scatter(stacked, "dp", scatter_dimension=0, tiled=True)
    grad_out, map_rows = direct(
        top_grad_body,
        [(top.shape, BF), ((8 * channels, GRID * GRID), BF)],
        (*returned, maps, fpn_all),
        "top_grad",
        flops=10**9,
        nbytes=3 * 10**6,
    )

    quarter = inner // 4

    incoming = None
    for tick in range(3):
        outs = [(shape, BF)]
        if tick > 0:
            outs.append((shape, BF))
        inputs = (grad_out,) if tick == 0 else (grad_out, incoming)
        results = call(
            functools.partial(backward_body, tick),
            outs,
            (places, *inputs, slope, tokens, w_first, w_second),
            f"block_backward_{tick}",
            scalars=1,
            chunks={1 + len(inputs): 1, 3 + len(inputs): 1, 4 + len(inputs): 0},
            vmem=28,
            flops=3 * 10**9,
            nbytes=18 * 10**6,
        )
        grad_in = results[0]
        if tick > 0:
            grad_out = results[1]
        if tick == 0:
            held = (grad_in, map_rows, normed_b)
            grad_in, map_rows, normed_b = lax.optimization_barrier(held)
            incoming = lax.ppermute(grad_in, "section", [(3, 2)])
            normed_parts = [normed_b] + [shifted(normed_b, "head", d) for d in (1, 2, 3)]
            order = np.zeros((8 * channels, 8 * channels))
            for r in range(8 * channels):
                order[r, ((r % 16) // 4) * 2 * channels + (r // 16) * 4 + r % 4] = 1.0
            (map_grads,) = direct(
                map_grads_body,
                [((8 * channels, width), BF)],
                (map_rows, jnp.asarray(order, BF), top, pooled),
                "map_grads",
                flops=10**9,
                nbytes=4 * 10**6,
            )
            incoming, map_grads = lax.optimization_barrier((incoming, map_grads))
        elif tick == 1:
            grad_in, act_pieces = lax.optimization_barrier((grad_in, act_pieces))
            incoming = lax.ppermute(grad_in, "section", [(2, 1)])
            act_parts = [act_pieces[0]] + [shifted_y(act_pieces[d], d) for d in (1, 2, 3)]
            held = (incoming, act_parts, stacked, map_grads)
            incoming, act_parts, stacked, map_grads = lax.optimization_barrier(held)
            map_grads = lax.psum_scatter(map_grads, "dp", scatter_dimension=0, tiled=True)
        else:
            incoming = lax.ppermute(grad_in, "section", [(1, 0)])
            incoming, normed_parts = lax.optimization_barrier((incoming, normed_parts))
    (grad_out,) = direct(
        pick_body, [(shape, BF)], (places, grad_out, incoming), "pick", scalars=1, nbytes=10**6
    )

    out_parts = [grad_out] + [shifted_y(grad_out, d) for d in (1, 2, 3)]
    pre_pieces = call(
        last_backward_body,
        [((shape[0], quarter), BF)] * 4,
        (places, grad_out, slope, w_second),
        "block_backward_3",
        scalars=1,
        chunks={2: 1, 3: 0},
        scratch=(pltpu.VMEM(wide_shape, BF),),
        flops=2 * 10**9,
        nbytes=10 * 10**6,
    )
    held = (pre_pieces, stacked, map_grads)
    pre_pieces, stacked, map_grads = lax.optimization_barrier(held)
    stacked = jnp.concatenate([stacked, map_grads], axis=1)
    stacked = lax.psum_scatter(stacked, "head", scatter_dimension=0, tiled=True)
    pre_parts = [pre_pieces[0]] + [shifted(pre_pieces[d], "head", d) for d in (1, 2, 3)]
    pre_parts, out_parts = lax.optimization_barrier((pre_parts, out_parts))
    rows_in = width // 8
    rows_out = quarter // 8
    mine_first, other_first = direct(
        first_grad_body,
        [((4, rows_in, quarter), BF)] * 2,
        (places, *normed_parts, *pre_parts),
        "first_grad",
        vmem=24,
        scalars=1,
        flops=2 * 10**9,
        nbytes=5 * 10**6,
    )
    mine_second, other_second = direct(
        second_grad_body,
        [((4, rows_out, width), BF)] * 2,
        (places, *act_parts, *out_parts),
        "second_grad",
        vmem=24,
        scalars=1,
        flops=2 * 10**9,
        nbytes=5 * 10**6,
    )
    other_second, stacked = lax.optimization_barrier((other_second, stacked))
    wide = crops.shape[1]
    fpn_part = stacked[:, wide + units :].reshape(4, 4, width)
    fpn_got = [lax.ppermute(fpn_part[s], "section", [(3, s)]) for s in range(3)]
    swapped_first = core_swapped(other_first)
    swapped_second = core_swapped(other_second)

    def pair_sums(which, mine, swapped, name):
        return direct(
            functools.partial(pair_body, which),
            [(mine.shape[1:], F32)] + [(mine.shape[1:], BF)] * 3,
            (places, mine, swapped),
            name,
            scalars=1,
            nbytes=5 * 10**6,
        )

    kept_first, *out_first = pair_sums(1, mine_first, swapped_first, "pair_first")
    grad_w_out, *out_second = pair_sums(2, mine_second, swapped_second, "pair_second")
    held = (out_first, out_second, fpn_got)
    out_first, out_second, fpn_got = lax.optimization_barrier(held)
    got_first = [shifted_y(out_first[d - 1], d) for d in (1, 2, 3)]
    got_second = [shifted(out_second[d - 1], "head", d) for d in (1, 2, 3)]
    own = jnp.where(section == 3, fpn_part[3], fpn_got[0] + fpn_got[1] + fpn_got[2])
    fpn_rows = lax.all_to_all(
        jnp.broadcast_to(own[None], (32,) + own.shape),
        ("dp", "head"),
        split_axis=0,
        concat_axis=0,
        tiled=True,
    )
    last_rows = rows_in // 4
    got_first, stacked = lax.optimization_barrier((got_first, stacked))
    kept_strip, *out_strips = direct(
        strips_body,
        [((last_rows, quarter), F32)] + [((last_rows, quarter), BF)] * 3,
        (places, kept_first, *got_first),
        "strips",
        scalars=1,
        nbytes=3 * 10**6,
    )
    strips = [shifted(out_strips[d - 1], "head", d) for d in (1, 2, 3)]
    for got in got_second:
        grad_w_out = grad_w_out + got.astype(F32)
    (grad_w_in,) = direct(
        join_body,
        [((last_rows, inner), F32)],
        (places, kept_strip, *strips),
        "join",
        scalars=1,
        nbytes=10**6,
    )

    fc6_part = stacked[:, :wide].reshape(-1, 2 * PAIRS, channels)[:, :BINS]
    fc6_out = jnp.transpose(fc6_part.astype(F32), (2, 1, 0))
    fc7_out = jnp.transpose(stacked[:, wide : wide + units].astype(F32))
    fpn_out = fpn_rows.astype(F32)
    fpn_out = jnp.transpose(fpn_out.reshape(2, channels, width), (0, 2, 1))
    return (grad_w_in[None], grad_w_out[None], fpn_out, fc6_out, fc7_out)


def solution(mesh):
    return jax.shard_map(
        per_device,
        mesh=mesh,
        in_specs=(
            P(("dp", "head"), None, None),
            P("section", None, None),
            P("section", None, None),
            P(None, None, "section"),
            P("section", None, None),
            P(),
            P(None, ("dp", "head"), None),
            P(None, None, None, ("dp", "head"), None),
            P(("dp", "head"), None, None),
            P(("dp", "head"), None, None, None),
        ),
        out_specs=(
            P("section", ("dp", "head"), None),
            P("section", ("dp", "head"), None),
            P(None, None, "section"),
            P("section", None, ("dp", "head")),
            P(None, ("dp", "head")),
        ),
        check_vma=False,
    )
```

```python
import functools
import math

import jax
import jax.numpy as jnp
import numpy as np
from jax import lax
from jax.experimental import pallas as pl
from jax.experimental.pallas import tpu as pltpu
from jax.sharding import PartitionSpec as P

GRID = 12
HALF = GRID // 2
SPAN = 4
POOLED = 7
BINS = POOLED * POOLED
PAIRS = (BINS + 1) // 2
CELLS = 256

EPS = 1e-06
GELU_C = math.sqrt(2.0 / math.pi)
BF = jnp.bfloat16
F32 = jnp.float32
STEP = 512
AHEAD = 3

NN = (((1,), (0,)), ((), ()))
NT = (((1,), (1,)), ((), ()))
TN = (((0,), (0,)), ((), ()))


def mm(left, right, dims=NN):
    return lax.dot_general(left, right, dims, preferred_element_type=F32)


def gelu_parts(values):
    inner_arg = GELU_C * (values + 0.044715 * values * values * values)
    tangent = jnp.tanh(inner_arg)
    result = 0.5 * values * (1.0 + tangent)
    slope = 0.5 * (1.0 + tangent) + 0.5 * values * (1.0 - tangent * tangent) * GELU_C * (
        1.0 + 3.0 * 0.044715 * values * values
    )
    return (result, slope)


def norm_parts(tokens):
    floats = tokens.astype(F32)
    centred = floats - jnp.mean(floats, axis=-1, keepdims=True)
    scale_inv = lax.rsqrt(jnp.mean(centred * centred, axis=-1, keepdims=True) + EPS)
    return (centred * scale_inv, scale_inv)


class Staged:
    def __init__(self, source, buffer, sems, chunk_axis):
        self.buffer = buffer
        self.shape = buffer.shape
        self.axis = chunk_axis
        self.copies = []
        self.waited = set()
        if chunk_axis is None:
            self.copies.append(pltpu.make_async_copy(source, buffer, sems.at[0]))
        else:
            for j in range(self.shape[chunk_axis] // STEP):
                at = self.part(j)
                self.copies.append(
                    pltpu.make_async_copy(source.at[at], buffer.at[at], sems.at[j])
                )

    def part(self, j):
        span = pl.ds(j * STEP, STEP)
        return (span, slice(None)) if self.axis == 0 else (slice(None), span)

    def start(self, j):
        if j < len(self.copies):
            self.copies[j].start()

    def wait(self, j):
        if j not in self.waited:
            self.waited.add(j)
            self.copies[j].wait()

    def chunk(self, j):
        self.wait(j)
        self.start(j + AHEAD)
        return self.buffer[self.part(j)]

    def __getitem__(self, index):
        self.wait(0)
        return self.buffer[index]

    def finish(self):
        for j in range(len(self.copies)):
            self.wait(j)


def call(body, outs, args, name, scratch=(), scalars=0, chunks=None, flops=0, nbytes=0, vmem=18):
    chunks = chunks or {}
    count = len(args) - scalars
    axes = [chunks.get(i + scalars) for i in range(count)]
    sizes = [
        1 if axis is None else arg.shape[axis] // STEP for axis, arg in zip(axes, args[scalars:])
    ]

    def kernel(*refs):
        given, sources = refs[:scalars], refs[scalars : len(args)]
        results = refs[len(args) : len(args) + len(outs)]
        rest = refs[len(args) + len(outs) :]
        buffers, sems, extra = rest[:count], rest[count : 2 * count], rest[2 * count :]
        staged = [Staged(*parts) for parts in zip(sources, buffers, sems, axes)]
        for j in range(AHEAD):
            for item in staged:
                item.start(j)
        body(*given, *staged, *results, *extra)
        for item in staged:
            item.finish()

    return pl.pallas_call(
        kernel,
        out_shape=[jax.ShapeDtypeStruct(s, d) for s, d in outs],
        in_specs=[pl.BlockSpec(memory_space=pltpu.SMEM)] * scalars
        + [pl.BlockSpec(memory_space=pl.ANY)] * count,
        out_specs=[pl.BlockSpec(memory_space=pltpu.VMEM) for _ in outs],
        scratch_shapes=[pltpu.VMEM(arg.shape, arg.dtype) for arg in args[scalars:]]
        + [pltpu.SemaphoreType.DMA((size,)) for size in sizes]
        + list(scratch),
        compiler_params=pltpu.CompilerParams(vmem_limit_bytes=vmem * 1024 * 1024),
        cost_estimate=pl.CostEstimate(flops=flops, bytes_accessed=nbytes, transcendentals=0),
        name=name,
    )(*args)


def direct(
    body,
    outs,
    args,
    name,
    scratch=(),
    scalars=0,
    flops=0,
    nbytes=0,
    vmem=18,
    out_space=pltpu.VMEM,
):
    return pl.pallas_call(
        body,
        out_shape=[jax.ShapeDtypeStruct(s, d) for s, d in outs],
        in_specs=[pl.BlockSpec(memory_space=pltpu.SMEM)] * scalars
        + [pl.BlockSpec(memory_space=pltpu.VMEM)] * (len(args) - scalars),
        out_specs=[pl.BlockSpec(memory_space=out_space) for _ in outs],
        scratch_shapes=list(scratch),
        compiler_params=pltpu.CompilerParams(vmem_limit_bytes=vmem * 1024 * 1024),
        cost_estimate=pl.CostEstimate(flops=flops, bytes_accessed=nbytes, transcendentals=0),
        name=name,
    )(*args)


def in_hbm(array):
    return pltpu.with_memory_space_constraint(array, pltpu.HBM)


def ring(axis, shift):
    size = lax.axis_size(axis)
    return [(i, (i + shift) % size) for i in range(size)]


def shifted(value, axis, shift):
    return lax.ppermute(value, axis, ring(axis, shift))


def shifted_y(value, shift):
    return shifted(value, "dp", 2 * shift)


def core_swapped(value):
    return lax.ppermute(value, "dp", [(i, i ^ 1) for i in range(lax.axis_size("dp"))])


def gelu_quick(values):
    square = values * values
    half = 0.5 + 0.5 * jnp.tanh(values * (GELU_C + (GELU_C * 0.044715) * square))
    return half, square


def forward_body(tick, place_ref, *refs):
    if tick == 3:
        *refs, held_ref = refs
    if tick == 0:
        old_ref, w1_ref, w2_ref, *outs = refs
        tokens = old_ref[...]
    else:
        old_ref, new_ref, w1_ref, w2_ref, *outs = refs
        tokens = jnp.where(place_ref[0] == tick, new_ref[...], old_ref[...])
    result_ref = outs[0]
    if tick > 0:
        outs[1][...] = tokens
    normed = norm_parts(tokens)[0].astype(BF)
    if tick == 3:
        outs[2][...] = normed
    total = tokens.astype(F32)
    count = w1_ref.shape[1] // STEP
    values = mm(normed, w1_ref.chunk(0))
    for j in range(count):
        later = mm(normed, w1_ref.chunk(j + 1)) if j + 1 < count else None
        half, square = gelu_quick(values)
        activ = (values * half).astype(BF)
        if tick == 3:
            span = slice(j * STEP, (j + 1) * STEP)
            held_ref[:, span] = activ
            outs[3][:, span] = half + (values * (2.0 * half) * (1.0 - half)) * (
                GELU_C + (3.0 * 0.044715 * GELU_C) * square
            )
        total = total + mm(activ, w2_ref.chunk(j))
        values = later
    result_ref[...] = total.astype(BF)
    if tick == 3:
        put_pieces(place_ref[1], held_ref, outs[4:])


def put_pieces(place, held_ref, outs):
    columns = outs[0].shape[1]
    for d, ref in enumerate(outs):
        at = pl.multiple_of(lax.rem(place + d, 4) * columns, 128)
        ref[...] = held_ref[:, pl.ds(at, columns)]


def backward_body(tick, place_ref, *refs):
    if tick == 0:
        old_ref, slope_ref, tokens_ref, w1_ref, w2_ref, *outs = refs
        grad_out = old_ref[...]
    else:
        old_ref, new_ref, slope_ref, tokens_ref, w1_ref, w2_ref, *outs = refs
        grad_out = jnp.where(place_ref[0] == 3 - tick, new_ref[...], old_ref[...])
        outs[1][...] = grad_out
    total = jnp.zeros(grad_out.shape, F32)
    count = w1_ref.shape[1] // STEP
    grad_act = mm(grad_out, w2_ref.chunk(0), NT)
    for j in range(count):
        later = mm(grad_out, w2_ref.chunk(j + 1), NT) if j + 1 < count else None
        grad_pre = (grad_act * slope_ref.chunk(j)).astype(BF)
        total = total + mm(grad_pre, w1_ref.chunk(j), NT)
        grad_act = later
    normed, scale_inv = norm_parts(tokens_ref[...])
    grad_tok = scale_inv * (
        total
        - jnp.mean(total, axis=-1, keepdims=True)
        - normed * jnp.mean(total * normed, axis=-1, keepdims=True)
    )
    outs[0][...] = (grad_out.astype(F32) + grad_tok).astype(BF)


def last_backward_body(place_ref, grad_ref, slope_ref, w2_ref, *refs):
    *outs, held_ref = refs
    grad_out = grad_ref[...]
    count = w2_ref.shape[0] // STEP
    grad_act = mm(grad_out, w2_ref.chunk(0), NT)
    for j in range(count):
        later = mm(grad_out, w2_ref.chunk(j + 1), NT) if j + 1 < count else None
        held_ref[:, j * STEP : (j + 1) * STEP] = (grad_act * slope_ref.chunk(j)).astype(BF)
        grad_act = later
    put_pieces(place_ref[2], held_ref, outs)


def pick_body(place_ref, old_ref, new_ref, out_ref):
    out_ref[...] = jnp.where(place_ref[0] == 0, new_ref[...], old_ref[...])


def pyramid_body(top_ref, weight_ref, avg_ref, place_ref, levels_ref, pooled_ref):
    top = top_ref[...]
    pooled = mm(avg_ref[...], top).astype(BF)
    pooled_ref[...] = pooled
    weights = weight_ref[...]
    from_top = mm(weights, top, NT)
    from_pooled = mm(weights, pooled, NT)
    half = weights.shape[0] // 8
    for s in range(4):
        base = 2 * half * s
        one = from_pooled[base + half : base + 2 * half]
        zero = from_top[base : base + half] + one
        levels_ref[s] = (
            mm(zero.astype(BF), place_ref[0]) + mm(one.astype(BF), place_ref[1])
        ).astype(BF)


def top_grad_body(z0_ref, z1_ref, z2_ref, z3_ref, weight_ref, grad_ref, rows_ref):
    rows = jnp.concatenate([z0_ref[...], z1_ref[...], z2_ref[...], z3_ref[...]], axis=0)
    rows_ref[...] = rows
    grad_ref[...] = mm(rows, weight_ref[...], TN).astype(BF)


def crops_body(
    sec_ref, levels_ref, r0_ref, r1_ref, r2_ref, rows_ref, cols_ref, fc6_ref, part_ref, crops_ref
):
    is_last = sec_ref[0] == 3
    arrived = r0_ref[...] + r1_ref[...] + r2_ref[...]
    own = jnp.where(is_last, levels_ref[3], arrived)
    blank = jnp.zeros_like(own)
    both = jnp.concatenate(
        [jnp.concatenate([own, blank], axis=1), jnp.concatenate([blank, own], axis=1)], axis=0
    )

    def weights(b):
        if b >= BINS:
            return jnp.zeros((rows_ref.shape[1], CELLS), BF)
        return (rows_ref[b // POOLED] * cols_ref[b % POOLED]).astype(BF)

    for p in range(PAIRS):
        pair = jnp.concatenate([weights(2 * p), weights(2 * p + 1)], axis=1)
        crops_ref[:, 128 * p : 128 * (p + 1)] = mm(pair, both, NT).astype(BF)
    depth = fc6_ref.shape[0]
    whole = depth // 128 * 128
    part = mm(crops_ref[:, :whole], fc6_ref[:whole])
    part = part + mm(crops_ref[:, whole:depth], fc6_ref[whole:])
    part_ref[...] = part.astype(BF)


def head_body(
    sec_ref,
    p0_ref,
    p1_ref,
    p2_ref,
    p3_ref,
    cot_ref,
    fc7_ref,
    fc6_ref,
    rows_ref,
    cols_ref,
    spread_ref,
    first_ref,
    second_ref,
    grad_ref,
    maps_ref,
    parts_ref,
    back_ref,
):
    sec = sec_ref[0]
    for d, ref in enumerate((p0_ref, p1_ref, p2_ref, p3_ref)):
        parts_ref[lax.rem(sec + 4 - d, 4)] = ref[...].astype(F32)
    first_pre = parts_ref[0] + parts_ref[1] + parts_ref[2] + parts_ref[3]
    first_act, first_slope = gelu_parts(first_pre)
    first_b = first_act.astype(BF)
    first_ref[...] = first_b
    second_pre = mm(first_b, fc7_ref[...])
    second_slope = gelu_parts(second_pre)[1]
    grad_second = (cot_ref[...].astype(F32) * second_slope).astype(BF)
    second_ref[...] = grad_second
    grad_first = (mm(grad_second, fc7_ref[...], NT) * first_slope).astype(BF)
    grad_ref[...] = grad_first
    depth = fc6_ref.shape[0]
    back_ref[:depth] = mm(fc6_ref[...], grad_first, NT).astype(BF)
    back_ref[depth:] = jnp.zeros((back_ref.shape[0] - depth, back_ref.shape[1]), BF)
    channels = back_ref.shape[0] // (2 * PAIRS)

    def weights(b):
        if b >= BINS:
            return jnp.zeros((rows_ref.shape[1], CELLS), BF)
        return (rows_ref[b // POOLED] * cols_ref[b % POOLED]).astype(BF)

    total = jnp.zeros((channels, CELLS), F32)
    for p in range(PAIRS):
        lo = 2 * p * channels
        left = jnp.concatenate(
            [back_ref[lo : lo + channels], back_ref[lo + channels : lo + 2 * channels]], axis=1
        )
        right = jnp.concatenate([weights(2 * p), weights(2 * p + 1)], axis=0)
        total = total + mm(left, right)
    total_b = total.astype(BF)
    maps_ref[:channels] = mm(total_b, spread_ref[0]).astype(BF)
    maps_ref[channels:] = mm(total_b, spread_ref[1]).astype(BF)


def head_grads_body(grad_ref, crops_ref, second_ref, first_ref, out_ref, held_ref, sems):
    wide = crops_ref.shape[1]
    rows = out_ref.shape[0] // 4
    copies = []
    for j in range(4):
        at = pl.ds(j * rows, rows)
        span = slice(j * rows, (j + 1) * rows)
        held_ref[at, :wide] = mm(grad_ref[:, span], crops_ref[...], TN).astype(BF)
        held_ref[at, wide:] = mm(second_ref[:, span], first_ref[...], TN).astype(BF)
        copies.append(pltpu.make_async_copy(held_ref.at[at], out_ref.at[at], sems.at[j]))
        copies[-1].start()
    for copy in copies:
        copy.wait()


def map_grads_body(maps_ref, order_ref, top_ref, pooled_ref, out_ref):
    ordered = mm(order_ref[...], maps_ref[...]).astype(BF)
    half = ordered.shape[0] // 2
    out_ref[:half] = mm(ordered[:half], top_ref[...]).astype(BF)
    out_ref[half:] = mm(ordered[half:], pooled_ref[...]).astype(BF)


def first_grad_body(
    core_ref, a0_ref, a1_ref, a2_ref, a3_ref, g0_ref, g1_ref, g2_ref, g3_ref, mine_ref, other_ref
):
    is_zero = core_ref[3] == 0
    lefts = (a0_ref, a1_ref, a2_ref, a3_ref)
    rights = (g0_ref, g1_ref, g2_ref, g3_ref)
    total = mm(lefts[0][...], rights[0][...], TN)
    for d in range(1, 4):
        total = total + mm(lefts[d][...], rights[d][...], TN)
    rows = mine_ref.shape[1]
    for y in range(4):
        low = total[2 * y * rows : (2 * y + 1) * rows]
        high = total[(2 * y + 1) * rows : (2 * y + 2) * rows]
        mine_ref[y] = jnp.where(is_zero, low, high).astype(BF)
        other_ref[y] = jnp.where(is_zero, high, low).astype(BF)


def second_grad_body(
    core_ref, a0_ref, a1_ref, a2_ref, a3_ref, g0_ref, g1_ref, g2_ref, g3_ref, mine_ref, other_ref
):
    is_zero = core_ref[3] == 0
    lefts = (a0_ref, a1_ref, a2_ref, a3_ref)
    rights = (g0_ref, g1_ref, g2_ref, g3_ref)
    total = mm(lefts[0][...], rights[0][...], TN)
    for d in range(1, 4):
        total = total + mm(lefts[d][...], rights[d][...], TN)
    rows = mine_ref.shape[1]
    for z in range(4):
        low = total[z * rows : (z + 1) * rows]
        high = total[(z + 4) * rows : (z + 5) * rows]
        mine_ref[z] = jnp.where(is_zero, low, high).astype(BF)
        other_ref[z] = jnp.where(is_zero, high, low).astype(BF)


def pair_body(which, place_ref, mine_ref, got_ref, kept_ref, one_ref, two_ref, three_ref):
    place = place_ref[which]

    def total(d):
        at = lax.rem(place + d, 4)
        return mine_ref[at].astype(F32) + got_ref[at].astype(F32)

    kept_ref[...] = total(0)
    for d, ref in enumerate((one_ref, two_ref, three_ref)):
        ref[...] = total(d + 1).astype(BF)


def strips_body(
    place_ref, kept_ref, g1_ref, g2_ref, g3_ref, own_ref, one_ref, two_ref, three_ref
):
    total = kept_ref[...]
    for ref in (g1_ref, g2_ref, g3_ref):
        total = total + ref[...].astype(F32)
    rows = own_ref.shape[0]
    strips = [total[j * rows : (j + 1) * rows] for j in range(4)]
    for d, ref in enumerate((own_ref, one_ref, two_ref, three_ref)):
        at = lax.rem(place_ref[2] + d, 4)
        picked = strips[3]
        for j in range(3):
            picked = jnp.where(at == j, strips[j], picked)
        ref[...] = picked.astype(ref.dtype)


def join_body(place_ref, own_ref, g1_ref, g2_ref, g3_ref, out_ref):
    columns = own_ref.shape[1]
    for d, ref in enumerate((own_ref, g1_ref, g2_ref, g3_ref)):
        at = pl.multiple_of(lax.rem(place_ref[2] + 4 - d, 4) * columns, 128)
        out_ref[:, pl.ds(at, columns)] = ref[...].astype(F32)


def cell_tables():
    index = np.arange(CELLS)
    zero = index < GRID * GRID
    one = (index >= GRID * GRID) & (index < GRID * GRID + HALF * HALF)
    inner = index - GRID * GRID
    row = np.where(zero, index // GRID, np.where(one, inner // HALF, -9))
    col = np.where(zero, index % GRID, np.where(one, inner % HALF, -9))
    return zero, one, row.astype(np.int32), col.astype(np.int32)


def grid_constants():
    cells = np.arange(GRID * GRID)
    block = (cells // GRID // 2) * HALF + (cells % GRID) // 2
    average = 0.25 * (block[:, None] == block[None, :])
    place = np.zeros((2, GRID * GRID, CELLS))
    place[0, cells, cells] = 1.0
    for b in range(HALF * HALF):
        place[1, np.where(block == b)[0][0], GRID * GRID + b] = 1.0
    spread = np.zeros((2, CELLS, GRID * GRID))
    spread[0, cells, cells] = 1.0
    spread[1, GRID * GRID + block, cells] = 0.25
    return average, place, spread


def tables_body(boxes_ref, weights_ref, cells_ref, fwd_ref, bwd_ref, cols_ref):
    row, col = cells_ref[0:1], cells_ref[1:2]
    zero, one = cells_ref[2:3] > 0, cells_ref[3:4] > 0
    box_zero = boxes_ref[:, 0:1] == 0
    forward = (box_zero & zero) | (~box_zero & one)
    backward = forward | (box_zero & one)
    halved = box_zero & one
    at_rows, at_cols = [], []
    for u in range(SPAN):
        at_y = boxes_ref[:, 1:2] + u
        at_x = boxes_ref[:, 2:3] + u
        at_rows.append(row == jnp.where(halved, at_y // 2, at_y))
        at_cols.append(col == jnp.where(halved, at_x // 2, at_x))
    for i in range(POOLED):
        rows = jnp.zeros(fwd_ref.shape[1:], F32)
        cols = jnp.zeros(fwd_ref.shape[1:], F32)
        for u in range(SPAN):
            y_at, x_at = SPAN * i + u, SPAN * (POOLED + i) + u
            rows = rows + jnp.where(at_rows[u], weights_ref[:, y_at : y_at + 1], 0.0)
            cols = cols + jnp.where(at_cols[u], weights_ref[:, x_at : x_at + 1], 0.0)
        fwd_ref[i] = jnp.where(forward, rows, 0.0)
        bwd_ref[i] = jnp.where(backward, rows, 0.0)
        cols_ref[i] = cols


def sampling_tables(windows, bilinear):
    zero, one, row, col = cell_tables()
    boxes = windows.shape[2]
    cells = np.stack([row, col, zero.astype(np.int32), one.astype(np.int32)] + [row] * 4)
    weights = jnp.transpose(bilinear.reshape(2 * POOLED * SPAN, boxes))
    corners = jnp.transpose(windows.reshape(3, boxes))
    return direct(
        tables_body,
        [((POOLED, boxes, CELLS), F32)] * 3,
        (corners, weights, jnp.asarray(cells, jnp.int32)),
        "tables",
        nbytes=4 * 10**6,
    )


def slot_rows(owner_ids, arrived):
    boxes = owner_ids.shape[0]
    index = jnp.arange(boxes)
    same = (owner_ids[:, None] == owner_ids[None, :]) & (index[None, :] < index[:, None])
    rank = jnp.sum(same.astype(jnp.int32), axis=1)
    slots = arrived.shape[1]
    flat = arrived.reshape(-1, arrived.shape[2])
    pick = (owner_ids * slots + rank)[:, None] == jnp.arange(flat.shape[0])[None, :]
    return mm(pick.astype(BF), flat).astype(BF)


def per_device(
    images, w_in, w_out, fpn_weight, fc6_weight, fc7_weight, windows, bilinear, owners, cotangent
):
    section = lax.axis_index("section")
    dp = lax.axis_index("dp")
    z_here = lax.axis_index("head")
    y_here = dp // 2
    core = dp % 2
    w_first = in_hbm(w_in[0])
    w_second = in_hbm(w_out[0])
    width = images.shape[2]
    inner = w_first.shape[1]
    channels = fc6_weight.shape[0]
    units = fc6_weight.shape[2]
    places = jnp.stack([section, y_here, z_here, core]).astype(jnp.int32)
    average, place, spread = grid_constants()
    average = jnp.asarray(average, BF)
    place = jnp.asarray(place, BF)
    spread = jnp.asarray(spread, BF)

    fpn_rows = jnp.transpose(fpn_weight, (0, 2, 1)).reshape(2 * channels, width)
    fpn_all = lax.all_gather(fpn_rows, "section", axis=0, tiled=True)
    fc6_rows = jnp.transpose(fc6_weight, (1, 0, 2)).reshape(BINS * channels, units)
    tokens = images[0]
    shape = tokens.shape
    wide_shape = (shape[0], inner)
    incoming = None
    for tick in range(4):
        outs = [(shape, BF)]
        if tick > 0:
            outs.append((shape, BF))
        if tick == 3:
            outs += [(shape, BF), (wide_shape, F32)] + [((shape[0], inner // 4), BF)] * 4
        inputs = (tokens,) if tick == 0 else (tokens, incoming)
        results = call(
            functools.partial(forward_body, tick),
            outs,
            (places, *inputs, w_first, w_second),
            f"block_forward_{tick}",
            scalars=1,
            chunks={1 + len(inputs): 1, 2 + len(inputs): 0},
            scratch=(pltpu.VMEM(wide_shape, BF),) if tick == 3 else (),
            vmem=28,
            flops=3 * 10**9,
            nbytes=18 * 10**6,
        )
        result = results[0]
        if tick > 0:
            tokens = results[1]
        if tick == 3:
            normed_b, slope, *act_pieces = results[2:]
            break
        if tick == 0:
            cotangent, result = lax.optimization_barrier((cotangent, result))
            padded = jnp.pad(cotangent[0], ((0, 0), (0, 2), (0, 0)))
            cot_arrived = lax.all_to_all(
                padded, ("dp", "head"), split_axis=0, concat_axis=0, tiled=True
            )
        incoming = lax.ppermute(result, "section", [(tick, tick + 1)])
        if tick == 0:
            windows, bilinear, result = lax.optimization_barrier((windows, bilinear, result))
            rows_fwd, rows_bwd, cols_all = sampling_tables(windows, bilinear)
            held = (incoming, rows_fwd, rows_bwd, cols_all)
            incoming, rows_fwd, rows_bwd, cols_all = lax.optimization_barrier(held)
        if tick == 1:
            owner_ids, result = lax.optimization_barrier((owners[0, :, 0], result))
            cot_rows = slot_rows(owner_ids, cot_arrived)
            incoming, cot_rows = lax.optimization_barrier((incoming, cot_rows))
        if tick == 2:
            incoming, fpn_all = lax.optimization_barrier((incoming, fpn_all))
    top = result

    levels, pooled = direct(
        pyramid_body,
        [((4, channels, CELLS), BF), (top.shape, BF)],
        (top, fpn_all, average, place),
        "pyramid",
        flops=10**9,
        nbytes=3 * 10**6,
    )
    sent = [lax.ppermute(levels[s], "section", [(3, s)]) for s in range(3)]
    boxes = windows.shape[2]
    part, crops = direct(
        crops_body,
        [((boxes, units), BF), ((boxes, 2 * PAIRS * channels), BF)],
        (places, levels, *sent, rows_fwd, cols_all, fc6_rows),
        "crops",
        scalars=1,
        flops=10**9,
        nbytes=6 * 10**6,
    )
    parts = [part] + [shifted(part, "section", d) for d in (1, 2, 3)]
    first_b, grad_second, grad_first, maps = direct(
        head_body,
        [((boxes, units), BF)] * 3 + [((2 * channels, GRID * GRID), BF)],
        (
            places,
            *parts,
            cot_rows,
            fc7_weight,
            fc6_rows,
            rows_bwd,
            cols_all,
            spread,
        ),
        "head",
        scratch=(
            pltpu.VMEM((4, boxes, units), F32),
            pltpu.VMEM((2 * PAIRS * channels, boxes), BF),
        ),
        scalars=1,
        flops=10**9,
        nbytes=6 * 10**6,
    )
    returned = [lax.ppermute(maps, "section", [(s, 3)]) for s in range(3)]
    stack_shape = (units, crops.shape[1] + units)
    (stacked,) = direct(
        head_grads_body,
        [(stack_shape, BF)],
        (grad_first, crops, grad_second, first_b),
        "head_grads",
        scratch=(pltpu.VMEM(stack_shape, BF), pltpu.SemaphoreType.DMA((4,))),
        flops=10**9,
        nbytes=6 * 10**6,
        out_space=pl.ANY,
    )
    returned, stacked = lax.optimization_barrier((returned, stacked))
    stacked = lax.psum_scatter(stacked, "dp", scatter_dimension=0, tiled=True)
    grad_out, map_rows = direct(
        top_grad_body,
        [(top.shape, BF), ((8 * channels, GRID * GRID), BF)],
        (*returned, maps, fpn_all),
        "top_grad",
        flops=10**9,
        nbytes=3 * 10**6,
    )

    quarter = inner // 4

    incoming = None
    for tick in range(3):
        outs = [(shape, BF)]
        if tick > 0:
            outs.append((shape, BF))
        inputs = (grad_out,) if tick == 0 else (grad_out, incoming)
        results = call(
            functools.partial(backward_body, tick),
            outs,
            (places, *inputs, slope, tokens, w_first, w_second),
            f"block_backward_{tick}",
            scalars=1,
            chunks={1 + len(inputs): 1, 3 + len(inputs): 1, 4 + len(inputs): 0},
            vmem=28,
            flops=3 * 10**9,
            nbytes=18 * 10**6,
        )
        grad_in = results[0]
        if tick > 0:
            grad_out = results[1]
        if tick == 0:
            held = (grad_in, map_rows, act_pieces)
            grad_in, map_rows, act_pieces = lax.optimization_barrier(held)
            incoming = lax.ppermute(grad_in, "section", [(3, 2)])
            act_parts = [act_pieces[0]] + [shifted_y(act_pieces[d], d) for d in (1, 2, 3)]
            order = np.zeros((8 * channels, 8 * channels))
            for r in range(8 * channels):
                order[r, ((r % 16) // 4) * 2 * channels + (r // 16) * 4 + r % 4] = 1.0
            (map_grads,) = direct(
                map_grads_body,
                [((8 * channels, width), BF)],
                (map_rows, jnp.asarray(order, BF), top, pooled),
                "map_grads",
                flops=10**9,
                nbytes=4 * 10**6,
            )
            incoming, map_grads = lax.optimization_barrier((incoming, map_grads))
        elif tick == 1:
            incoming = lax.ppermute(grad_in, "section", [(2, 1)])
            held = (incoming, act_parts, stacked, map_grads)
            incoming, act_parts, stacked, map_grads = lax.optimization_barrier(held)
            map_grads = lax.psum_scatter(map_grads, "dp", scatter_dimension=0, tiled=True)
        else:
            grad_in, normed_b = lax.optimization_barrier((grad_in, normed_b))
            incoming = lax.ppermute(grad_in, "section", [(1, 0)])
            normed_parts = [normed_b] + [shifted(normed_b, "head", d) for d in (1, 2, 3)]
    (grad_out,) = direct(
        pick_body, [(shape, BF)], (places, grad_out, incoming), "pick", scalars=1, nbytes=10**6
    )

    out_parts = [grad_out] + [shifted_y(grad_out, d) for d in (1, 2, 3)]
    pre_pieces = call(
        last_backward_body,
        [((shape[0], quarter), BF)] * 4,
        (places, grad_out, slope, w_second),
        "block_backward_3",
        scalars=1,
        chunks={2: 1, 3: 0},
        scratch=(pltpu.VMEM(wide_shape, BF),),
        flops=2 * 10**9,
        nbytes=10 * 10**6,
    )
    held = (pre_pieces, out_parts, normed_parts, stacked, map_grads)
    pre_pieces, out_parts, normed_parts, stacked, map_grads = lax.optimization_barrier(held)
    stacked = jnp.concatenate([stacked, map_grads], axis=1)
    stacked = lax.psum_scatter(stacked, "head", scatter_dimension=0, tiled=True)
    pre_parts = [pre_pieces[0]] + [shifted(pre_pieces[d], "head", d) for d in (1, 2, 3)]
    rows_in = width // 8
    rows_out = quarter // 8
    mine_first, other_first = direct(
        first_grad_body,
        [((4, rows_in, quarter), BF)] * 2,
        (places, *normed_parts, *pre_parts),
        "first_grad",
        vmem=24,
        scalars=1,
        flops=2 * 10**9,
        nbytes=5 * 10**6,
    )
    mine_second, other_second = direct(
        second_grad_body,
        [((4, rows_out, width), BF)] * 2,
        (places, *act_parts, *out_parts),
        "second_grad",
        vmem=24,
        scalars=1,
        flops=2 * 10**9,
        nbytes=5 * 10**6,
    )
    swapped_first = core_swapped(other_first)
    swapped_second = core_swapped(other_second)

    def pair_sums(which, mine, swapped, name):
        return direct(
            functools.partial(pair_body, which),
            [(mine.shape[1:], F32)] + [(mine.shape[1:], BF)] * 3,
            (places, mine, swapped),
            name,
            scalars=1,
            nbytes=5 * 10**6,
        )

    kept_first, *out_first = pair_sums(1, mine_first, swapped_first, "pair_first")
    grad_w_out, *out_second = pair_sums(2, mine_second, swapped_second, "pair_second")
    out_second, stacked = lax.optimization_barrier((out_second, stacked))
    wide = crops.shape[1]
    fpn_part = stacked[:, wide + units :].reshape(4, 4, width)
    fpn_got = [lax.ppermute(fpn_part[s], "section", [(3, s)]) for s in range(3)]
    got_first = [shifted_y(out_first[d - 1], d) for d in (1, 2, 3)]
    got_second = [shifted(out_second[d - 1], "head", d) for d in (1, 2, 3)]
    own = jnp.where(section == 3, fpn_part[3], fpn_got[0] + fpn_got[1] + fpn_got[2])
    fpn_rows = lax.all_to_all(
        jnp.broadcast_to(own[None], (32,) + own.shape),
        ("dp", "head"),
        split_axis=0,
        concat_axis=0,
        tiled=True,
    )
    last_rows = rows_in // 4
    got_first, stacked = lax.optimization_barrier((got_first, stacked))
    kept_strip, *out_strips = direct(
        strips_body,
        [((last_rows, quarter), F32)] + [((last_rows, quarter), BF)] * 3,
        (places, kept_first, *got_first),
        "strips",
        scalars=1,
        nbytes=3 * 10**6,
    )
    strips = [shifted(out_strips[d - 1], "head", d) for d in (1, 2, 3)]
    for got in got_second:
        grad_w_out = grad_w_out + got.astype(F32)
    (grad_w_in,) = direct(
        join_body,
        [((last_rows, inner), F32)],
        (places, kept_strip, *strips),
        "join",
        scalars=1,
        nbytes=10**6,
    )

    fc6_part = stacked[:, :wide].reshape(-1, 2 * PAIRS, channels)[:, :BINS]
    fc6_out = jnp.transpose(fc6_part.astype(F32), (2, 1, 0))
    fc7_out = jnp.transpose(stacked[:, wide : wide + units].astype(F32))
    fpn_out = fpn_rows.astype(F32)
    fpn_out = jnp.transpose(fpn_out.reshape(2, channels, width), (0, 2, 1))
    return (grad_w_in[None], grad_w_out[None], fpn_out, fc6_out, fc7_out)


def solution(mesh):
    return jax.shard_map(
        per_device,
        mesh=mesh,
        in_specs=(
            P(("dp", "head"), None, None),
            P("section", None, None),
            P("section", None, None),
            P(None, None, "section"),
            P("section", None, None),
            P(),
            P(None, ("dp", "head"), None),
            P(None, None, None, ("dp", "head"), None),
            P(("dp", "head"), None, None),
            P(("dp", "head"), None, None, None),
        ),
        out_specs=(
            P("section", ("dp", "head"), None),
            P("section", ("dp", "head"), None),
            P(None, None, "section"),
            P("section", None, ("dp", "head")),
            P(None, ("dp", "head")),
        ),
        check_vma=False,
    )
```

```python
import functools
import math

import jax
import jax.numpy as jnp
import numpy as np
from jax import lax
from jax.experimental import pallas as pl
from jax.experimental.pallas import tpu as pltpu
from jax.sharding import PartitionSpec as P

GRID = 12
HALF = GRID // 2
SPAN = 4
POOLED = 7
BINS = POOLED * POOLED
PAIRS = (BINS + 1) // 2
CELLS = 256

EPS = 1e-06
GELU_C = math.sqrt(2.0 / math.pi)
BF = jnp.bfloat16
F32 = jnp.float32
STEP = 512
AHEAD = 3

NN = (((1,), (0,)), ((), ()))
NT = (((1,), (1,)), ((), ()))
TN = (((0,), (0,)), ((), ()))


def mm(left, right, dims=NN):
    return lax.dot_general(left, right, dims, preferred_element_type=F32)


def gelu_parts(values):
    inner_arg = GELU_C * (values + 0.044715 * values * values * values)
    tangent = jnp.tanh(inner_arg)
    result = 0.5 * values * (1.0 + tangent)
    slope = 0.5 * (1.0 + tangent) + 0.5 * values * (1.0 - tangent * tangent) * GELU_C * (
        1.0 + 3.0 * 0.044715 * values * values
    )
    return (result, slope)


def norm_parts(tokens):
    floats = tokens.astype(F32)
    centred = floats - jnp.mean(floats, axis=-1, keepdims=True)
    scale_inv = lax.rsqrt(jnp.mean(centred * centred, axis=-1, keepdims=True) + EPS)
    return (centred * scale_inv, scale_inv)


class Staged:
    def __init__(self, source, buffer, sems, chunk_axis):
        self.buffer = buffer
        self.shape = buffer.shape
        self.axis = chunk_axis
        self.copies = []
        self.waited = set()
        if chunk_axis is None:
            self.copies.append(pltpu.make_async_copy(source, buffer, sems.at[0]))
        else:
            for j in range(self.shape[chunk_axis] // STEP):
                at = self.part(j)
                self.copies.append(
                    pltpu.make_async_copy(source.at[at], buffer.at[at], sems.at[j])
                )

    def part(self, j):
        span = pl.ds(j * STEP, STEP)
        return (span, slice(None)) if self.axis == 0 else (slice(None), span)

    def start(self, j):
        if j < len(self.copies):
            self.copies[j].start()

    def wait(self, j):
        if j not in self.waited:
            self.waited.add(j)
            self.copies[j].wait()

    def chunk(self, j):
        self.wait(j)
        self.start(j + AHEAD)
        return self.buffer[self.part(j)]

    def __getitem__(self, index):
        self.wait(0)
        return self.buffer[index]

    def finish(self):
        for j in range(len(self.copies)):
            self.wait(j)


class Held(Staged):
    def __init__(self, buffer, chunk_axis):
        self.buffer = buffer
        self.shape = buffer.shape
        self.axis = chunk_axis
        self.copies = []

    def wait(self, j):
        pass


def load_body(*refs):
    count = (len(refs) - 1) // 2
    copies = [
        pltpu.make_async_copy(refs[i], refs[count + i], refs[-1].at[i]) for i in range(count)
    ]
    for copy in copies:
        copy.start()
    for copy in copies:
        copy.wait()


def loaded(name, *arrays):
    return pl.pallas_call(
        load_body,
        out_shape=[jax.ShapeDtypeStruct(a.shape, a.dtype) for a in arrays],
        in_specs=[pl.BlockSpec(memory_space=pl.ANY)] * len(arrays),
        out_specs=[pl.BlockSpec(memory_space=pl.ANY)] * len(arrays),
        scratch_shapes=[pltpu.SemaphoreType.DMA((len(arrays),))],
        compiler_params=pltpu.CompilerParams(vmem_limit_bytes=2 * 1024 * 1024),
        cost_estimate=pl.CostEstimate(
            flops=0, bytes_accessed=10**5, transcendentals=0
        ),
        name=name,
    )(*[in_hbm(a) for a in arrays])


def call(
    body,
    outs,
    args,
    name,
    scratch=(),
    scalars=0,
    chunks=None,
    flops=0,
    nbytes=0,
    vmem=18,
    ready=0,
):
    chunks = chunks or {}
    count = len(args) - scalars - ready
    axes = [chunks.get(i + scalars) for i in range(count)]
    last_axes = [chunks.get(i + scalars) for i in range(count, count + ready)]
    copied = args[scalars : scalars + count]
    sizes = [1 if axis is None else arg.shape[axis] // STEP for axis, arg in zip(axes, copied)]

    def kernel(*refs):
        given, sources = refs[:scalars], refs[scalars : scalars + count]
        kept = [Held(*parts) for parts in zip(refs[scalars + count : len(args)], last_axes)]
        results = refs[len(args) : len(args) + len(outs)]
        rest = refs[len(args) + len(outs) :]
        buffers, sems, extra = rest[:count], rest[count : 2 * count], rest[2 * count :]
        staged = [Staged(*parts) for parts in zip(sources, buffers, sems, axes)]
        for j in range(AHEAD):
            for item in staged:
                item.start(j)
        body(*given, *staged, *kept, *results, *extra)
        for item in staged:
            item.finish()

    return pl.pallas_call(
        kernel,
        out_shape=[jax.ShapeDtypeStruct(s, d) for s, d in outs],
        in_specs=[pl.BlockSpec(memory_space=pltpu.SMEM)] * scalars
        + [pl.BlockSpec(memory_space=pl.ANY)] * count
        + [pl.BlockSpec(memory_space=pltpu.VMEM)] * ready,
        out_specs=[pl.BlockSpec(memory_space=pltpu.VMEM) for _ in outs],
        scratch_shapes=[pltpu.VMEM(arg.shape, arg.dtype) for arg in copied]
        + [pltpu.SemaphoreType.DMA((size,)) for size in sizes]
        + list(scratch),
        compiler_params=pltpu.CompilerParams(vmem_limit_bytes=vmem * 1024 * 1024),
        cost_estimate=pl.CostEstimate(flops=flops, bytes_accessed=nbytes, transcendentals=0),
        name=name,
    )(*args)


def direct(
    body,
    outs,
    args,
    name,
    scratch=(),
    scalars=0,
    flops=0,
    nbytes=0,
    vmem=18,
    out_space=pltpu.VMEM,
):
    return pl.pallas_call(
        body,
        out_shape=[jax.ShapeDtypeStruct(s, d) for s, d in outs],
        in_specs=[pl.BlockSpec(memory_space=pltpu.SMEM)] * scalars
        + [pl.BlockSpec(memory_space=pltpu.VMEM)] * (len(args) - scalars),
        out_specs=[pl.BlockSpec(memory_space=out_space) for _ in outs],
        scratch_shapes=list(scratch),
        compiler_params=pltpu.CompilerParams(vmem_limit_bytes=vmem * 1024 * 1024),
        cost_estimate=pl.CostEstimate(flops=flops, bytes_accessed=nbytes, transcendentals=0),
        name=name,
    )(*args)


def in_hbm(array):
    return pltpu.with_memory_space_constraint(array, pltpu.HBM)


def ring(axis, shift):
    size = lax.axis_size(axis)
    return [(i, (i + shift) % size) for i in range(size)]


def shifted(value, axis, shift):
    return lax.ppermute(value, axis, ring(axis, shift))


def shifted_y(value, shift):
    return shifted(value, "dp", 2 * shift)


def core_swapped(value):
    return lax.ppermute(value, "dp", [(i, i ^ 1) for i in range(lax.axis_size("dp"))])


def gelu_quick(values):
    square = values * values
    half = 0.5 + 0.5 * jnp.tanh(values * (GELU_C + (GELU_C * 0.044715) * square))
    return half, square


def forward_body(tick, place_ref, *refs):
    if tick == 3:
        *refs, held_ref = refs
    if tick == 0:
        old_ref, w1_ref, w2_ref, *outs = refs
        tokens = old_ref[...]
    else:
        old_ref, new_ref, w1_ref, w2_ref, *outs = refs
        tokens = jnp.where(place_ref[0] == tick, new_ref[...], old_ref[...])
    result_ref = outs[0]
    if tick > 0:
        outs[1][...] = tokens
    normed = norm_parts(tokens)[0].astype(BF)
    if tick == 3:
        outs[2][...] = normed
    total = tokens.astype(F32)
    count = w1_ref.shape[1] // STEP
    values = mm(normed, w1_ref.chunk(0))
    for j in range(count):
        later = mm(normed, w1_ref.chunk(j + 1)) if j + 1 < count else None
        half, square = gelu_quick(values)
        activ = (values * half).astype(BF)
        if tick == 3:
            span = slice(j * STEP, (j + 1) * STEP)
            held_ref[:, span] = activ
            outs[3][:, span] = half + (values * (2.0 * half) * (1.0 - half)) * (
                GELU_C + (3.0 * 0.044715 * GELU_C) * square
            )
        total = total + mm(activ, w2_ref.chunk(j))
        values = later
    result_ref[...] = total.astype(BF)
    if tick == 3:
        put_pieces(place_ref[1], held_ref, outs[4:])


def put_pieces(place, held_ref, outs):
    columns = outs[0].shape[1]
    for d, ref in enumerate(outs):
        at = pl.multiple_of(lax.rem(place + d, 4) * columns, 128)
        ref[...] = held_ref[:, pl.ds(at, columns)]


def backward_body(tick, place_ref, *refs):
    if tick == 0:
        old_ref, slope_ref, tokens_ref, w1_ref, w2_ref, *outs = refs
        grad_out = old_ref[...]
    else:
        old_ref, new_ref, slope_ref, tokens_ref, w1_ref, w2_ref, *outs = refs
        grad_out = jnp.where(place_ref[0] == 3 - tick, new_ref[...], old_ref[...])
        outs[1][...] = grad_out
    total = jnp.zeros(grad_out.shape, F32)
    count = w1_ref.shape[1] // STEP
    grad_act = mm(grad_out, w2_ref.chunk(0), NT)
    for j in range(count):
        later = mm(grad_out, w2_ref.chunk(j + 1), NT) if j + 1 < count else None
        grad_pre = (grad_act * slope_ref.chunk(j)).astype(BF)
        total = total + mm(grad_pre, w1_ref.chunk(j), NT)
        grad_act = later
    normed, scale_inv = norm_parts(tokens_ref[...])
    grad_tok = scale_inv * (
        total
        - jnp.mean(total, axis=-1, keepdims=True)
        - normed * jnp.mean(total * normed, axis=-1, keepdims=True)
    )
    outs[0][...] = (grad_out.astype(F32) + grad_tok).astype(BF)


def last_backward_body(place_ref, grad_ref, slope_ref, w2_ref, *refs):
    *outs, held_ref = refs
    grad_out = grad_ref[...]
    count = w2_ref.shape[0] // STEP
    grad_act = mm(grad_out, w2_ref.chunk(0), NT)
    for j in range(count):
        later = mm(grad_out, w2_ref.chunk(j + 1), NT) if j + 1 < count else None
        held_ref[:, j * STEP : (j + 1) * STEP] = (grad_act * slope_ref.chunk(j)).astype(BF)
        grad_act = later
    put_pieces(place_ref[2], held_ref, outs)


def pick_body(place_ref, old_ref, new_ref, out_ref):
    out_ref[...] = jnp.where(place_ref[0] == 0, new_ref[...], old_ref[...])


def pyramid_body(top_ref, weight_ref, avg_ref, place_ref, levels_ref, pooled_ref):
    top = top_ref[...]
    pooled = mm(avg_ref[...], top).astype(BF)
    pooled_ref[...] = pooled
    weights = weight_ref[...]
    from_top = mm(weights, top, NT)
    from_pooled = mm(weights, pooled, NT)
    half = weights.shape[0] // 8
    for s in range(4):
        base = 2 * half * s
        one = from_pooled[base + half : base + 2 * half]
        zero = from_top[base : base + half] + one
        levels_ref[s] = (
            mm(zero.astype(BF), place_ref[0]) + mm(one.astype(BF), place_ref[1])
        ).astype(BF)


def top_grad_body(z0_ref, z1_ref, z2_ref, z3_ref, weight_ref, grad_ref, rows_ref):
    rows = jnp.concatenate([z0_ref[...], z1_ref[...], z2_ref[...], z3_ref[...]], axis=0)
    rows_ref[...] = rows
    grad_ref[...] = mm(rows, weight_ref[...], TN).astype(BF)


def crops_body(
    sec_ref, levels_ref, r0_ref, r1_ref, r2_ref, rows_ref, cols_ref, fc6_ref, part_ref, crops_ref
):
    is_last = sec_ref[0] == 3
    arrived = r0_ref[...] + r1_ref[...] + r2_ref[...]
    own = jnp.where(is_last, levels_ref[3], arrived)
    blank = jnp.zeros_like(own)
    both = jnp.concatenate(
        [jnp.concatenate([own, blank], axis=1), jnp.concatenate([blank, own], axis=1)], axis=0
    )

    def weights(b):
        if b >= BINS:
            return jnp.zeros((rows_ref.shape[1], CELLS), BF)
        return (rows_ref[b // POOLED] * cols_ref[b % POOLED]).astype(BF)

    for p in range(PAIRS):
        pair = jnp.concatenate([weights(2 * p), weights(2 * p + 1)], axis=1)
        crops_ref[:, 128 * p : 128 * (p + 1)] = mm(pair, both, NT).astype(BF)
    depth = fc6_ref.shape[0]
    whole = depth // 128 * 128
    part = mm(crops_ref[:, :whole], fc6_ref[:whole])
    part = part + mm(crops_ref[:, whole:depth], fc6_ref[whole:])
    part_ref[...] = part.astype(BF)


def head_body(
    sec_ref,
    p0_ref,
    p1_ref,
    p2_ref,
    p3_ref,
    cot_ref,
    fc7_ref,
    fc6_ref,
    rows_ref,
    cols_ref,
    spread_ref,
    first_ref,
    second_ref,
    grad_ref,
    maps_ref,
    parts_ref,
    back_ref,
):
    sec = sec_ref[0]
    for d, ref in enumerate((p0_ref, p1_ref, p2_ref, p3_ref)):
        parts_ref[lax.rem(sec + 4 - d, 4)] = ref[...].astype(F32)
    first_pre = parts_ref[0] + parts_ref[1] + parts_ref[2] + parts_ref[3]
    first_act, first_slope = gelu_parts(first_pre)
    first_b = first_act.astype(BF)
    first_ref[...] = first_b
    second_pre = mm(first_b, fc7_ref[...])
    second_slope = gelu_parts(second_pre)[1]
    grad_second = (cot_ref[...].astype(F32) * second_slope).astype(BF)
    second_ref[...] = grad_second
    grad_first = (mm(grad_second, fc7_ref[...], NT) * first_slope).astype(BF)
    grad_ref[...] = grad_first
    depth = fc6_ref.shape[0]
    back_ref[:depth] = mm(fc6_ref[...], grad_first, NT).astype(BF)
    back_ref[depth:] = jnp.zeros((back_ref.shape[0] - depth, back_ref.shape[1]), BF)
    channels = back_ref.shape[0] // (2 * PAIRS)

    def weights(b):
        if b >= BINS:
            return jnp.zeros((rows_ref.shape[1], CELLS), BF)
        return (rows_ref[b // POOLED] * cols_ref[b % POOLED]).astype(BF)

    total = jnp.zeros((channels, CELLS), F32)
    for p in range(PAIRS):
        lo = 2 * p * channels
        left = jnp.concatenate(
            [back_ref[lo : lo + channels], back_ref[lo + channels : lo + 2 * channels]], axis=1
        )
        right = jnp.concatenate([weights(2 * p), weights(2 * p + 1)], axis=0)
        total = total + mm(left, right)
    total_b = total.astype(BF)
    maps_ref[:channels] = mm(total_b, spread_ref[0]).astype(BF)
    maps_ref[channels:] = mm(total_b, spread_ref[1]).astype(BF)


def head_grads_body(grad_ref, crops_ref, second_ref, first_ref, out_ref, held_ref, sems):
    wide = crops_ref.shape[1]
    rows = out_ref.shape[0] // 4
    span_all = pl.ds(0, held_ref.shape[1])
    copies = []
    for j in range(4):
        at = pl.ds(j * rows, rows)
        span = slice(j * rows, (j + 1) * rows)
        held_ref[at, :wide] = mm(grad_ref[:, span], crops_ref[...], TN).astype(BF)
        held_ref[at, wide:] = mm(second_ref[:, span], first_ref[...], TN).astype(BF)
        copies.append(
            pltpu.make_async_copy(held_ref.at[at], out_ref.at[at, span_all], sems.at[j])
        )
        copies[-1].start()
    for copy in copies:
        copy.wait()


def map_grads_body(maps_ref, order_ref, top_ref, pooled_ref, _, out_ref, held_ref, sems):
    ordered = mm(order_ref[...], maps_ref[...]).astype(BF)
    half = ordered.shape[0] // 2
    width = held_ref.shape[1]
    span = pl.ds(out_ref.shape[1] - width, width)
    copies = []
    for j, cells in enumerate((top_ref, pooled_ref)):
        at = pl.ds(j * half, half)
        held_ref[at] = mm(ordered[j * half : (j + 1) * half], cells[...]).astype(BF)
        copies.append(pltpu.make_async_copy(held_ref.at[at], out_ref.at[at, span], sems.at[j]))
        copies[-1].start()
    for copy in copies:
        copy.wait()


def first_grad_body(
    core_ref, a0_ref, a1_ref, a2_ref, a3_ref, g0_ref, g1_ref, g2_ref, g3_ref, mine_ref, other_ref
):
    is_zero = core_ref[3] == 0
    lefts = (a0_ref, a1_ref, a2_ref, a3_ref)
    rights = (g0_ref, g1_ref, g2_ref, g3_ref)
    total = mm(lefts[0][...], rights[0][...], TN)
    for d in range(1, 4):
        total = total + mm(lefts[d][...], rights[d][...], TN)
    rows = mine_ref.shape[1]
    for y in range(4):
        low = total[2 * y * rows : (2 * y + 1) * rows]
        high = total[(2 * y + 1) * rows : (2 * y + 2) * rows]
        mine_ref[y] = jnp.where(is_zero, low, high).astype(BF)
        other_ref[y] = jnp.where(is_zero, high, low).astype(BF)


def second_grad_body(
    core_ref, a0_ref, a1_ref, a2_ref, a3_ref, g0_ref, g1_ref, g2_ref, g3_ref, mine_ref, other_ref
):
    is_zero = core_ref[3] == 0
    lefts = (a0_ref, a1_ref, a2_ref, a3_ref)
    rights = (g0_ref, g1_ref, g2_ref, g3_ref)
    total = mm(lefts[0][...], rights[0][...], TN)
    for d in range(1, 4):
        total = total + mm(lefts[d][...], rights[d][...], TN)
    rows = mine_ref.shape[1]
    for z in range(4):
        low = total[z * rows : (z + 1) * rows]
        high = total[(z + 4) * rows : (z + 5) * rows]
        mine_ref[z] = jnp.where(is_zero, low, high).astype(BF)
        other_ref[z] = jnp.where(is_zero, high, low).astype(BF)


def pair_body(which, place_ref, mine_ref, got_ref, kept_ref, one_ref, two_ref, three_ref):
    place = place_ref[which]

    def total(d):
        at = lax.rem(place + d, 4)
        return mine_ref[at].astype(F32) + got_ref[at].astype(F32)

    kept_ref[...] = total(0)
    for d, ref in enumerate((one_ref, two_ref, three_ref)):
        ref[...] = total(d + 1).astype(BF)


def strips_body(
    place_ref, kept_ref, g1_ref, g2_ref, g3_ref, own_ref, one_ref, two_ref, three_ref
):
    total = kept_ref[...]
    for ref in (g1_ref, g2_ref, g3_ref):
        total = total + ref[...].astype(F32)
    rows = own_ref.shape[0]
    strips = [total[j * rows : (j + 1) * rows] for j in range(4)]
    for d, ref in enumerate((own_ref, one_ref, two_ref, three_ref)):
        at = lax.rem(place_ref[2] + d, 4)
        picked = strips[3]
        for j in range(3):
            picked = jnp.where(at == j, strips[j], picked)
        ref[...] = picked.astype(ref.dtype)


def join_body(place_ref, own_ref, g1_ref, g2_ref, g3_ref, out_ref):
    columns = own_ref.shape[1]
    for d, ref in enumerate((own_ref, g1_ref, g2_ref, g3_ref)):
        at = pl.multiple_of(lax.rem(place_ref[2] + 4 - d, 4) * columns, 128)
        out_ref[:, pl.ds(at, columns)] = ref[...].astype(F32)


def cell_tables():
    index = np.arange(CELLS)
    zero = index < GRID * GRID
    one = (index >= GRID * GRID) & (index < GRID * GRID + HALF * HALF)
    inner = index - GRID * GRID
    row = np.where(zero, index // GRID, np.where(one, inner // HALF, -9))
    col = np.where(zero, index % GRID, np.where(one, inner % HALF, -9))
    return zero, one, row.astype(np.int32), col.astype(np.int32)


def grid_constants():
    cells = np.arange(GRID * GRID)
    block = (cells // GRID // 2) * HALF + (cells % GRID) // 2
    average = 0.25 * (block[:, None] == block[None, :])
    place = np.zeros((2, GRID * GRID, CELLS))
    place[0, cells, cells] = 1.0
    for b in range(HALF * HALF):
        place[1, np.where(block == b)[0][0], GRID * GRID + b] = 1.0
    spread = np.zeros((2, CELLS, GRID * GRID))
    spread[0, cells, cells] = 1.0
    spread[1, GRID * GRID + block, cells] = 0.25
    return average, place, spread


def tables_body(boxes_ref, weights_ref, cells_ref, fwd_ref, bwd_ref, cols_ref):
    row, col = cells_ref[0:1], cells_ref[1:2]
    zero, one = cells_ref[2:3] > 0, cells_ref[3:4] > 0
    box_zero = boxes_ref[:, 0:1] == 0
    forward = (box_zero & zero) | (~box_zero & one)
    backward = forward | (box_zero & one)
    halved = box_zero & one
    at_rows, at_cols = [], []
    for u in range(SPAN):
        at_y = boxes_ref[:, 1:2] + u
        at_x = boxes_ref[:, 2:3] + u
        at_rows.append(row == jnp.where(halved, at_y // 2, at_y))
        at_cols.append(col == jnp.where(halved, at_x // 2, at_x))
    for i in range(POOLED):
        rows = jnp.zeros(fwd_ref.shape[1:], F32)
        cols = jnp.zeros(fwd_ref.shape[1:], F32)
        for u in range(SPAN):
            y_at, x_at = SPAN * i + u, SPAN * (POOLED + i) + u
            rows = rows + jnp.where(at_rows[u], weights_ref[:, y_at : y_at + 1], 0.0)
            cols = cols + jnp.where(at_cols[u], weights_ref[:, x_at : x_at + 1], 0.0)
        fwd_ref[i] = jnp.where(forward, rows, 0.0)
        bwd_ref[i] = jnp.where(backward, rows, 0.0)
        cols_ref[i] = cols


def sampling_tables(windows, bilinear):
    zero, one, row, col = cell_tables()
    boxes = windows.shape[2]
    cells = np.stack([row, col, zero.astype(np.int32), one.astype(np.int32)] + [row] * 4)
    weights = jnp.transpose(bilinear.reshape(2 * POOLED * SPAN, boxes))
    corners = jnp.transpose(windows.reshape(3, boxes))
    return direct(
        tables_body,
        [((POOLED, boxes, CELLS), F32)] * 3,
        (corners, weights, jnp.asarray(cells, jnp.int32)),
        "tables",
        nbytes=4 * 10**6,
    )


def slot_rows(owner_ids, arrived):
    boxes = owner_ids.shape[0]
    index = jnp.arange(boxes)
    same = (owner_ids[:, None] == owner_ids[None, :]) & (index[None, :] < index[:, None])
    rank = jnp.sum(same.astype(jnp.int32), axis=1)
    slots = arrived.shape[1]
    flat = arrived.reshape(-1, arrived.shape[2])
    pick = (owner_ids * slots + rank)[:, None] == jnp.arange(flat.shape[0])[None, :]
    return mm(pick.astype(BF), flat).astype(BF)


def per_device(
    images, w_in, w_out, fpn_weight, fc6_weight, fc7_weight, windows, bilinear, owners, cotangent
):
    section = lax.axis_index("section")
    dp = lax.axis_index("dp")
    z_here = lax.axis_index("head")
    y_here = dp // 2
    core = dp % 2
    w_first = w_in[0]
    w_second = w_out[0]
    width = images.shape[2]
    inner = w_first.shape[1]
    channels = fc6_weight.shape[0]
    units = fc6_weight.shape[2]
    places = jnp.stack([section, y_here, z_here, core]).astype(jnp.int32)
    average, place, spread = grid_constants()
    average = jnp.asarray(average, BF)
    place = jnp.asarray(place, BF)
    spread = jnp.asarray(spread, BF)

    fpn_rows = jnp.transpose(fpn_weight, (0, 2, 1)).reshape(2 * channels, width)
    fpn_all = lax.all_gather(fpn_rows, "section", axis=0, tiled=True)
    fc6_rows = jnp.transpose(fc6_weight, (1, 0, 2)).reshape(BINS * channels, units)
    tokens = images[0]
    shape = tokens.shape
    wide_shape = (shape[0], inner)
    incoming = None
    weights = (in_hbm(w_first), in_hbm(w_second))
    for tick in range(4):
        outs = [(shape, BF)]
        if tick > 0:
            outs.append((shape, BF))
        if tick == 3:
            outs += [(shape, BF), (wide_shape, F32)] + [((shape[0], inner // 4), BF)] * 4
        inputs = (tokens,) if tick == 0 else (tokens, incoming)
        results = call(
            functools.partial(forward_body, tick),
            outs,
            (places, *inputs, *weights),
            f"block_forward_{tick}",
            ready=2 if tick > 1 else 0,
            scalars=1,
            chunks={1 + len(inputs): 1, 2 + len(inputs): 0},
            scratch=(pltpu.VMEM(wide_shape, BF),) if tick == 3 else (),
            vmem=28 if tick < 2 else 14,
            flops=3 * 10**9,
            nbytes=18 * 10**6,
        )
        result = results[0]
        if tick > 0:
            tokens = results[1]
        if tick == 3:
            normed_b, slope, *act_pieces = results[2:]
            break
        if tick == 0:
            cotangent, result = lax.optimization_barrier((cotangent, result))
            padded = jnp.pad(cotangent[0], ((0, 0), (0, 2), (0, 0)))
            cot_arrived = lax.all_to_all(
                padded, ("dp", "head"), split_axis=0, concat_axis=0, tiled=True
            )
        incoming = lax.ppermute(result, "section", [(tick, tick + 1)])
        if tick == 0:
            windows, bilinear, result = lax.optimization_barrier((windows, bilinear, result))
            rows_fwd, rows_bwd, cols_all = sampling_tables(windows, bilinear)
            held = (incoming, rows_fwd, rows_bwd, cols_all)
            incoming, rows_fwd, rows_bwd, cols_all = lax.optimization_barrier(held)
        if tick == 1:
            owner_ids, result = lax.optimization_barrier((owners[0, :, 0], result))
            cot_rows = slot_rows(owner_ids, cot_arrived)
            held = (cot_rows, fpn_all, w_first, w_second)
            cot_rows, fpn_all, w_first, w_second = lax.optimization_barrier(held)
            weights = loaded("weights_1", w_first, w_second)
            held = (incoming, cot_rows, weights)
            incoming, cot_rows, weights = lax.optimization_barrier(held)
        if tick == 2:
            w_first, w_second, result = lax.optimization_barrier((w_first, w_second, result))
            weights = loaded("weights_2", w_first, w_second)
            incoming, weights = lax.optimization_barrier((incoming, weights))
    top = result

    levels, pooled = direct(
        pyramid_body,
        [((4, channels, CELLS), BF), (top.shape, BF)],
        (top, fpn_all, average, place),
        "pyramid",
        flops=10**9,
        nbytes=3 * 10**6,
    )
    sent = [lax.ppermute(levels[s], "section", [(3, s)]) for s in range(3)]
    boxes = windows.shape[2]
    part, crops = direct(
        crops_body,
        [((boxes, units), BF), ((boxes, 2 * PAIRS * channels), BF)],
        (places, levels, *sent, rows_fwd, cols_all, fc6_rows),
        "crops",
        scalars=1,
        flops=10**9,
        nbytes=6 * 10**6,
    )
    parts = [part] + [shifted(part, "section", d) for d in (1, 2, 3)]
    first_b, grad_second, grad_first, maps = direct(
        head_body,
        [((boxes, units), BF)] * 3 + [((2 * channels, GRID * GRID), BF)],
        (
            places,
            *parts,
            cot_rows,
            fc7_weight,
            fc6_rows,
            rows_bwd,
            cols_all,
            spread,
        ),
        "head",
        scratch=(
            pltpu.VMEM((4, boxes, units), F32),
            pltpu.VMEM((2 * PAIRS * channels, boxes), BF),
        ),
        scalars=1,
        flops=10**9,
        nbytes=6 * 10**6,
    )
    returned = [lax.ppermute(maps, "section", [(s, 3)]) for s in range(3)]
    stack_shape = (units, crops.shape[1] + units + width)
    (stacked,) = direct(
        head_grads_body,
        [(stack_shape, BF)],
        (grad_first, crops, grad_second, first_b),
        "head_grads",
        scratch=(
            pltpu.VMEM((units, crops.shape[1] + units), BF),
            pltpu.SemaphoreType.DMA((4,)),
        ),
        flops=10**9,
        nbytes=6 * 10**6,
        out_space=pl.ANY,
    )
    returned, stacked = lax.optimization_barrier((returned, stacked))
    grad_out, map_rows = direct(
        top_grad_body,
        [(top.shape, BF), ((8 * channels, GRID * GRID), BF)],
        (*returned, maps, fpn_all),
        "top_grad",
        flops=10**9,
        nbytes=3 * 10**6,
    )

    quarter = inner // 4

    incoming = None
    weights = (in_hbm(w_first), in_hbm(w_second))
    for tick in range(3):
        outs = [(shape, BF)]
        if tick > 0:
            outs.append((shape, BF))
        inputs = (grad_out,) if tick == 0 else (grad_out, incoming)
        results = call(
            functools.partial(backward_body, tick),
            outs,
            (places, *inputs, slope, tokens, *weights),
            f"block_backward_{tick}",
            ready=2 if tick > 0 else 0,
            scalars=1,
            chunks={1 + len(inputs): 1, 3 + len(inputs): 1, 4 + len(inputs): 0},
            vmem=28 if tick < 1 else 14,
            flops=3 * 10**9,
            nbytes=18 * 10**6,
        )
        grad_in = results[0]
        if tick > 0:
            grad_out = results[1]
        if tick == 0:
            held = (grad_in, map_rows, act_pieces)
            grad_in, map_rows, act_pieces = lax.optimization_barrier(held)
            incoming = lax.ppermute(grad_in, "section", [(3, 2)])
            act_parts = [act_pieces[0]] + [shifted_y(act_pieces[d], d) for d in (1, 2, 3)]
            order = np.zeros((8 * channels, 8 * channels))
            for r in range(8 * channels):
                order[r, ((r % 16) // 4) * 2 * channels + (r // 16) * 4 + r % 4] = 1.0
            stacked = pl.pallas_call(
                map_grads_body,
                out_shape=jax.ShapeDtypeStruct(stack_shape, BF),
                in_specs=[pl.BlockSpec(memory_space=pltpu.VMEM)] * 4
                + [pl.BlockSpec(memory_space=pl.ANY)],
                out_specs=pl.BlockSpec(memory_space=pl.ANY),
                scratch_shapes=[
                    pltpu.VMEM((8 * channels, width), BF),
                    pltpu.SemaphoreType.DMA((2,)),
                ],
                input_output_aliases={4: 0},
                compiler_params=pltpu.CompilerParams(vmem_limit_bytes=18 * 1024 * 1024),
                cost_estimate=pl.CostEstimate(
                    flops=10**9, bytes_accessed=4 * 10**6, transcendentals=0
                ),
                name="map_grads",
            )(map_rows, jnp.asarray(order, BF), top, pooled, in_hbm(stacked))
            stacked = lax.psum_scatter(stacked, "dp", scatter_dimension=0, tiled=True)
            w_first, w_second, grad_in = lax.optimization_barrier((w_first, w_second, grad_in))
            weights = loaded("weights_3", w_first, w_second)
            incoming, weights = lax.optimization_barrier((incoming, weights))
        elif tick == 1:
            incoming = lax.ppermute(grad_in, "section", [(2, 1)])
            w_first, w_second, grad_in = lax.optimization_barrier((w_first, w_second, grad_in))
            weights = loaded("weights_4", w_first, w_second)
            held = (incoming, act_parts, weights)
            incoming, act_parts, weights = lax.optimization_barrier(held)
        else:
            grad_in, normed_b = lax.optimization_barrier((grad_in, normed_b))
            incoming = lax.ppermute(grad_in, "section", [(1, 0)])
            normed_parts = [normed_b] + [shifted(normed_b, "head", d) for d in (1, 2, 3)]
    (grad_out,) = direct(
        pick_body, [(shape, BF)], (places, grad_out, incoming), "pick", scalars=1, nbytes=10**6
    )

    out_parts = [grad_out] + [shifted_y(grad_out, d) for d in (1, 2, 3)]
    pre_pieces = call(
        last_backward_body,
        [((shape[0], quarter), BF)] * 4,
        (places, grad_out, slope, in_hbm(w_second)),
        "block_backward_3",
        scalars=1,
        chunks={2: 1, 3: 0},
        scratch=(pltpu.VMEM(wide_shape, BF),),
        flops=2 * 10**9,
        nbytes=10 * 10**6,
    )
    held = (pre_pieces, out_parts, normed_parts, stacked)
    pre_pieces, out_parts, normed_parts, stacked = lax.optimization_barrier(held)
    stacked = lax.psum_scatter(stacked, "head", scatter_dimension=0, tiled=True)
    pre_parts = [pre_pieces[0]] + [shifted(pre_pieces[d], "head", d) for d in (1, 2, 3)]
    rows_in = width // 8
    rows_out = quarter // 8
    mine_first, other_first = direct(
        first_grad_body,
        [((4, rows_in, quarter), BF)] * 2,
        (places, *normed_parts, *pre_parts),
        "first_grad",
        vmem=24,
        scalars=1,
        flops=2 * 10**9,
        nbytes=5 * 10**6,
    )
    mine_second, other_second = direct(
        second_grad_body,
        [((4, rows_out, width), BF)] * 2,
        (places, *act_parts, *out_parts),
        "second_grad",
        vmem=24,
        scalars=1,
        flops=2 * 10**9,
        nbytes=5 * 10**6,
    )
    swapped_first = core_swapped(other_first)
    swapped_second = core_swapped(other_second)

    def pair_sums(which, mine, swapped, name):
        return direct(
            functools.partial(pair_body, which),
            [(mine.shape[1:], F32)] + [(mine.shape[1:], BF)] * 3,
            (places, mine, swapped),
            name,
            scalars=1,
            nbytes=5 * 10**6,
        )

    kept_first, *out_first = pair_sums(1, mine_first, swapped_first, "pair_first")
    grad_w_out, *out_second = pair_sums(2, mine_second, swapped_second, "pair_second")
    out_second, stacked = lax.optimization_barrier((out_second, stacked))
    wide = crops.shape[1]
    fpn_part = stacked[:, wide + units :].reshape(4, 4, width)
    fpn_got = [lax.ppermute(fpn_part[s], "section", [(3, s)]) for s in range(3)]
    got_first = [shifted_y(out_first[d - 1], d) for d in (1, 2, 3)]
    got_second = [shifted(out_second[d - 1], "head", d) for d in (1, 2, 3)]
    own = jnp.where(section == 3, fpn_part[3], fpn_got[0] + fpn_got[1] + fpn_got[2])
    fpn_rows = lax.all_to_all(
        jnp.broadcast_to(own[None], (32,) + own.shape),
        ("dp", "head"),
        split_axis=0,
        concat_axis=0,
        tiled=True,
    )
    last_rows = rows_in // 4
    got_first, stacked = lax.optimization_barrier((got_first, stacked))
    kept_strip, *out_strips = direct(
        strips_body,
        [((last_rows, quarter), F32)] + [((last_rows, quarter), BF)] * 3,
        (places, kept_first, *got_first),
        "strips",
        scalars=1,
        nbytes=3 * 10**6,
    )
    strips = [shifted(out_strips[d - 1], "head", d) for d in (1, 2, 3)]
    for got in got_second:
        grad_w_out = grad_w_out + got.astype(F32)
    (grad_w_in,) = direct(
        join_body,
        [((last_rows, inner), F32)],
        (places, kept_strip, *strips),
        "join",
        scalars=1,
        nbytes=10**6,
    )

    fc6_part = stacked[:, :wide].reshape(-1, 2 * PAIRS, channels)[:, :BINS]
    fc6_out = jnp.transpose(fc6_part.astype(F32), (2, 1, 0))
    fc7_out = jnp.transpose(stacked[:, wide : wide + units].astype(F32))
    fpn_out = fpn_rows.astype(F32)
    fpn_out = jnp.transpose(fpn_out.reshape(2, channels, width), (0, 2, 1))
    return (grad_w_in[None], grad_w_out[None], fpn_out, fc6_out, fc7_out)


def solution(mesh):
    return jax.shard_map(
        per_device,
        mesh=mesh,
        in_specs=(
            P(("dp", "head"), None, None),
            P("section", None, None),
            P("section", None, None),
            P(None, None, "section"),
            P("section", None, None),
            P(),
            P(None, ("dp", "head"), None),
            P(None, None, None, ("dp", "head"), None),
            P(("dp", "head"), None, None),
            P(("dp", "head"), None, None, None),
        ),
        out_specs=(
            P("section", ("dp", "head"), None),
            P("section", ("dp", "head"), None),
            P(None, None, "section"),
            P("section", None, ("dp", "head")),
            P(None, ("dp", "head")),
        ),
        check_vma=False,
    )
```

```python
import functools
import math

import jax
import jax.numpy as jnp
import numpy as np
from jax import lax
from jax.experimental import pallas as pl
from jax.experimental.pallas import tpu as pltpu
from jax.sharding import PartitionSpec as P

GRID = 12
HALF = GRID // 2
SPAN = 4
POOLED = 7
BINS = POOLED * POOLED
PAIRS = (BINS + 1) // 2
CELLS = 256

EPS = 1e-06
GELU_C = math.sqrt(2.0 / math.pi)
BF = jnp.bfloat16
F32 = jnp.float32
STEP = 512
AHEAD = 3

NN = (((1,), (0,)), ((), ()))
NT = (((1,), (1,)), ((), ()))
TN = (((0,), (0,)), ((), ()))


def mm(left, right, dims=NN):
    return lax.dot_general(left, right, dims, preferred_element_type=F32)


def gelu_parts(values):
    inner_arg = GELU_C * (values + 0.044715 * values * values * values)
    tangent = jnp.tanh(inner_arg)
    result = 0.5 * values * (1.0 + tangent)
    slope = 0.5 * (1.0 + tangent) + 0.5 * values * (1.0 - tangent * tangent) * GELU_C * (
        1.0 + 3.0 * 0.044715 * values * values
    )
    return (result, slope)


def norm_parts(tokens):
    floats = tokens.astype(F32)
    centred = floats - jnp.mean(floats, axis=-1, keepdims=True)
    scale_inv = lax.rsqrt(jnp.mean(centred * centred, axis=-1, keepdims=True) + EPS)
    return (centred * scale_inv, scale_inv)


class Staged:
    def __init__(self, source, buffer, sems, chunk_axis):
        self.buffer = buffer
        self.shape = buffer.shape
        self.axis = chunk_axis
        self.copies = []
        self.waited = set()
        if chunk_axis is None:
            self.copies.append(pltpu.make_async_copy(source, buffer, sems.at[0]))
        else:
            for j in range(self.shape[chunk_axis] // STEP):
                at = self.part(j)
                self.copies.append(
                    pltpu.make_async_copy(source.at[at], buffer.at[at], sems.at[j])
                )

    def part(self, j):
        span = pl.ds(j * STEP, STEP)
        return (span, slice(None)) if self.axis == 0 else (slice(None), span)

    def start(self, j):
        if j < len(self.copies):
            self.copies[j].start()

    def wait(self, j):
        if j not in self.waited:
            self.waited.add(j)
            self.copies[j].wait()

    def chunk(self, j):
        self.wait(j)
        self.start(j + AHEAD)
        return self.buffer[self.part(j)]

    def __getitem__(self, index):
        self.wait(0)
        return self.buffer[index]

    def finish(self):
        for j in range(len(self.copies)):
            self.wait(j)


class Held(Staged):
    def __init__(self, buffer, chunk_axis):
        self.buffer = buffer
        self.shape = buffer.shape
        self.axis = chunk_axis
        self.copies = []

    def wait(self, j):
        pass


def load_body(*refs):
    count = (len(refs) - 1) // 2
    copies = [
        pltpu.make_async_copy(refs[i], refs[count + i], refs[-1].at[i]) for i in range(count)
    ]
    for copy in copies:
        copy.start()
    for copy in copies:
        copy.wait()


def loaded(name, *arrays):
    return pl.pallas_call(
        load_body,
        out_shape=[jax.ShapeDtypeStruct(a.shape, a.dtype) for a in arrays],
        in_specs=[pl.BlockSpec(memory_space=pl.ANY)] * len(arrays),
        out_specs=[pl.BlockSpec(memory_space=pl.ANY)] * len(arrays),
        scratch_shapes=[pltpu.SemaphoreType.DMA((len(arrays),))],
        compiler_params=pltpu.CompilerParams(vmem_limit_bytes=2 * 1024 * 1024),
        cost_estimate=pl.CostEstimate(
            flops=0, bytes_accessed=10**5, transcendentals=0
        ),
        name=name,
    )(*[in_hbm(a) for a in arrays])


def call(
    body,
    outs,
    args,
    name,
    scratch=(),
    scalars=0,
    chunks=None,
    flops=0,
    nbytes=0,
    vmem=18,
    ready=0,
):
    chunks = chunks or {}
    count = len(args) - scalars - ready
    axes = [chunks.get(i + scalars) for i in range(count)]
    last_axes = [chunks.get(i + scalars) for i in range(count, count + ready)]
    copied = args[scalars : scalars + count]
    sizes = [1 if axis is None else arg.shape[axis] // STEP for axis, arg in zip(axes, copied)]

    def kernel(*refs):
        given, sources = refs[:scalars], refs[scalars : scalars + count]
        kept = [Held(*parts) for parts in zip(refs[scalars + count : len(args)], last_axes)]
        results = refs[len(args) : len(args) + len(outs)]
        rest = refs[len(args) + len(outs) :]
        buffers, sems, extra = rest[:count], rest[count : 2 * count], rest[2 * count :]
        staged = [Staged(*parts) for parts in zip(sources, buffers, sems, axes)]
        for j in range(AHEAD):
            for item in staged:
                item.start(j)
        body(*given, *staged, *kept, *results, *extra)
        for item in staged:
            item.finish()

    return pl.pallas_call(
        kernel,
        out_shape=[jax.ShapeDtypeStruct(s, d) for s, d in outs],
        in_specs=[pl.BlockSpec(memory_space=pltpu.SMEM)] * scalars
        + [pl.BlockSpec(memory_space=pl.ANY)] * count
        + [pl.BlockSpec(memory_space=pltpu.VMEM)] * ready,
        out_specs=[pl.BlockSpec(memory_space=pltpu.VMEM) for _ in outs],
        scratch_shapes=[pltpu.VMEM(arg.shape, arg.dtype) for arg in copied]
        + [pltpu.SemaphoreType.DMA((size,)) for size in sizes]
        + list(scratch),
        compiler_params=pltpu.CompilerParams(vmem_limit_bytes=vmem * 1024 * 1024),
        cost_estimate=pl.CostEstimate(flops=flops, bytes_accessed=nbytes, transcendentals=0),
        name=name,
    )(*args)


def direct(
    body,
    outs,
    args,
    name,
    scratch=(),
    scalars=0,
    flops=0,
    nbytes=0,
    vmem=18,
    out_space=pltpu.VMEM,
):
    return pl.pallas_call(
        body,
        out_shape=[jax.ShapeDtypeStruct(s, d) for s, d in outs],
        in_specs=[pl.BlockSpec(memory_space=pltpu.SMEM)] * scalars
        + [pl.BlockSpec(memory_space=pltpu.VMEM)] * (len(args) - scalars),
        out_specs=[pl.BlockSpec(memory_space=out_space) for _ in outs],
        scratch_shapes=list(scratch),
        compiler_params=pltpu.CompilerParams(vmem_limit_bytes=vmem * 1024 * 1024),
        cost_estimate=pl.CostEstimate(flops=flops, bytes_accessed=nbytes, transcendentals=0),
        name=name,
    )(*args)


def in_hbm(array):
    return pltpu.with_memory_space_constraint(array, pltpu.HBM)


def ring(axis, shift):
    size = lax.axis_size(axis)
    return [(i, (i + shift) % size) for i in range(size)]


def shifted(value, axis, shift):
    return lax.ppermute(value, axis, ring(axis, shift))


def shifted_y(value, shift):
    return shifted(value, "dp", 2 * shift)


def core_swapped(value):
    return lax.ppermute(value, "dp", [(i, i ^ 1) for i in range(lax.axis_size("dp"))])


def gelu_quick(values):
    square = values * values
    half = 0.5 + 0.5 * jnp.tanh(values * (GELU_C + (GELU_C * 0.044715) * square))
    return half, square


def forward_body(tick, place_ref, *refs):
    if tick == 3:
        *refs, held_ref = refs
    if tick == 0:
        old_ref, w1_ref, w2_ref, *outs = refs
        tokens = old_ref[...]
    else:
        old_ref, new_ref, w1_ref, w2_ref, *outs = refs
        tokens = jnp.where(place_ref[0] == tick, new_ref[...], old_ref[...])
    result_ref = outs[0]
    if tick > 0:
        outs[1][...] = tokens
    normed = norm_parts(tokens)[0].astype(BF)
    if tick == 3:
        outs[2][...] = normed
    total = tokens.astype(F32)
    count = w1_ref.shape[1] // STEP
    values = mm(normed, w1_ref.chunk(0))
    for j in range(count):
        later = mm(normed, w1_ref.chunk(j + 1)) if j + 1 < count else None
        half, square = gelu_quick(values)
        activ = (values * half).astype(BF)
        if tick == 3:
            span = slice(j * STEP, (j + 1) * STEP)
            held_ref[:, span] = activ
            outs[3][:, span] = half + (values * (2.0 * half) * (1.0 - half)) * (
                GELU_C + (3.0 * 0.044715 * GELU_C) * square
            )
        total = total + mm(activ, w2_ref.chunk(j))
        values = later
    result_ref[...] = total.astype(BF)
    if tick == 3:
        put_pieces(place_ref[1], held_ref, outs[4:])


def put_pieces(place, held_ref, outs):
    columns = outs[0].shape[1]
    for d, ref in enumerate(outs):
        at = pl.multiple_of(lax.rem(place + d, 4) * columns, 128)
        ref[...] = held_ref[:, pl.ds(at, columns)]


def backward_body(tick, place_ref, *refs):
    if tick == 0:
        old_ref, slope_ref, tokens_ref, w1_ref, w2_ref, *outs = refs
        grad_out = old_ref[...]
    else:
        old_ref, new_ref, slope_ref, tokens_ref, w1_ref, w2_ref, *outs = refs
        grad_out = jnp.where(place_ref[0] == 3 - tick, new_ref[...], old_ref[...])
        outs[1][...] = grad_out
    total = jnp.zeros(grad_out.shape, F32)
    count = w1_ref.shape[1] // STEP
    grad_act = mm(grad_out, w2_ref.chunk(0), NT)
    for j in range(count):
        later = mm(grad_out, w2_ref.chunk(j + 1), NT) if j + 1 < count else None
        grad_pre = (grad_act * slope_ref.chunk(j)).astype(BF)
        total = total + mm(grad_pre, w1_ref.chunk(j), NT)
        grad_act = later
    normed, scale_inv = norm_parts(tokens_ref[...])
    grad_tok = scale_inv * (
        total
        - jnp.mean(total, axis=-1, keepdims=True)
        - normed * jnp.mean(total * normed, axis=-1, keepdims=True)
    )
    outs[0][...] = (grad_out.astype(F32) + grad_tok).astype(BF)


def last_backward_body(place_ref, grad_ref, slope_ref, w2_ref, *refs):
    *outs, held_ref = refs
    grad_out = grad_ref[...]
    count = w2_ref.shape[0] // STEP
    grad_act = mm(grad_out, w2_ref.chunk(0), NT)
    for j in range(count):
        later = mm(grad_out, w2_ref.chunk(j + 1), NT) if j + 1 < count else None
        held_ref[:, j * STEP : (j + 1) * STEP] = (grad_act * slope_ref.chunk(j)).astype(BF)
        grad_act = later
    put_pieces(place_ref[2], held_ref, outs)


def pick_body(place_ref, old_ref, new_ref, out_ref):
    out_ref[...] = jnp.where(place_ref[0] == 0, new_ref[...], old_ref[...])


def pyramid_body(top_ref, weight_ref, avg_ref, place_ref, levels_ref, pooled_ref):
    top = top_ref[...]
    pooled = mm(avg_ref[...], top).astype(BF)
    pooled_ref[...] = pooled
    weights = weight_ref[...]
    from_top = mm(weights, top, NT)
    from_pooled = mm(weights, pooled, NT)
    half = weights.shape[0] // 8
    for s in range(4):
        base = 2 * half * s
        one = from_pooled[base + half : base + 2 * half]
        zero = from_top[base : base + half] + one
        levels_ref[s] = (
            mm(zero.astype(BF), place_ref[0]) + mm(one.astype(BF), place_ref[1])
        ).astype(BF)


def top_grad_body(z0_ref, z1_ref, z2_ref, z3_ref, weight_ref, grad_ref, rows_ref):
    rows = jnp.concatenate([z0_ref[...], z1_ref[...], z2_ref[...], z3_ref[...]], axis=0)
    rows_ref[...] = rows
    grad_ref[...] = mm(rows, weight_ref[...], TN).astype(BF)


def crops_body(
    sec_ref, levels_ref, r0_ref, r1_ref, r2_ref, rows_ref, cols_ref, fc6_ref, part_ref, crops_ref
):
    is_last = sec_ref[0] == 3
    arrived = r0_ref[...] + r1_ref[...] + r2_ref[...]
    own = jnp.where(is_last, levels_ref[3], arrived)
    blank = jnp.zeros_like(own)
    both = jnp.concatenate(
        [jnp.concatenate([own, blank], axis=1), jnp.concatenate([blank, own], axis=1)], axis=0
    )

    def weights(b):
        if b >= BINS:
            return jnp.zeros((rows_ref.shape[1], CELLS), BF)
        return (rows_ref[b // POOLED] * cols_ref[b % POOLED]).astype(BF)

    for p in range(PAIRS):
        pair = jnp.concatenate([weights(2 * p), weights(2 * p + 1)], axis=1)
        crops_ref[:, 128 * p : 128 * (p + 1)] = mm(pair, both, NT).astype(BF)
    depth = fc6_ref.shape[0]
    whole = depth // 128 * 128
    part = mm(crops_ref[:, :whole], fc6_ref[:whole])
    part = part + mm(crops_ref[:, whole:depth], fc6_ref[whole:])
    part_ref[...] = part.astype(BF)


def head_body(
    sec_ref,
    p0_ref,
    p1_ref,
    p2_ref,
    p3_ref,
    cot_ref,
    fc7_ref,
    fc6_ref,
    rows_ref,
    cols_ref,
    spread_ref,
    first_ref,
    second_ref,
    grad_ref,
    maps_ref,
    parts_ref,
    back_ref,
):
    sec = sec_ref[0]
    for d, ref in enumerate((p0_ref, p1_ref, p2_ref, p3_ref)):
        parts_ref[lax.rem(sec + 4 - d, 4)] = ref[...].astype(F32)
    first_pre = parts_ref[0] + parts_ref[1] + parts_ref[2] + parts_ref[3]
    first_act, first_slope = gelu_parts(first_pre)
    first_b = first_act.astype(BF)
    first_ref[...] = first_b
    second_pre = mm(first_b, fc7_ref[...])
    second_slope = gelu_parts(second_pre)[1]
    grad_second = (cot_ref[...].astype(F32) * second_slope).astype(BF)
    second_ref[...] = grad_second
    grad_first = (mm(grad_second, fc7_ref[...], NT) * first_slope).astype(BF)
    grad_ref[...] = grad_first
    depth = fc6_ref.shape[0]
    back_ref[:depth] = mm(fc6_ref[...], grad_first, NT).astype(BF)
    back_ref[depth:] = jnp.zeros((back_ref.shape[0] - depth, back_ref.shape[1]), BF)
    channels = back_ref.shape[0] // (2 * PAIRS)

    def weights(b):
        if b >= BINS:
            return jnp.zeros((rows_ref.shape[1], CELLS), BF)
        return (rows_ref[b // POOLED] * cols_ref[b % POOLED]).astype(BF)

    total = jnp.zeros((channels, CELLS), F32)
    for p in range(PAIRS):
        lo = 2 * p * channels
        left = jnp.concatenate(
            [back_ref[lo : lo + channels], back_ref[lo + channels : lo + 2 * channels]], axis=1
        )
        right = jnp.concatenate([weights(2 * p), weights(2 * p + 1)], axis=0)
        total = total + mm(left, right)
    total_b = total.astype(BF)
    maps_ref[:channels] = mm(total_b, spread_ref[0]).astype(BF)
    maps_ref[channels:] = mm(total_b, spread_ref[1]).astype(BF)


def head_grads_body(grad_ref, crops_ref, second_ref, first_ref, out_ref, held_ref, sems):
    wide = crops_ref.shape[1]
    rows = out_ref.shape[0] // 4
    span_all = pl.ds(0, held_ref.shape[1])
    copies = []
    for j in range(4):
        at = pl.ds(j * rows, rows)
        span = slice(j * rows, (j + 1) * rows)
        held_ref[at, :wide] = mm(grad_ref[:, span], crops_ref[...], TN).astype(BF)
        held_ref[at, wide:] = mm(second_ref[:, span], first_ref[...], TN).astype(BF)
        copies.append(
            pltpu.make_async_copy(held_ref.at[at], out_ref.at[at, span_all], sems.at[j])
        )
        copies[-1].start()
    for copy in copies:
        copy.wait()


def map_grads_body(maps_ref, order_ref, top_ref, pooled_ref, _, out_ref, held_ref, sems):
    ordered = mm(order_ref[...], maps_ref[...]).astype(BF)
    half = ordered.shape[0] // 2
    width = held_ref.shape[1]
    span = pl.ds(out_ref.shape[1] - width, width)
    copies = []
    for j, cells in enumerate((top_ref, pooled_ref)):
        at = pl.ds(j * half, half)
        held_ref[at] = mm(ordered[j * half : (j + 1) * half], cells[...]).astype(BF)
        copies.append(pltpu.make_async_copy(held_ref.at[at], out_ref.at[at, span], sems.at[j]))
        copies[-1].start()
    for copy in copies:
        copy.wait()


def first_grad_body(
    core_ref, a0_ref, a1_ref, a2_ref, a3_ref, g0_ref, g1_ref, g2_ref, g3_ref, mine_ref, other_ref
):
    is_zero = core_ref[3] == 0
    lefts = (a0_ref, a1_ref, a2_ref, a3_ref)
    rights = (g0_ref, g1_ref, g2_ref, g3_ref)
    total = mm(lefts[0][...], rights[0][...], TN)
    for d in range(1, 4):
        total = total + mm(lefts[d][...], rights[d][...], TN)
    rows = mine_ref.shape[1]
    for y in range(4):
        low = total[2 * y * rows : (2 * y + 1) * rows]
        high = total[(2 * y + 1) * rows : (2 * y + 2) * rows]
        mine_ref[y] = jnp.where(is_zero, low, high).astype(BF)
        other_ref[y] = jnp.where(is_zero, high, low).astype(BF)


def second_grad_body(
    core_ref, a0_ref, a1_ref, a2_ref, a3_ref, g0_ref, g1_ref, g2_ref, g3_ref, mine_ref, other_ref
):
    is_zero = core_ref[3] == 0
    lefts = (a0_ref, a1_ref, a2_ref, a3_ref)
    rights = (g0_ref, g1_ref, g2_ref, g3_ref)
    total = mm(lefts[0][...], rights[0][...], TN)
    for d in range(1, 4):
        total = total + mm(lefts[d][...], rights[d][...], TN)
    rows = mine_ref.shape[1]
    for z in range(4):
        low = total[z * rows : (z + 1) * rows]
        high = total[(z + 4) * rows : (z + 5) * rows]
        mine_ref[z] = jnp.where(is_zero, low, high).astype(BF)
        other_ref[z] = jnp.where(is_zero, high, low).astype(BF)


def pair_body(which, place_ref, mine_ref, got_ref, kept_ref, one_ref, two_ref, three_ref):
    place = place_ref[which]

    def total(d):
        at = lax.rem(place + d, 4)
        return mine_ref[at].astype(F32) + got_ref[at].astype(F32)

    kept_ref[...] = total(0)
    for d, ref in enumerate((one_ref, two_ref, three_ref)):
        ref[...] = total(d + 1).astype(BF)


def split_body(place_ref, stack_ref, *outs):
    rows = outs[0].shape[0]
    for d, ref in enumerate(outs):
        at = pl.multiple_of(lax.rem(place_ref[2] + d, 4) * rows, rows)
        ref[...] = stack_ref[pl.ds(at, rows)]


def sum_body(own_ref, g1_ref, g2_ref, g3_ref, out_ref):
    total = own_ref[...].astype(F32)
    for ref in (g1_ref, g2_ref, g3_ref):
        total = total + ref[...].astype(F32)
    out_ref[...] = total


def strips_body(
    place_ref, kept_ref, g1_ref, g2_ref, g3_ref, own_ref, one_ref, two_ref, three_ref
):
    total = kept_ref[...]
    for ref in (g1_ref, g2_ref, g3_ref):
        total = total + ref[...].astype(F32)
    rows = own_ref.shape[0]
    strips = [total[j * rows : (j + 1) * rows] for j in range(4)]
    for d, ref in enumerate((own_ref, one_ref, two_ref, three_ref)):
        at = lax.rem(place_ref[2] + d, 4)
        picked = strips[3]
        for j in range(3):
            picked = jnp.where(at == j, strips[j], picked)
        ref[...] = picked.astype(ref.dtype)


def join_body(place_ref, own_ref, g1_ref, g2_ref, g3_ref, out_ref):
    columns = own_ref.shape[1]
    for d, ref in enumerate((own_ref, g1_ref, g2_ref, g3_ref)):
        at = pl.multiple_of(lax.rem(place_ref[2] + 4 - d, 4) * columns, 128)
        out_ref[:, pl.ds(at, columns)] = ref[...].astype(F32)


def cell_tables():
    index = np.arange(CELLS)
    zero = index < GRID * GRID
    one = (index >= GRID * GRID) & (index < GRID * GRID + HALF * HALF)
    inner = index - GRID * GRID
    row = np.where(zero, index // GRID, np.where(one, inner // HALF, -9))
    col = np.where(zero, index % GRID, np.where(one, inner % HALF, -9))
    return zero, one, row.astype(np.int32), col.astype(np.int32)


def grid_constants():
    cells = np.arange(GRID * GRID)
    block = (cells // GRID // 2) * HALF + (cells % GRID) // 2
    average = 0.25 * (block[:, None] == block[None, :])
    place = np.zeros((2, GRID * GRID, CELLS))
    place[0, cells, cells] = 1.0
    for b in range(HALF * HALF):
        place[1, np.where(block == b)[0][0], GRID * GRID + b] = 1.0
    spread = np.zeros((2, CELLS, GRID * GRID))
    spread[0, cells, cells] = 1.0
    spread[1, GRID * GRID + block, cells] = 0.25
    return average, place, spread


def tables_body(boxes_ref, weights_ref, cells_ref, fwd_ref, bwd_ref, cols_ref):
    row, col = cells_ref[0:1], cells_ref[1:2]
    zero, one = cells_ref[2:3] > 0, cells_ref[3:4] > 0
    box_zero = boxes_ref[:, 0:1] == 0
    forward = (box_zero & zero) | (~box_zero & one)
    backward = forward | (box_zero & one)
    halved = box_zero & one
    at_rows, at_cols = [], []
    for u in range(SPAN):
        at_y = boxes_ref[:, 1:2] + u
        at_x = boxes_ref[:, 2:3] + u
        at_rows.append(row == jnp.where(halved, at_y // 2, at_y))
        at_cols.append(col == jnp.where(halved, at_x // 2, at_x))
    for i in range(POOLED):
        rows = jnp.zeros(fwd_ref.shape[1:], F32)
        cols = jnp.zeros(fwd_ref.shape[1:], F32)
        for u in range(SPAN):
            y_at, x_at = SPAN * i + u, SPAN * (POOLED + i) + u
            rows = rows + jnp.where(at_rows[u], weights_ref[:, y_at : y_at + 1], 0.0)
            cols = cols + jnp.where(at_cols[u], weights_ref[:, x_at : x_at + 1], 0.0)
        fwd_ref[i] = jnp.where(forward, rows, 0.0)
        bwd_ref[i] = jnp.where(backward, rows, 0.0)
        cols_ref[i] = cols


def sampling_tables(windows, bilinear):
    zero, one, row, col = cell_tables()
    boxes = windows.shape[2]
    cells = np.stack([row, col, zero.astype(np.int32), one.astype(np.int32)] + [row] * 4)
    weights = jnp.transpose(bilinear.reshape(2 * POOLED * SPAN, boxes))
    corners = jnp.transpose(windows.reshape(3, boxes))
    return direct(
        tables_body,
        [((POOLED, boxes, CELLS), F32)] * 3,
        (corners, weights, jnp.asarray(cells, jnp.int32)),
        "tables",
        nbytes=4 * 10**6,
    )


def slot_rows(owner_ids, arrived):
    boxes = owner_ids.shape[0]
    index = jnp.arange(boxes)
    same = (owner_ids[:, None] == owner_ids[None, :]) & (index[None, :] < index[:, None])
    rank = jnp.sum(same.astype(jnp.int32), axis=1)
    slots = arrived.shape[1]
    flat = arrived.reshape(-1, arrived.shape[2])
    pick = (owner_ids * slots + rank)[:, None] == jnp.arange(flat.shape[0])[None, :]
    return mm(pick.astype(BF), flat).astype(BF)


def per_device(
    images, w_in, w_out, fpn_weight, fc6_weight, fc7_weight, windows, bilinear, owners, cotangent
):
    section = lax.axis_index("section")
    dp = lax.axis_index("dp")
    z_here = lax.axis_index("head")
    y_here = dp // 2
    core = dp % 2
    w_first = w_in[0]
    w_second = w_out[0]
    width = images.shape[2]
    inner = w_first.shape[1]
    channels = fc6_weight.shape[0]
    units = fc6_weight.shape[2]
    places = jnp.stack([section, y_here, z_here, core]).astype(jnp.int32)
    average, place, spread = grid_constants()
    average = jnp.asarray(average, BF)
    place = jnp.asarray(place, BF)
    spread = jnp.asarray(spread, BF)

    fpn_rows = jnp.transpose(fpn_weight, (0, 2, 1)).reshape(2 * channels, width)
    fpn_all = lax.all_gather(fpn_rows, "section", axis=0, tiled=True)
    fc6_rows = jnp.transpose(fc6_weight, (1, 0, 2)).reshape(BINS * channels, units)
    tokens = images[0]
    shape = tokens.shape
    wide_shape = (shape[0], inner)
    incoming = None
    weights = (in_hbm(w_first), in_hbm(w_second))
    for tick in range(4):
        outs = [(shape, BF)]
        if tick > 0:
            outs.append((shape, BF))
        if tick == 3:
            outs += [(shape, BF), (wide_shape, F32)] + [((shape[0], inner // 4), BF)] * 4
        inputs = (tokens,) if tick == 0 else (tokens, incoming)
        results = call(
            functools.partial(forward_body, tick),
            outs,
            (places, *inputs, *weights),
            f"block_forward_{tick}",
            ready=2 + len(inputs) if tick > 1 else 0,
            scalars=1,
            chunks={1 + len(inputs): 1, 2 + len(inputs): 0},
            scratch=(pltpu.VMEM(wide_shape, BF),) if tick == 3 else (),
            vmem=28 if tick < 2 else 14,
            flops=3 * 10**9,
            nbytes=18 * 10**6,
        )
        result = results[0]
        if tick > 0:
            tokens = results[1]
        if tick == 3:
            normed_b, slope, *act_pieces = results[2:]
            break
        if tick == 0:
            cotangent, result = lax.optimization_barrier((cotangent, result))
            padded = jnp.pad(cotangent[0], ((0, 0), (0, 2), (0, 0)))
            cot_arrived = lax.all_to_all(
                padded, ("dp", "head"), split_axis=0, concat_axis=0, tiled=True
            )
        incoming = lax.ppermute(result, "section", [(tick, tick + 1)])
        if tick == 0:
            windows, bilinear, result = lax.optimization_barrier((windows, bilinear, result))
            rows_fwd, rows_bwd, cols_all = sampling_tables(windows, bilinear)
            held = (incoming, rows_fwd, rows_bwd, cols_all)
            incoming, rows_fwd, rows_bwd, cols_all = lax.optimization_barrier(held)
        if tick == 1:
            owner_ids, result = lax.optimization_barrier((owners[0, :, 0], result))
            cot_rows = slot_rows(owner_ids, cot_arrived)
            held = (cot_rows, fpn_all, w_first, w_second)
            cot_rows, fpn_all, w_first, w_second = lax.optimization_barrier(held)
            weights = loaded("weights_1", w_first, w_second)
            held = (incoming, cot_rows, weights)
            incoming, cot_rows, weights = lax.optimization_barrier(held)
    top = result

    levels, pooled = direct(
        pyramid_body,
        [((4, channels, CELLS), BF), (top.shape, BF)],
        (top, fpn_all, average, place),
        "pyramid",
        flops=10**9,
        nbytes=3 * 10**6,
    )
    sent = [lax.ppermute(levels[s], "section", [(3, s)]) for s in range(3)]
    boxes = windows.shape[2]
    part, crops = direct(
        crops_body,
        [((boxes, units), BF), ((boxes, 2 * PAIRS * channels), BF)],
        (places, levels, *sent, rows_fwd, cols_all, fc6_rows),
        "crops",
        scalars=1,
        flops=10**9,
        nbytes=6 * 10**6,
    )
    parts = [part] + [shifted(part, "section", d) for d in (1, 2, 3)]
    first_b, grad_second, grad_first, maps = direct(
        head_body,
        [((boxes, units), BF)] * 3 + [((2 * channels, GRID * GRID), BF)],
        (
            places,
            *parts,
            cot_rows,
            fc7_weight,
            fc6_rows,
            rows_bwd,
            cols_all,
            spread,
        ),
        "head",
        scratch=(
            pltpu.VMEM((4, boxes, units), F32),
            pltpu.VMEM((2 * PAIRS * channels, boxes), BF),
        ),
        scalars=1,
        flops=10**9,
        nbytes=6 * 10**6,
    )
    returned = [lax.ppermute(maps, "section", [(s, 3)]) for s in range(3)]
    stack_shape = (units, crops.shape[1] + units + width)
    (stacked,) = direct(
        head_grads_body,
        [(stack_shape, BF)],
        (grad_first, crops, grad_second, first_b),
        "head_grads",
        scratch=(
            pltpu.VMEM((units, crops.shape[1] + units), BF),
            pltpu.SemaphoreType.DMA((4,)),
        ),
        flops=10**9,
        nbytes=6 * 10**6,
        out_space=pl.ANY,
    )
    returned, stacked = lax.optimization_barrier((returned, stacked))
    grad_out, map_rows = direct(
        top_grad_body,
        [(top.shape, BF), ((8 * channels, GRID * GRID), BF)],
        (*returned, maps, fpn_all),
        "top_grad",
        flops=10**9,
        nbytes=3 * 10**6,
    )

    quarter = inner // 4

    incoming = None
    for tick in range(3):
        outs = [(shape, BF)]
        if tick > 0:
            outs.append((shape, BF))
        inputs = (grad_out,) if tick == 0 else (grad_out, incoming)
        results = call(
            functools.partial(backward_body, tick),
            outs,
            (places, *inputs, slope, tokens, *weights),
            f"block_backward_{tick}",
            ready=4 + len(inputs),
            scalars=1,
            chunks={1 + len(inputs): 1, 3 + len(inputs): 1, 4 + len(inputs): 0},
            vmem=14,
            flops=3 * 10**9,
            nbytes=18 * 10**6,
        )
        grad_in = results[0]
        if tick > 0:
            grad_out = results[1]
        if tick == 0:
            held = (grad_in, map_rows, act_pieces)
            grad_in, map_rows, act_pieces = lax.optimization_barrier(held)
            incoming = lax.ppermute(grad_in, "section", [(3, 2)])
            act_parts = [act_pieces[0]] + [shifted_y(act_pieces[d], d) for d in (1, 2, 3)]
            order = np.zeros((8 * channels, 8 * channels))
            for r in range(8 * channels):
                order[r, ((r % 16) // 4) * 2 * channels + (r // 16) * 4 + r % 4] = 1.0
            stacked = pl.pallas_call(
                map_grads_body,
                out_shape=jax.ShapeDtypeStruct(stack_shape, BF),
                in_specs=[pl.BlockSpec(memory_space=pltpu.VMEM)] * 4
                + [pl.BlockSpec(memory_space=pl.ANY)],
                out_specs=pl.BlockSpec(memory_space=pl.ANY),
                scratch_shapes=[
                    pltpu.VMEM((8 * channels, width), BF),
                    pltpu.SemaphoreType.DMA((2,)),
                ],
                input_output_aliases={4: 0},
                compiler_params=pltpu.CompilerParams(vmem_limit_bytes=18 * 1024 * 1024),
                cost_estimate=pl.CostEstimate(
                    flops=10**9, bytes_accessed=4 * 10**6, transcendentals=0
                ),
                name="map_grads",
            )(map_rows, jnp.asarray(order, BF), top, pooled, in_hbm(stacked))
            stacked = lax.psum_scatter(stacked, "dp", scatter_dimension=0, tiled=True)
            w_first, w_second, grad_in = lax.optimization_barrier((w_first, w_second, grad_in))
            weights = loaded("weights_2", w_first, w_second)
            incoming, weights = lax.optimization_barrier((incoming, weights))
        elif tick == 1:
            incoming = lax.ppermute(grad_in, "section", [(2, 1)])
            incoming, act_parts = lax.optimization_barrier((incoming, act_parts))
        else:
            grad_in, normed_b = lax.optimization_barrier((grad_in, normed_b))
            incoming = lax.ppermute(grad_in, "section", [(1, 0)])
            normed_parts = [normed_b] + [shifted(normed_b, "head", d) for d in (1, 2, 3)]
    (grad_out,) = direct(
        pick_body, [(shape, BF)], (places, grad_out, incoming), "pick", scalars=1, nbytes=10**6
    )

    out_parts = [grad_out] + [shifted_y(grad_out, d) for d in (1, 2, 3)]
    pre_pieces = call(
        last_backward_body,
        [((shape[0], quarter), BF)] * 4,
        (places, grad_out, slope, weights[1]),
        "block_backward_3",
        scalars=1,
        ready=3,
        vmem=14,
        chunks={2: 1, 3: 0},
        scratch=(pltpu.VMEM(wide_shape, BF),),
        flops=2 * 10**9,
        nbytes=10 * 10**6,
    )
    pre_parts = [pre_pieces[0]] + [shifted(pre_pieces[d], "head", d) for d in (1, 2, 3)]
    held = (pre_parts, out_parts, normed_parts)
    pre_parts, out_parts, normed_parts = lax.optimization_barrier(held)
    rows_in = width // 8
    rows_out = quarter // 8
    mine_first, other_first = direct(
        first_grad_body,
        [((4, rows_in, quarter), BF)] * 2,
        (places, *normed_parts, *pre_parts),
        "first_grad",
        vmem=24,
        scalars=1,
        flops=2 * 10**9,
        nbytes=5 * 10**6,
    )
    mine_second, other_second = direct(
        second_grad_body,
        [((4, rows_out, width), BF)] * 2,
        (places, *act_parts, *out_parts),
        "second_grad",
        vmem=24,
        scalars=1,
        flops=2 * 10**9,
        nbytes=5 * 10**6,
    )
    swapped_first = core_swapped(other_first)
    swapped_second = core_swapped(other_second)

    def pair_sums(which, mine, swapped, name):
        return direct(
            functools.partial(pair_body, which),
            [(mine.shape[1:], F32)] + [(mine.shape[1:], BF)] * 3,
            (places, mine, swapped),
            name,
            scalars=1,
            nbytes=5 * 10**6,
        )

    kept_first, *out_first = pair_sums(1, mine_first, swapped_first, "pair_first")
    grad_w_out, *out_second = pair_sums(2, mine_second, swapped_second, "pair_second")
    held = (out_first, out_second, stacked)
    out_first, out_second, stacked = lax.optimization_barrier(held)
    stack_rows = units // 32
    kept_stack, *out_stack = direct(
        split_body,
        [((stack_rows, stacked.shape[1]), BF)] * 4,
        (places, stacked),
        "split",
        scalars=1,
        nbytes=10**6,
    )
    got_stack = [shifted(out_stack[d - 1], "head", d) for d in (1, 2, 3)]
    (stacked,) = direct(
        sum_body,
        [(kept_stack.shape, F32)],
        (kept_stack, *got_stack),
        "stack_sum",
        nbytes=10**6,
    )
    got_first = [shifted_y(out_first[d - 1], d) for d in (1, 2, 3)]
    wide = crops.shape[1]
    fpn_part = stacked[:, wide + units :].astype(BF).reshape(4, 4, width)
    fpn_got = [lax.ppermute(fpn_part[s], "section", [(3, s)]) for s in range(3)]
    got_second = [shifted(out_second[d - 1], "head", d) for d in (1, 2, 3)]
    own = jnp.where(section == 3, fpn_part[3], fpn_got[0] + fpn_got[1] + fpn_got[2])
    fpn_rows = lax.all_to_all(
        jnp.broadcast_to(own[None], (32,) + own.shape),
        ("dp", "head"),
        split_axis=0,
        concat_axis=0,
        tiled=True,
    )
    last_rows = rows_in // 4
    got_first, stacked = lax.optimization_barrier((got_first, stacked))
    kept_strip, *out_strips = direct(
        strips_body,
        [((last_rows, quarter), F32)] + [((last_rows, quarter), BF)] * 3,
        (places, kept_first, *got_first),
        "strips",
        scalars=1,
        nbytes=3 * 10**6,
    )
    strips = [shifted(out_strips[d - 1], "head", d) for d in (1, 2, 3)]
    for got in got_second:
        grad_w_out = grad_w_out + got.astype(F32)
    (grad_w_in,) = direct(
        join_body,
        [((last_rows, inner), F32)],
        (places, kept_strip, *strips),
        "join",
        scalars=1,
        nbytes=10**6,
    )

    fc6_part = stacked[:, :wide].reshape(-1, 2 * PAIRS, channels)[:, :BINS]
    fc6_out = jnp.transpose(fc6_part.astype(F32), (2, 1, 0))
    fc7_out = jnp.transpose(stacked[:, wide : wide + units].astype(F32))
    fpn_out = fpn_rows.astype(F32)
    fpn_out = jnp.transpose(fpn_out.reshape(2, channels, width), (0, 2, 1))
    return (grad_w_in[None], grad_w_out[None], fpn_out, fc6_out, fc7_out)


def solution(mesh):
    return jax.shard_map(
        per_device,
        mesh=mesh,
        in_specs=(
            P(("dp", "head"), None, None),
            P("section", None, None),
            P("section", None, None),
            P(None, None, "section"),
            P("section", None, None),
            P(),
            P(None, ("dp", "head"), None),
            P(None, None, None, ("dp", "head"), None),
            P(("dp", "head"), None, None),
            P(("dp", "head"), None, None, None),
        ),
        out_specs=(
            P("section", ("dp", "head"), None),
            P("section", ("dp", "head"), None),
            P(None, None, "section"),
            P("section", None, ("dp", "head")),
            P(None, ("dp", "head")),
        ),
        check_vma=False,
    )
```

```python
import functools
import math

import jax
import jax.numpy as jnp
import numpy as np
from jax import lax
from jax.experimental import pallas as pl
from jax.experimental.pallas import tpu as pltpu
from jax.sharding import PartitionSpec as P

GRID = 12
HALF = GRID // 2
SPAN = 4
POOLED = 7
BINS = POOLED * POOLED
PAIRS = (BINS + 1) // 2
CELLS = 256

EPS = 1e-06
GELU_C = math.sqrt(2.0 / math.pi)
BF = jnp.bfloat16
F32 = jnp.float32
STEP = 512
AHEAD = 3

NN = (((1,), (0,)), ((), ()))
NT = (((1,), (1,)), ((), ()))
TN = (((0,), (0,)), ((), ()))


def mm(left, right, dims=NN):
    return lax.dot_general(left, right, dims, preferred_element_type=F32)


def gelu_parts(values):
    inner_arg = GELU_C * (values + 0.044715 * values * values * values)
    tangent = jnp.tanh(inner_arg)
    result = 0.5 * values * (1.0 + tangent)
    slope = 0.5 * (1.0 + tangent) + 0.5 * values * (1.0 - tangent * tangent) * GELU_C * (
        1.0 + 3.0 * 0.044715 * values * values
    )
    return (result, slope)


def norm_parts(tokens):
    floats = tokens.astype(F32)
    centred = floats - jnp.mean(floats, axis=-1, keepdims=True)
    scale_inv = lax.rsqrt(jnp.mean(centred * centred, axis=-1, keepdims=True) + EPS)
    return (centred * scale_inv, scale_inv)


class Staged:
    def __init__(self, source, buffer, sems, chunk_axis):
        self.buffer = buffer
        self.shape = buffer.shape
        self.axis = chunk_axis
        self.copies = []
        self.waited = set()
        if chunk_axis is None:
            self.copies.append(pltpu.make_async_copy(source, buffer, sems.at[0]))
        else:
            for j in range(self.shape[chunk_axis] // STEP):
                at = self.part(j)
                self.copies.append(
                    pltpu.make_async_copy(source.at[at], buffer.at[at], sems.at[j])
                )

    def part(self, j):
        span = pl.ds(j * STEP, STEP)
        return (span, slice(None)) if self.axis == 0 else (slice(None), span)

    def start(self, j):
        if j < len(self.copies):
            self.copies[j].start()

    def wait(self, j):
        if j not in self.waited:
            self.waited.add(j)
            self.copies[j].wait()

    def chunk(self, j):
        self.wait(j)
        self.start(j + AHEAD)
        return self.buffer[self.part(j)]

    def __getitem__(self, index):
        self.wait(0)
        return self.buffer[index]

    def finish(self):
        for j in range(len(self.copies)):
            self.wait(j)


class Held(Staged):
    def __init__(self, buffer, chunk_axis):
        self.buffer = buffer
        self.shape = buffer.shape
        self.axis = chunk_axis
        self.copies = []

    def wait(self, j):
        pass


def load_body(*refs):
    count = (len(refs) - 1) // 2
    copies = [
        pltpu.make_async_copy(refs[i], refs[count + i], refs[-1].at[i]) for i in range(count)
    ]
    for copy in copies:
        copy.start()
    for copy in copies:
        copy.wait()


def loaded(name, *arrays):
    return pl.pallas_call(
        load_body,
        out_shape=[jax.ShapeDtypeStruct(a.shape, a.dtype) for a in arrays],
        in_specs=[pl.BlockSpec(memory_space=pl.ANY)] * len(arrays),
        out_specs=[pl.BlockSpec(memory_space=pl.ANY)] * len(arrays),
        scratch_shapes=[pltpu.SemaphoreType.DMA((len(arrays),))],
        compiler_params=pltpu.CompilerParams(vmem_limit_bytes=2 * 1024 * 1024),
        cost_estimate=pl.CostEstimate(
            flops=0, bytes_accessed=10**5, transcendentals=0
        ),
        name=name,
    )(*[in_hbm(a) for a in arrays])


def call(
    body,
    outs,
    args,
    name,
    scratch=(),
    scalars=0,
    chunks=None,
    flops=0,
    nbytes=0,
    vmem=18,
    ready=0,
):
    chunks = chunks or {}
    count = len(args) - scalars - ready
    axes = [chunks.get(i + scalars) for i in range(count)]
    last_axes = [chunks.get(i + scalars) for i in range(count, count + ready)]
    copied = args[scalars : scalars + count]
    sizes = [1 if axis is None else arg.shape[axis] // STEP for axis, arg in zip(axes, copied)]

    def kernel(*refs):
        given, sources = refs[:scalars], refs[scalars : scalars + count]
        kept = [Held(*parts) for parts in zip(refs[scalars + count : len(args)], last_axes)]
        results = refs[len(args) : len(args) + len(outs)]
        rest = refs[len(args) + len(outs) :]
        buffers, sems, extra = rest[:count], rest[count : 2 * count], rest[2 * count :]
        staged = [Staged(*parts) for parts in zip(sources, buffers, sems, axes)]
        for j in range(AHEAD):
            for item in staged:
                item.start(j)
        body(*given, *staged, *kept, *results, *extra)
        for item in staged:
            item.finish()

    return pl.pallas_call(
        kernel,
        out_shape=[jax.ShapeDtypeStruct(s, d) for s, d in outs],
        in_specs=[pl.BlockSpec(memory_space=pltpu.SMEM)] * scalars
        + [pl.BlockSpec(memory_space=pl.ANY)] * count
        + [pl.BlockSpec(memory_space=pltpu.VMEM)] * ready,
        out_specs=[pl.BlockSpec(memory_space=pltpu.VMEM) for _ in outs],
        scratch_shapes=[pltpu.VMEM(arg.shape, arg.dtype) for arg in copied]
        + [pltpu.SemaphoreType.DMA((size,)) for size in sizes]
        + list(scratch),
        compiler_params=pltpu.CompilerParams(vmem_limit_bytes=vmem * 1024 * 1024),
        cost_estimate=pl.CostEstimate(flops=flops, bytes_accessed=nbytes, transcendentals=0),
        name=name,
    )(*args)


def direct(
    body,
    outs,
    args,
    name,
    scratch=(),
    scalars=0,
    flops=0,
    nbytes=0,
    vmem=18,
    out_space=pltpu.VMEM,
):
    return pl.pallas_call(
        body,
        out_shape=[jax.ShapeDtypeStruct(s, d) for s, d in outs],
        in_specs=[pl.BlockSpec(memory_space=pltpu.SMEM)] * scalars
        + [pl.BlockSpec(memory_space=pltpu.VMEM)] * (len(args) - scalars),
        out_specs=[pl.BlockSpec(memory_space=out_space) for _ in outs],
        scratch_shapes=list(scratch),
        compiler_params=pltpu.CompilerParams(vmem_limit_bytes=vmem * 1024 * 1024),
        cost_estimate=pl.CostEstimate(flops=flops, bytes_accessed=nbytes, transcendentals=0),
        name=name,
    )(*args)


def in_hbm(array):
    return pltpu.with_memory_space_constraint(array, pltpu.HBM)


def ring(axis, shift):
    size = lax.axis_size(axis)
    return [(i, (i + shift) % size) for i in range(size)]


def shifted(value, axis, shift):
    return lax.ppermute(value, axis, ring(axis, shift))


def shifted_y(value, shift):
    return shifted(value, "dp", 2 * shift)


def core_swapped(value):
    return lax.ppermute(value, "dp", [(i, i ^ 1) for i in range(lax.axis_size("dp"))])


def gelu_quick(values):
    square = values * values
    half = 0.5 + 0.5 * jnp.tanh(values * (GELU_C + (GELU_C * 0.044715) * square))
    return half, square


def forward_body(tick, place_ref, *refs):
    if tick == 3:
        *refs, held_ref = refs
    if tick == 0:
        old_ref, w1_ref, w2_ref, *outs = refs
        tokens = old_ref[...]
    else:
        old_ref, new_ref, w1_ref, w2_ref, *outs = refs
        tokens = jnp.where(place_ref[0] == tick, new_ref[...], old_ref[...])
    result_ref = outs[0]
    if tick > 0:
        outs[1][...] = tokens
    normed = norm_parts(tokens)[0].astype(BF)
    if tick == 3:
        outs[2][...] = normed
    total = tokens.astype(F32)
    count = w1_ref.shape[1] // STEP
    values = mm(normed, w1_ref.chunk(0))
    for j in range(count):
        later = mm(normed, w1_ref.chunk(j + 1)) if j + 1 < count else None
        half, square = gelu_quick(values)
        activ = (values * half).astype(BF)
        if tick == 3:
            span = slice(j * STEP, (j + 1) * STEP)
            held_ref[:, span] = activ
            outs[3][:, span] = half + (values * (2.0 * half) * (1.0 - half)) * (
                GELU_C + (3.0 * 0.044715 * GELU_C) * square
            )
        total = total + mm(activ, w2_ref.chunk(j))
        values = later
    result_ref[...] = total.astype(BF)
    if tick == 3:
        put_pieces(place_ref[1], held_ref, outs[4:])


def put_pieces(place, held_ref, outs):
    columns = outs[0].shape[1]
    for d, ref in enumerate(outs):
        at = pl.multiple_of(lax.rem(place + d, 4) * columns, 128)
        ref[...] = held_ref[:, pl.ds(at, columns)]


def backward_body(tick, place_ref, *refs):
    if tick == 0:
        old_ref, slope_ref, tokens_ref, w1_ref, w2_ref, *outs = refs
        grad_out = old_ref[...]
    else:
        old_ref, new_ref, slope_ref, tokens_ref, w1_ref, w2_ref, *outs = refs
        grad_out = jnp.where(place_ref[0] == 3 - tick, new_ref[...], old_ref[...])
        outs[1][...] = grad_out
    total = jnp.zeros(grad_out.shape, F32)
    count = w1_ref.shape[1] // STEP
    grad_act = mm(grad_out, w2_ref.chunk(0), NT)
    for j in range(count):
        later = mm(grad_out, w2_ref.chunk(j + 1), NT) if j + 1 < count else None
        grad_pre = (grad_act * slope_ref.chunk(j)).astype(BF)
        total = total + mm(grad_pre, w1_ref.chunk(j), NT)
        grad_act = later
    normed, scale_inv = norm_parts(tokens_ref[...])
    grad_tok = scale_inv * (
        total
        - jnp.mean(total, axis=-1, keepdims=True)
        - normed * jnp.mean(total * normed, axis=-1, keepdims=True)
    )
    outs[0][...] = (grad_out.astype(F32) + grad_tok).astype(BF)


def last_backward_body(place_ref, grad_ref, slope_ref, w2_ref, *refs):
    *outs, held_ref = refs
    grad_out = grad_ref[...]
    count = w2_ref.shape[0] // STEP
    grad_act = mm(grad_out, w2_ref.chunk(0), NT)
    for j in range(count):
        later = mm(grad_out, w2_ref.chunk(j + 1), NT) if j + 1 < count else None
        held_ref[:, j * STEP : (j + 1) * STEP] = (grad_act * slope_ref.chunk(j)).astype(BF)
        grad_act = later
    put_pieces(place_ref[2], held_ref, outs)


def pick_body(place_ref, old_ref, new_ref, out_ref):
    out_ref[...] = jnp.where(place_ref[0] == 0, new_ref[...], old_ref[...])


def pyramid_body(top_ref, weight_ref, avg_ref, place_ref, levels_ref, pooled_ref):
    top = top_ref[...]
    pooled = mm(avg_ref[...], top).astype(BF)
    pooled_ref[...] = pooled
    weights = weight_ref[...]
    from_top = mm(weights, top, NT)
    from_pooled = mm(weights, pooled, NT)
    half = weights.shape[0] // 8
    for s in range(4):
        base = 2 * half * s
        one = from_pooled[base + half : base + 2 * half]
        zero = from_top[base : base + half] + one
        levels_ref[s] = (
            mm(zero.astype(BF), place_ref[0]) + mm(one.astype(BF), place_ref[1])
        ).astype(BF)


def top_grad_body(z0_ref, z1_ref, z2_ref, z3_ref, weight_ref, grad_ref, rows_ref):
    rows = jnp.concatenate([z0_ref[...], z1_ref[...], z2_ref[...], z3_ref[...]], axis=0)
    rows_ref[...] = rows
    grad_ref[...] = mm(rows, weight_ref[...], TN).astype(BF)


def crops_body(
    sec_ref, levels_ref, r0_ref, r1_ref, r2_ref, rows_ref, cols_ref, fc6_ref, part_ref, crops_ref
):
    is_last = sec_ref[0] == 3
    arrived = r0_ref[...] + r1_ref[...] + r2_ref[...]
    own = jnp.where(is_last, levels_ref[3], arrived)
    blank = jnp.zeros_like(own)
    both = jnp.concatenate(
        [jnp.concatenate([own, blank], axis=1), jnp.concatenate([blank, own], axis=1)], axis=0
    )

    def weights(b):
        if b >= BINS:
            return jnp.zeros((rows_ref.shape[1], CELLS), BF)
        return (rows_ref[b // POOLED] * cols_ref[b % POOLED]).astype(BF)

    for p in range(PAIRS):
        pair = jnp.concatenate([weights(2 * p), weights(2 * p + 1)], axis=1)
        crops_ref[:, 128 * p : 128 * (p + 1)] = mm(pair, both, NT).astype(BF)
    depth = fc6_ref.shape[0]
    whole = depth // 128 * 128
    part = mm(crops_ref[:, :whole], fc6_ref[:whole])
    part = part + mm(crops_ref[:, whole:depth], fc6_ref[whole:])
    part_ref[...] = part.astype(BF)


def head_body(
    sec_ref,
    p0_ref,
    p1_ref,
    p2_ref,
    p3_ref,
    cot_ref,
    fc7_ref,
    fc6_ref,
    rows_ref,
    cols_ref,
    spread_ref,
    first_ref,
    second_ref,
    grad_ref,
    maps_ref,
    parts_ref,
    back_ref,
):
    sec = sec_ref[0]
    for d, ref in enumerate((p0_ref, p1_ref, p2_ref, p3_ref)):
        parts_ref[lax.rem(sec + 4 - d, 4)] = ref[...].astype(F32)
    first_pre = parts_ref[0] + parts_ref[1] + parts_ref[2] + parts_ref[3]
    first_act, first_slope = gelu_parts(first_pre)
    first_b = first_act.astype(BF)
    first_ref[...] = first_b
    second_pre = mm(first_b, fc7_ref[...])
    second_slope = gelu_parts(second_pre)[1]
    grad_second = (cot_ref[...].astype(F32) * second_slope).astype(BF)
    second_ref[...] = grad_second
    grad_first = (mm(grad_second, fc7_ref[...], NT) * first_slope).astype(BF)
    grad_ref[...] = grad_first
    depth = fc6_ref.shape[0]
    back_ref[:depth] = mm(fc6_ref[...], grad_first, NT).astype(BF)
    back_ref[depth:] = jnp.zeros((back_ref.shape[0] - depth, back_ref.shape[1]), BF)
    channels = back_ref.shape[0] // (2 * PAIRS)

    def weights(b):
        if b >= BINS:
            return jnp.zeros((rows_ref.shape[1], CELLS), BF)
        return (rows_ref[b // POOLED] * cols_ref[b % POOLED]).astype(BF)

    total = jnp.zeros((channels, CELLS), F32)
    for p in range(PAIRS):
        lo = 2 * p * channels
        left = jnp.concatenate(
            [back_ref[lo : lo + channels], back_ref[lo + channels : lo + 2 * channels]], axis=1
        )
        right = jnp.concatenate([weights(2 * p), weights(2 * p + 1)], axis=0)
        total = total + mm(left, right)
    total_b = total.astype(BF)
    maps_ref[:channels] = mm(total_b, spread_ref[0]).astype(BF)
    maps_ref[channels:] = mm(total_b, spread_ref[1]).astype(BF)


def head_grads_body(grad_ref, crops_ref, second_ref, first_ref, out_ref, held_ref, sems):
    wide = crops_ref.shape[1]
    rows = out_ref.shape[0] // 4
    span_all = pl.ds(0, held_ref.shape[1])
    copies = []
    for j in range(4):
        at = pl.ds(j * rows, rows)
        span = slice(j * rows, (j + 1) * rows)
        held_ref[at, :wide] = mm(grad_ref[:, span], crops_ref[...], TN).astype(BF)
        held_ref[at, wide:] = mm(second_ref[:, span], first_ref[...], TN).astype(BF)
        copies.append(
            pltpu.make_async_copy(held_ref.at[at], out_ref.at[at, span_all], sems.at[j])
        )
        copies[-1].start()
    for copy in copies:
        copy.wait()


def map_grads_body(maps_ref, order_ref, top_ref, pooled_ref, _, out_ref, held_ref, sems):
    ordered = mm(order_ref[...], maps_ref[...]).astype(BF)
    half = ordered.shape[0] // 2
    width = held_ref.shape[1]
    span = pl.ds(out_ref.shape[1] - width, width)
    copies = []
    for j, cells in enumerate((top_ref, pooled_ref)):
        at = pl.ds(j * half, half)
        held_ref[at] = mm(ordered[j * half : (j + 1) * half], cells[...]).astype(BF)
        copies.append(pltpu.make_async_copy(held_ref.at[at], out_ref.at[at, span], sems.at[j]))
        copies[-1].start()
    for copy in copies:
        copy.wait()


def first_grad_body(
    core_ref, a0_ref, a1_ref, a2_ref, a3_ref, g0_ref, g1_ref, g2_ref, g3_ref, mine_ref, other_ref
):
    is_zero = core_ref[3] == 0
    lefts = (a0_ref, a1_ref, a2_ref, a3_ref)
    rights = (g0_ref, g1_ref, g2_ref, g3_ref)
    total = mm(lefts[0][...], rights[0][...], TN)
    for d in range(1, 4):
        total = total + mm(lefts[d][...], rights[d][...], TN)
    rows = mine_ref.shape[1]
    for y in range(4):
        low = total[2 * y * rows : (2 * y + 1) * rows]
        high = total[(2 * y + 1) * rows : (2 * y + 2) * rows]
        mine_ref[y] = jnp.where(is_zero, low, high).astype(BF)
        other_ref[y] = jnp.where(is_zero, high, low).astype(BF)


def second_grad_body(
    core_ref, a0_ref, a1_ref, a2_ref, a3_ref, g0_ref, g1_ref, g2_ref, g3_ref, mine_ref, other_ref
):
    is_zero = core_ref[3] == 0
    lefts = (a0_ref, a1_ref, a2_ref, a3_ref)
    rights = (g0_ref, g1_ref, g2_ref, g3_ref)
    total = mm(lefts[0][...], rights[0][...], TN)
    for d in range(1, 4):
        total = total + mm(lefts[d][...], rights[d][...], TN)
    rows = mine_ref.shape[1]
    for z in range(4):
        low = total[z * rows : (z + 1) * rows]
        high = total[(z + 4) * rows : (z + 5) * rows]
        mine_ref[z] = jnp.where(is_zero, low, high).astype(BF)
        other_ref[z] = jnp.where(is_zero, high, low).astype(BF)


def pair_body(which, place_ref, mine_ref, got_ref, kept_ref, one_ref, two_ref, three_ref):
    place = place_ref[which]

    def total(d):
        at = lax.rem(place + d, 4)
        return mine_ref[at].astype(F32) + got_ref[at].astype(F32)

    kept_ref[...] = total(0)
    for d, ref in enumerate((one_ref, two_ref, three_ref)):
        ref[...] = total(d + 1).astype(BF)


def split_body(place_ref, stack_ref, *outs):
    rows = outs[0].shape[0]
    for d, ref in enumerate(outs):
        at = pl.multiple_of(lax.rem(place_ref[2] + d, 4) * rows, rows)
        ref[...] = stack_ref[pl.ds(at, rows)]


def sum_body(own_ref, g1_ref, g2_ref, g3_ref, out_ref):
    total = own_ref[...].astype(F32)
    for ref in (g1_ref, g2_ref, g3_ref):
        total = total + ref[...].astype(F32)
    out_ref[...] = total


def strips_body(
    place_ref, kept_ref, g1_ref, g2_ref, g3_ref, own_ref, one_ref, two_ref, three_ref
):
    total = kept_ref[...]
    for ref in (g1_ref, g2_ref, g3_ref):
        total = total + ref[...].astype(F32)
    rows = own_ref.shape[0]
    strips = [total[j * rows : (j + 1) * rows] for j in range(4)]
    for d, ref in enumerate((own_ref, one_ref, two_ref, three_ref)):
        at = lax.rem(place_ref[2] + d, 4)
        picked = strips[3]
        for j in range(3):
            picked = jnp.where(at == j, strips[j], picked)
        ref[...] = picked.astype(ref.dtype)


def join_body(place_ref, own_ref, g1_ref, g2_ref, g3_ref, out_ref):
    columns = own_ref.shape[1]
    for d, ref in enumerate((own_ref, g1_ref, g2_ref, g3_ref)):
        at = pl.multiple_of(lax.rem(place_ref[2] + 4 - d, 4) * columns, 128)
        out_ref[:, pl.ds(at, columns)] = ref[...].astype(F32)


def cell_tables():
    index = np.arange(CELLS)
    zero = index < GRID * GRID
    one = (index >= GRID * GRID) & (index < GRID * GRID + HALF * HALF)
    inner = index - GRID * GRID
    row = np.where(zero, index // GRID, np.where(one, inner // HALF, -9))
    col = np.where(zero, index % GRID, np.where(one, inner % HALF, -9))
    return zero, one, row.astype(np.int32), col.astype(np.int32)


def grid_constants():
    cells = np.arange(GRID * GRID)
    block = (cells // GRID // 2) * HALF + (cells % GRID) // 2
    average = 0.25 * (block[:, None] == block[None, :])
    place = np.zeros((2, GRID * GRID, CELLS))
    place[0, cells, cells] = 1.0
    for b in range(HALF * HALF):
        place[1, np.where(block == b)[0][0], GRID * GRID + b] = 1.0
    spread = np.zeros((2, CELLS, GRID * GRID))
    spread[0, cells, cells] = 1.0
    spread[1, GRID * GRID + block, cells] = 0.25
    return average, place, spread


def tables_body(boxes_ref, weights_ref, cells_ref, fwd_ref, bwd_ref, cols_ref):
    row, col = cells_ref[0:1], cells_ref[1:2]
    zero, one = cells_ref[2:3] > 0, cells_ref[3:4] > 0
    box_zero = boxes_ref[:, 0:1] == 0
    forward = (box_zero & zero) | (~box_zero & one)
    backward = forward | (box_zero & one)
    halved = box_zero & one
    at_rows, at_cols = [], []
    for u in range(SPAN):
        at_y = boxes_ref[:, 1:2] + u
        at_x = boxes_ref[:, 2:3] + u
        at_rows.append(row == jnp.where(halved, at_y // 2, at_y))
        at_cols.append(col == jnp.where(halved, at_x // 2, at_x))
    for i in range(POOLED):
        rows = jnp.zeros(fwd_ref.shape[1:], F32)
        cols = jnp.zeros(fwd_ref.shape[1:], F32)
        for u in range(SPAN):
            y_at, x_at = SPAN * i + u, SPAN * (POOLED + i) + u
            rows = rows + jnp.where(at_rows[u], weights_ref[:, y_at : y_at + 1], 0.0)
            cols = cols + jnp.where(at_cols[u], weights_ref[:, x_at : x_at + 1], 0.0)
        fwd_ref[i] = jnp.where(forward, rows, 0.0)
        bwd_ref[i] = jnp.where(backward, rows, 0.0)
        cols_ref[i] = cols


def sampling_tables(windows, bilinear):
    zero, one, row, col = cell_tables()
    boxes = windows.shape[2]
    cells = np.stack([row, col, zero.astype(np.int32), one.astype(np.int32)] + [row] * 4)
    weights = jnp.transpose(bilinear.reshape(2 * POOLED * SPAN, boxes))
    corners = jnp.transpose(windows.reshape(3, boxes))
    return direct(
        tables_body,
        [((POOLED, boxes, CELLS), F32)] * 3,
        (corners, weights, jnp.asarray(cells, jnp.int32)),
        "tables",
        nbytes=4 * 10**6,
    )


def slot_rows(owner_ids, arrived):
    boxes = owner_ids.shape[0]
    index = jnp.arange(boxes)
    same = (owner_ids[:, None] == owner_ids[None, :]) & (index[None, :] < index[:, None])
    rank = jnp.sum(same.astype(jnp.int32), axis=1)
    slots = arrived.shape[1]
    flat = arrived.reshape(-1, arrived.shape[2])
    pick = (owner_ids * slots + rank)[:, None] == jnp.arange(flat.shape[0])[None, :]
    return mm(pick.astype(BF), flat).astype(BF)


def per_device(
    images, w_in, w_out, fpn_weight, fc6_weight, fc7_weight, windows, bilinear, owners, cotangent
):
    section = lax.axis_index("section")
    dp = lax.axis_index("dp")
    z_here = lax.axis_index("head")
    y_here = dp // 2
    core = dp % 2
    w_first = w_in[0]
    w_second = w_out[0]
    width = images.shape[2]
    inner = w_first.shape[1]
    channels = fc6_weight.shape[0]
    units = fc6_weight.shape[2]
    places = jnp.stack([section, y_here, z_here, core]).astype(jnp.int32)
    average, place, spread = grid_constants()
    average = jnp.asarray(average, BF)
    place = jnp.asarray(place, BF)
    spread = jnp.asarray(spread, BF)

    fpn_rows = jnp.transpose(fpn_weight, (0, 2, 1)).reshape(2 * channels, width)
    fpn_all = lax.all_gather(fpn_rows, "section", axis=0, tiled=True)
    fc6_rows = jnp.transpose(fc6_weight, (1, 0, 2)).reshape(BINS * channels, units)
    tokens = images[0]
    shape = tokens.shape
    wide_shape = (shape[0], inner)
    incoming = None
    weights = (in_hbm(w_first), in_hbm(w_second))
    for tick in range(4):
        outs = [(shape, BF)]
        if tick > 0:
            outs.append((shape, BF))
        if tick == 3:
            outs += [(shape, BF), (wide_shape, F32)] + [((shape[0], inner // 4), BF)] * 4
        inputs = (tokens,) if tick == 0 else (tokens, incoming)
        results = call(
            functools.partial(forward_body, tick),
            outs,
            (places, *inputs, *weights),
            f"block_forward_{tick}",
            ready=2 + len(inputs) if tick > 1 else 0,
            scalars=1,
            chunks={1 + len(inputs): 1, 2 + len(inputs): 0},
            scratch=(pltpu.VMEM(wide_shape, BF),) if tick == 3 else (),
            vmem=28 if tick < 2 else 14,
            flops=3 * 10**9,
            nbytes=18 * 10**6,
        )
        result = results[0]
        if tick > 0:
            tokens = results[1]
        if tick == 3:
            normed_b, slope, *act_pieces = results[2:]
            break
        if tick == 0:
            cotangent, result = lax.optimization_barrier((cotangent, result))
            padded = jnp.pad(cotangent[0], ((0, 0), (0, 2), (0, 0)))
            cot_arrived = lax.all_to_all(
                padded, ("dp", "head"), split_axis=0, concat_axis=0, tiled=True
            )
        incoming = lax.ppermute(result, "section", [(tick, tick + 1)])
        if tick == 0:
            windows, bilinear, result = lax.optimization_barrier((windows, bilinear, result))
            rows_fwd, rows_bwd, cols_all = sampling_tables(windows, bilinear)
            held = (incoming, rows_fwd, rows_bwd, cols_all)
            incoming, rows_fwd, rows_bwd, cols_all = lax.optimization_barrier(held)
        if tick == 1:
            owner_ids, result = lax.optimization_barrier((owners[0, :, 0], result))
            cot_rows = slot_rows(owner_ids, cot_arrived)
            held = (cot_rows, fpn_all, w_first, w_second)
            cot_rows, fpn_all, w_first, w_second = lax.optimization_barrier(held)
            weights = loaded("weights_1", w_first, w_second)
            held = (incoming, cot_rows, weights)
            incoming, cot_rows, weights = lax.optimization_barrier(held)
    top = result

    levels, pooled = direct(
        pyramid_body,
        [((4, channels, CELLS), BF), (top.shape, BF)],
        (top, fpn_all, average, place),
        "pyramid",
        flops=10**9,
        nbytes=3 * 10**6,
    )
    sent = [lax.ppermute(levels[s], "section", [(3, s)]) for s in range(3)]
    boxes = windows.shape[2]
    part, crops = direct(
        crops_body,
        [((boxes, units), BF), ((boxes, 2 * PAIRS * channels), BF)],
        (places, levels, *sent, rows_fwd, cols_all, fc6_rows),
        "crops",
        scalars=1,
        flops=10**9,
        nbytes=6 * 10**6,
    )
    parts = [part] + [shifted(part, "section", d) for d in (1, 2, 3)]
    first_b, grad_second, grad_first, maps = direct(
        head_body,
        [((boxes, units), BF)] * 3 + [((2 * channels, GRID * GRID), BF)],
        (
            places,
            *parts,
            cot_rows,
            fc7_weight,
            fc6_rows,
            rows_bwd,
            cols_all,
            spread,
        ),
        "head",
        scratch=(
            pltpu.VMEM((4, boxes, units), F32),
            pltpu.VMEM((2 * PAIRS * channels, boxes), BF),
        ),
        scalars=1,
        flops=10**9,
        nbytes=6 * 10**6,
    )
    returned = [lax.ppermute(maps, "section", [(s, 3)]) for s in range(3)]
    stack_shape = (units, crops.shape[1] + units + width)
    (stacked,) = direct(
        head_grads_body,
        [(stack_shape, BF)],
        (grad_first, crops, grad_second, first_b),
        "head_grads",
        scratch=(
            pltpu.VMEM((units, crops.shape[1] + units), BF),
            pltpu.SemaphoreType.DMA((4,)),
        ),
        flops=10**9,
        nbytes=6 * 10**6,
        out_space=pl.ANY,
    )
    returned, stacked = lax.optimization_barrier((returned, stacked))
    grad_out, map_rows = direct(
        top_grad_body,
        [(top.shape, BF), ((8 * channels, GRID * GRID), BF)],
        (*returned, maps, fpn_all),
        "top_grad",
        flops=10**9,
        nbytes=3 * 10**6,
    )

    quarter = inner // 4

    incoming = None
    for tick in range(3):
        outs = [(shape, BF)]
        if tick > 0:
            outs.append((shape, BF))
        inputs = (grad_out,) if tick == 0 else (grad_out, incoming)
        results = call(
            functools.partial(backward_body, tick),
            outs,
            (places, *inputs, slope, tokens, *weights),
            f"block_backward_{tick}",
            ready=4 + len(inputs),
            scalars=1,
            chunks={1 + len(inputs): 1, 3 + len(inputs): 1, 4 + len(inputs): 0},
            vmem=14,
            flops=3 * 10**9,
            nbytes=18 * 10**6,
        )
        grad_in = results[0]
        if tick > 0:
            grad_out = results[1]
        if tick == 0:
            held = (grad_in, map_rows, act_pieces)
            grad_in, map_rows, act_pieces = lax.optimization_barrier(held)
            incoming = lax.ppermute(grad_in, "section", [(3, 2)])
            act_parts = [act_pieces[0]] + [shifted_y(act_pieces[d], d) for d in (1, 2, 3)]
            order = np.zeros((8 * channels, 8 * channels))
            for r in range(8 * channels):
                order[r, ((r % 16) // 4) * 2 * channels + (r // 16) * 4 + r % 4] = 1.0
            stacked = pl.pallas_call(
                map_grads_body,
                out_shape=jax.ShapeDtypeStruct(stack_shape, BF),
                in_specs=[pl.BlockSpec(memory_space=pltpu.VMEM)] * 4
                + [pl.BlockSpec(memory_space=pl.ANY)],
                out_specs=pl.BlockSpec(memory_space=pl.ANY),
                scratch_shapes=[
                    pltpu.VMEM((8 * channels, width), BF),
                    pltpu.SemaphoreType.DMA((2,)),
                ],
                input_output_aliases={4: 0},
                compiler_params=pltpu.CompilerParams(vmem_limit_bytes=18 * 1024 * 1024),
                cost_estimate=pl.CostEstimate(
                    flops=10**9, bytes_accessed=4 * 10**6, transcendentals=0
                ),
                name="map_grads",
            )(map_rows, jnp.asarray(order, BF), top, pooled, in_hbm(stacked))
            stacked = lax.psum_scatter(stacked, "dp", scatter_dimension=0, tiled=True)
            w_first, w_second, grad_in = lax.optimization_barrier((w_first, w_second, grad_in))
            weights = loaded("weights_2", w_first, w_second)
            incoming, weights = lax.optimization_barrier((incoming, weights))
        elif tick == 1:
            grad_in, normed_b = lax.optimization_barrier((grad_in, normed_b))
            incoming = lax.ppermute(grad_in, "section", [(2, 1)])
            normed_near = shifted(normed_b, "head", 1)
            held = (incoming, act_parts, normed_near)
            incoming, act_parts, normed_near = lax.optimization_barrier(held)
        else:
            grad_in, normed_b = lax.optimization_barrier((grad_in, normed_b))
            incoming = lax.ppermute(grad_in, "section", [(1, 0)])
            normed_parts = [normed_b, normed_near] + [shifted(normed_b, "head", d) for d in (2, 3)]
    (grad_out,) = direct(
        pick_body, [(shape, BF)], (places, grad_out, incoming), "pick", scalars=1, nbytes=10**6
    )

    out_parts = [grad_out] + [shifted_y(grad_out, d) for d in (1, 2, 3)]
    pre_pieces = call(
        last_backward_body,
        [((shape[0], quarter), BF)] * 4,
        (places, grad_out, slope, weights[1]),
        "block_backward_3",
        scalars=1,
        ready=3,
        vmem=14,
        chunks={2: 1, 3: 0},
        scratch=(pltpu.VMEM(wide_shape, BF),),
        flops=2 * 10**9,
        nbytes=10 * 10**6,
    )
    pre_parts = [pre_pieces[0]] + [shifted(pre_pieces[d], "head", d) for d in (1, 2, 3)]
    held = (pre_parts, out_parts, normed_parts)
    pre_parts, out_parts, normed_parts = lax.optimization_barrier(held)
    rows_in = width // 8
    rows_out = quarter // 8
    mine_first, other_first = direct(
        first_grad_body,
        [((4, rows_in, quarter), BF)] * 2,
        (places, *normed_parts, *pre_parts),
        "first_grad",
        vmem=24,
        scalars=1,
        flops=2 * 10**9,
        nbytes=5 * 10**6,
    )
    mine_second, other_second = direct(
        second_grad_body,
        [((4, rows_out, width), BF)] * 2,
        (places, *act_parts, *out_parts),
        "second_grad",
        vmem=24,
        scalars=1,
        flops=2 * 10**9,
        nbytes=5 * 10**6,
    )
    swapped_first = core_swapped(other_first)
    swapped_second = core_swapped(other_second)

    def pair_sums(which, mine, swapped, name):
        return direct(
            functools.partial(pair_body, which),
            [(mine.shape[1:], F32)] + [(mine.shape[1:], BF)] * 3,
            (places, mine, swapped),
            name,
            scalars=1,
            nbytes=5 * 10**6,
        )

    kept_first, *out_first = pair_sums(1, mine_first, swapped_first, "pair_first")
    grad_w_out, *out_second = pair_sums(2, mine_second, swapped_second, "pair_second")
    held = (out_first, out_second, stacked)
    out_first, out_second, stacked = lax.optimization_barrier(held)
    stack_rows = units // 32
    kept_stack, *out_stack = direct(
        split_body,
        [((stack_rows, stacked.shape[1]), BF)] * 4,
        (places, stacked),
        "split",
        scalars=1,
        nbytes=10**6,
    )
    got_stack = [shifted(out_stack[d - 1], "head", d) for d in (1, 2, 3)]
    (stacked,) = direct(
        sum_body,
        [(kept_stack.shape, F32)],
        (kept_stack, *got_stack),
        "stack_sum",
        nbytes=10**6,
    )
    got_first = [shifted_y(out_first[d - 1], d) for d in (1, 2, 3)]
    wide = crops.shape[1]
    fpn_part = stacked[:, wide + units :].astype(BF).reshape(4, 4, width)
    fpn_got = [lax.ppermute(fpn_part[s], "section", [(3, s)]) for s in range(3)]
    got_second = [shifted(out_second[d - 1], "head", d) for d in (1, 2, 3)]
    own = jnp.where(section == 3, fpn_part[3], fpn_got[0] + fpn_got[1] + fpn_got[2])
    fpn_rows = lax.all_to_all(
        jnp.broadcast_to(own[None], (32,) + own.shape),
        ("dp", "head"),
        split_axis=0,
        concat_axis=0,
        tiled=True,
    )
    last_rows = rows_in // 4
    got_first, stacked = lax.optimization_barrier((got_first, stacked))
    kept_strip, *out_strips = direct(
        strips_body,
        [((last_rows, quarter), F32)] + [((last_rows, quarter), BF)] * 3,
        (places, kept_first, *got_first),
        "strips",
        scalars=1,
        nbytes=3 * 10**6,
    )
    strips = [shifted(out_strips[d - 1], "head", d) for d in (1, 2, 3)]
    for got in got_second:
        grad_w_out = grad_w_out + got.astype(F32)
    (grad_w_in,) = direct(
        join_body,
        [((last_rows, inner), F32)],
        (places, kept_strip, *strips),
        "join",
        scalars=1,
        nbytes=10**6,
    )

    fc6_part = stacked[:, :wide].reshape(-1, 2 * PAIRS, channels)[:, :BINS]
    fc6_out = jnp.transpose(fc6_part.astype(F32), (2, 1, 0))
    fc7_out = jnp.transpose(stacked[:, wide : wide + units].astype(F32))
    fpn_out = fpn_rows.astype(F32)
    fpn_out = jnp.transpose(fpn_out.reshape(2, channels, width), (0, 2, 1))
    return (grad_w_in[None], grad_w_out[None], fpn_out, fc6_out, fc7_out)


def solution(mesh):
    return jax.shard_map(
        per_device,
        mesh=mesh,
        in_specs=(
            P(("dp", "head"), None, None),
            P("section", None, None),
            P("section", None, None),
            P(None, None, "section"),
            P("section", None, None),
            P(),
            P(None, ("dp", "head"), None),
            P(None, None, None, ("dp", "head"), None),
            P(("dp", "head"), None, None),
            P(("dp", "head"), None, None, None),
        ),
        out_specs=(
            P("section", ("dp", "head"), None),
            P("section", ("dp", "head"), None),
            P(None, None, "section"),
            P("section", None, ("dp", "head")),
            P(None, ("dp", "head")),
        ),
        check_vma=False,
    )
```
